256 devices in a mesh: illum: 16 (over z_hi, x), row: 4 (over y), col: 4 (over z_lo, core).
Axes of the slice: x: 4, y: 4, z: 8 (z_hi: 4, z_lo: 2; z = z_hi * 2 + z_lo), core: 2. Of those that a mesh axis runs over, the one named last changes fastest.
Arguments:
- phase_delay: float32 [2, 512, 4096], P(None, ('row', 'illum'), 'col'), may hold values from -1 to 1
- angles: int32 [16, 2], P('illum'), may hold values from -8 to 8
- measured: bfloat16 [2, 16, 512, 4096], P(None, 'illum', 'row', 'col'), may hold values from -120 to 120, as said below
Outputs:
- phase_grad: float32 [2, 512, 4096], P(None, ('row', 'illum'), 'col')
The draws below stay inside these ranges and needn't reach their ends.
Inputs may be any that keep to these rules, and one draw needn't show every extreme that they name: Real and imaginary parts of a measured field, with scales that vary over rows and columns.
All inputs are finite; a program needn't handle non-finite values.
Results may differ from the reference program's by a relative error of at most 0.0003.
Values sent between devices are 32-bit elements; how exact they have to be, the bound alone decides.
A program may use at most 64 MiB of HBM per device.

```python
import math
import jax
import jax.numpy as jnp
from jax import lax

SLICES = 2
SWEEPS = 2
NX = 512
NY = 4096
ILLUMS = 16


def draw_measured(key, part):
    key_base, key_rows, key_cols = jax.random.split(key, 3)
    ramp = 3.0 ** (jnp.arange(NX, dtype=jnp.float32) / max(NX - 1, 1))
    base = jnp.clip(jax.random.normal(key_base, (2, ILLUMS, NX, NY), jnp.float32), -4.0, 4.0)
    row_scale = jnp.exp(jax.random.uniform(key_rows, (NX,), jnp.float32, 0.0, 1.1513))
    col_scale = jnp.exp(jax.random.uniform(key_cols, (NY,), jnp.float32, 0.0, 1.1513))
    scaled = base * (row_scale * ramp)[:, None] * col_scale[None, :]
    return scaled.astype(jnp.bfloat16)


def with_ends(drawn, rng, least, high):
    dims = drawn.shape
    spot = [jax.random.randint(jax.random.fold_in(rng, axis), (), 0, dims[axis]) for axis in range(len(dims))]
    drawn = drawn.at[tuple(spot)].set(least)
    longest = dims.index(max(dims))
    spot[longest] = (spot[longest] + 1) % dims[longest]
    return drawn.at[tuple(spot)].set(high)


def steps_of(rng, extent, cuts, smallest, largest):
    def one(dim, parts):
        draws = jax.random.uniform(jax.random.fold_in(jax.random.fold_in(rng, 6), dim), (parts,), jnp.float32, smallest / len(cuts), largest / len(cuts))
        return jnp.repeat(jnp.exp(draws), extent[dim] // parts).reshape((-1,) + (1,) * (len(extent) - dim - 1))

    factor_of = one(*cuts[0])
    for cut in cuts[1:]:
        factor_of = factor_of * one(*cut)
    return factor_of


def setup_inputs(seed: int = 0) -> dict:
    arg_keys = jax.random.split(jax.random.key(seed), 4)
    return {
        "phase_delay": jnp.clip(jax.random.uniform(arg_keys[0], (SLICES, NX, NY), jnp.float32, -1.0, 1.0) * steps_of(arg_keys[0], (SLICES, NX, NY), ((1, 64), (2, 4)), -0.4, 0.0), -1.0, 1.0),
        "angles": with_ends(jax.random.randint(arg_keys[1], (ILLUMS, 2), -8, 9), jax.random.fold_in(arg_keys[1], 1), -8, 8).astype(jnp.int32),
        "measured": draw_measured(jax.random.fold_in(arg_keys[3], 71), 0),
    }


beta_step = 0.5
eps_energy = 1e-06

def neighbour_sum(padded):
    return padded[..., 2:, 1:-1] + padded[..., :-2, 1:-1] + padded[..., 1:-1, 2:] + padded[..., 1:-1, :-2]

def around_of(wave_field):
    return neighbour_sum(jnp.pad(wave_field, ((0, 0), (1, 1), (1, 1))))

def propagate(wave_field, direction):
    beta_sign = direction * beta_step
    divisor = 1.0 + 16.0 * beta_sign * beta_sign
    beside_all = around_of(wave_field)
    real_part, imag_part = (wave_field[0], wave_field[1])
    rhs_real = real_part + 4.0 * beta_sign * imag_part - beta_sign * beside_all[1]
    rhs_imag = imag_part - 4.0 * beta_sign * real_part + beta_sign * beside_all[0]
    for sweep in range(SWEEPS):
        if sweep > 0:
            beside_all = around_of(jnp.stack([real_part, imag_part]))
        total_real = rhs_real - beta_sign * beside_all[1]
        total_imag = rhs_imag + beta_sign * beside_all[0]
        real_part = (total_real + 4.0 * beta_sign * total_imag) / divisor
        imag_part = (total_imag - 4.0 * beta_sign * total_real) / divisor
    return jnp.stack([real_part, imag_part])

def incident(angle_pair):
    row_ids = lax.iota(jnp.int32, NX)
    col_ids = lax.iota(jnp.int32, NY)
    along_x = angle_pair[0] * row_ids % NX
    along_y = angle_pair[1] * col_ids % NY
    angle_phase = 2.0 * math.pi * (along_x.astype(jnp.float32)[:, None] / NX + along_y.astype(jnp.float32)[None, :] / NY)
    return jnp.stack([jnp.cos(angle_phase), jnp.sin(angle_phase)])

def reference(phase_delay, angles, measured):

    def one_wave(carry, which):
        angle_pair = lax.dynamic_index_in_dim(angles, which, 0, keepdims=False)
        target = lax.dynamic_index_in_dim(measured, which, 1, keepdims=False).astype(jnp.float32)
        energy = jnp.sum(target * target) / (NX * NY) + eps_energy

        def loss_of(phases):
            wave_field = incident(angle_pair)
            for depth_index in range(SLICES):
                cosine = jnp.cos(phases[depth_index])
                sine_part = jnp.sin(phases[depth_index])
                modulated = jnp.stack([wave_field[0] * cosine - wave_field[1] * sine_part, wave_field[0] * sine_part + wave_field[1] * cosine])
                wave_field = propagate(modulated, 1.0)
            return jnp.sum((wave_field - target) ** 2) / energy
        return (carry + jax.grad(loss_of)(phase_delay), None)
    zeros = jnp.zeros(phase_delay.shape, jnp.float32)
    summed, _ = lax.scan(one_wave, zeros, jnp.arange(ILLUMS, dtype=jnp.int32))
    return summed
```

```python
import math

import jax
import jax.numpy as jnp
from jax import lax
from jax.experimental import pallas as pl
from jax.experimental.pallas import tpu as pltpu
from jax.sharding import PartitionSpec as P

ROWS, COLS, NLB = 128, 1024, 8
EXT, STEPS = 144, 18
TOTAL_ROWS, TOTAL_COLS = 512, 4096
EPS_ENERGY = 1e-06
MESH = pl.DeviceIdType.MESH
AG_UNITS = ((0, 7, "zx"), (7, 9, "xz"))
RS_UNITS = ((0, 6, "xz"), (6, 8, "zx"))
N_SEM = 200


def sincos(x):
    t = x * x
    s = x * (1.0 + t * (-1 / 6 + t * (1 / 120 + t * (-1 / 5040 + t * (1 / 362880)))))
    c = 1.0 + t * (-0.5 + t * (1 / 24 + t * (-1 / 720 + t * (1 / 40320 + t * (-1 / 3628800)))))
    return s, c


class Place:
    def __init__(self):
        illum = lax.axis_index("illum")
        self.zh, self.x = illum // 4, lax.rem(illum, 4)
        self.y, self.c = lax.axis_index("row"), lax.axis_index("col")

    def block(self, dz, dx):
        return lax.rem(self.zh + dz + 4, 4) * 4 + lax.rem(self.x + dx + 4, 4)

    def rows(self, dz, dx):
        return pl.ds(pl.multiple_of(8 * self.block(dz, dx), 8), 8)

    def illum(self, dz, dx):
        return {"illum": self.block(dz, dx)}

    def tile(self, dy, dc):
        return {"row": lax.rem(self.y + dy + 4, 4), "col": lax.rem(self.c + dc + 4, 4)}


class Wire:
    def __init__(self, send, recv):
        self.send, self.recv, self.all = send, recv, []

    def start(self, src, dst, device):
        k = len(self.all)
        copy = pltpu.make_async_remote_copy(
            src_ref=src,
            dst_ref=dst,
            send_sem=self.send.at[k],
            recv_sem=self.recv.at[k],
            device_id=device,
            device_id_type=MESH,
        )
        copy.start()
        self.all.append(copy)
        return copy


class Gather:
    def __init__(self, wire, place, planes, unit):
        self.w, self.p, self.planes = wire, place, planes
        self.b0, self.b1, self.order = unit
        self.along = {}

    def pos(self, da, db):
        return (da, db) if self.order == "zx" else (db, da)

    def part(self, da, db, plane=None):
        rows = self.p.rows(*self.pos(da, db))
        lead = slice(None) if plane is None else plane
        return self.planes.at[lead, self.b0 : self.b1, rows, :]

    def send(self, da, db, step, plane=None):
        ref = self.part(da, db, plane)
        return self.w.start(ref, ref, self.p.illum(*self.pos(*step)))

    def start_first(self):
        self.first = [self.send(0, 0, (1, 0)), self.send(0, 0, (-1, 0))]

    def relay_first(self, way):
        self.first[way].wait_recv()
        if way == 0:
            self.first.append(self.send(-1, 0, (1, 0), 0))
        else:
            self.first.append(self.send(1, 0, (-1, 0), 1))

    def end_first(self):
        self.first[2].wait_recv()
        self.first[3].wait_recv()

    def start_second(self, da):
        self.along[da] = [self.send(da, 0, (0, 1)), self.send(da, 0, (0, -1))]

    def relay_second(self, da):
        copies = self.along[da]
        copies[0].wait_recv()
        copies.append(self.send(da, -1, (0, 1), 0))
        copies[1].wait_recv()
        copies.append(self.send(da, 1, (0, -1), 1))

    def end_second(self, da):
        self.along[da][2].wait_recv()
        self.along[da][3].wait_recv()


class Scatter:
    def __init__(self, wire, place, grads, unit, bufs):
        self.w, self.p, self.g = wire, place, grads
        self.b0, self.b1, self.order = unit
        self.t1, self.t2, self.sums, self.t3, self.t4 = bufs

    def pos(self, da, db):
        return (da, db) if self.order == "zx" else (db, da)

    def part(self, da, dq, plane):
        return (plane, slice(self.b0, self.b1), self.p.rows(*self.pos(da, dq)), slice(None))

    def to(self, da, db):
        return self.p.illum(*self.pos(da, db))

    def start_first(self):
        self.c1, self.c2 = {}, []
        for dq in (2, 1, 3, 0):
            up = self.w.start(self.g.at[self.part(2, dq, 0)], self.t1.at[0, dq], self.to(1, 0))
            down = self.w.start(self.g.at[self.part(2, dq, 1)], self.t1.at[1, dq], self.to(-1, 0))
            self.c1[dq] = (up, down)
        self.c2e = {}
        for dq in (2, 1, 3, 0):
            up = self.w.start(self.g.at[self.part(1, dq, 1)], self.t2.at[0, dq, 1], self.to(1, 0))
            down = self.w.start(self.g.at[self.part(-1, dq, 0)], self.t2.at[1, dq, 0], self.to(-1, 0))
            self.c2e[dq] = (up, down)

    def middle_first(self):
        self.c2 = {}
        for dq in (2, 1, 3, 0):
            up, down = self.c1[dq]
            up.wait_recv()
            at = self.part(1, dq, 0)
            self.g[at] = self.g[at] + self.t1[0, dq]
            one = self.w.start(self.g.at[at], self.t2.at[0, dq, 0], self.to(1, 0))
            down.wait_recv()
            at = self.part(-1, dq, 1)
            self.g[at] = self.g[at] + self.t1[1, dq]
            two = self.w.start(self.g.at[at], self.t2.at[1, dq, 1], self.to(-1, 0))
            self.c2[dq] = (one, two)

    def add_first(self, dq):
        for copy in self.c2[dq] + self.c2e[dq]:
            copy.wait_recv()
        for plane in (0, 1):
            own = self.g[self.part(0, dq, plane)]
            self.sums[dq, plane] = own + self.t2[0, dq, plane] + self.t2[1, dq, plane]

    def start_second(self):
        self.add_first(2)
        self.c3 = (
            self.w.start(self.sums.at[2, 0], self.t3.at[0], self.to(0, 1)),
            self.w.start(self.sums.at[2, 1], self.t3.at[1], self.to(0, -1)),
        )
        self.add_first(1)
        self.c4 = [self.w.start(self.sums.at[1, 1], self.t4.at[0, 1], self.to(0, 1))]
        self.add_first(3)
        self.c4.append(self.w.start(self.sums.at[3, 0], self.t4.at[1, 0], self.to(0, -1)))
        self.add_first(0)

    def middle_second(self):
        self.c3[0].wait_recv()
        self.sums[1, 0] = self.sums[1, 0] + self.t3[0]
        self.c4.append(self.w.start(self.sums.at[1, 0], self.t4.at[0, 0], self.to(0, 1)))
        self.c3[1].wait_recv()
        self.sums[3, 1] = self.sums[3, 1] + self.t3[1]
        self.c4.append(self.w.start(self.sums.at[3, 1], self.t4.at[1, 1], self.to(0, -1)))

    def end_second(self, out):
        for copy in self.c4:
            copy.wait_recv()
        for plane in (0, 1):
            total = self.sums[0, plane] + self.t4[0, plane] + self.t4[1, plane]
            for b in range(self.b0, self.b1):
                out[plane, :, 128 * b : 128 * (b + 1)] = total[b - self.b0]


def strided(m):
    return pl.ds(m, 8, stride=STEPS)


def lanes_of(shape):
    return lax.broadcasted_iota(jnp.int32, shape, len(shape) - 1)


def kernel(
    phase_hbm, angles, meas_hbm, out,
    planes, edges, raw, meas, beside, w0, w1, rim, adj, turn, rowf, colf, rowm, energy, energy_in, grads,
    t1a, t2a, suma, t3a, t4a, t1b, t2b, sumb, t3b, t4b,
    local, send, recv,
):
    place = Place()
    wire = Wire(send, recv)
    own = place.rows(0, 0)
    fetch = [
        pltpu.make_async_copy(
            phase_hbm.at[:, :, 128 * b : 128 * (b + 1)], planes.at[:, b, own, :], local.at[b]
        )
        for b in range(NLB)
    ]
    fetch.append(pltpu.make_async_copy(meas_hbm.at[:, 0], raw, local.at[NLB]))
    for copy in fetch:
        copy.start()

    partners = [place.illum(1, 0), place.illum(-1, 0), place.illum(0, 1), place.illum(0, -1)]
    partners += [place.tile(d, 0) for d in (1, 2, 3)] + [place.tile(0, d) for d in (1, 2, 3)]
    partners += [place.tile(d, e) for d in (1, -1) for e in (1, -1)]
    barrier = pltpu.get_barrier_semaphore()
    for device in partners:
        pl.semaphore_signal(barrier, inc=1, device_id=device, device_id_type=MESH)
    pl.semaphore_wait(barrier, len(partners))

    for copy in fetch[:NLB]:
        copy.wait()
    edge_copies = [
        wire.start(planes.at[:, 0, own, :], edges.at[0], place.tile(0, -1)),
        wire.start(planes.at[:, NLB - 1, own, :], edges.at[1], place.tile(0, 1)),
    ]
    one, two = (Gather(wire, place, planes, unit) for unit in AG_UNITS)
    one.start_second(0)
    one.start_first()

    fetch[NLB].wait()
    energy[0] = jnp.zeros((8, 128), jnp.float32)

    def widen(g, carry):
        rows = pl.ds(pl.multiple_of(16 * g, 16), 16)
        for part in (0, 1):
            x = raw[part, rows, :].astype(jnp.float32)
            squares = x * x
            for b in range(NLB):
                meas[part, b, rows, :] = x[:, 128 * b : 128 * (b + 1)]
            half = squares[:8] + squares[8:]
            total = half[:, :128]
            for b in range(1, NLB):
                total = total + half[:, 128 * b : 128 * (b + 1)]
            energy[0] = energy[0] + total
        return carry

    lax.fori_loop(0, ROWS // 16, widen, 0)
    for copy in edge_copies:
        copy.wait_recv()
    lane = lanes_of((2, 8, 128))
    planes[:, NLB, own, :] = jnp.where(lane < 64, edges[0], edges[1])

    step_a, step_b = angles[0, 0], angles[0, 1]
    sub = lax.broadcasted_iota(jnp.int32, (8, 128), 0)

    def row_factor(m, carry):
        r = sub * STEPS + m
        gr = place.y * ROWS + jnp.where(r < 136, r, r - EXT)
        inside = jnp.where((gr >= 0) & (gr < TOTAL_ROWS), 1.0, 0.0)
        turns = jnp.bitwise_and(step_a * gr, TOTAL_ROWS - 1).astype(jnp.float32)
        theta = turns * (2.0 * math.pi / TOTAL_ROWS)
        co, si = jnp.cos(theta), jnp.sin(theta)
        rowf[0, m] = inside * (-0.28 * co - 0.96 * si)
        rowf[1, m] = inside * (0.96 * co - 0.28 * si)
        rowm[m] = inside
        return carry

    lane = lanes_of((8, 128))

    def col_of(b):
        edge = jnp.where(lane < 64, COLS + lane, lane - 128)
        return place.c * COLS + jnp.where(b < NLB, 128 * b + lane, edge)

    def col_factor(b, carry):
        gc = col_of(b)
        inside = jnp.where((gc >= 0) & (gc < TOTAL_COLS), 1.0, 0.0)
        turns = jnp.bitwise_and(step_b * gc, TOTAL_COLS - 1).astype(jnp.float32)
        theta = turns * (2.0 * math.pi / TOTAL_COLS)
        colf[0, b] = inside * jnp.cos(theta)
        colf[1, b] = inside * jnp.sin(theta)
        return carry

    two.start_first()
    two.start_second(0)
    energy_copies = [wire.start(energy.at[0], energy_in.at[d - 1], place.tile(d, 0)) for d in (1, 2, 3)]
    rims = []
    last, first = slice(120, 128), slice(0, 8)
    after, before = slice(128, 136), slice(136, 144)
    tile_rows = slice(0, 128)
    rims.append(wire.start(meas.at[:, :, last, :], meas.at[:, :, before, :], place.tile(1, 0)))
    rims.append(wire.start(meas.at[:, :, first, :], meas.at[:, :, after, :], place.tile(-1, 0)))
    for side, b, dc in ((0, 0, -1), (1, NLB - 1, 1)):
        rims.append(
            wire.start(meas.at[:, b, tile_rows, :], beside.at[side, :, tile_rows, :], place.tile(0, dc))
        )
        rims.append(wire.start(meas.at[:, b, last, :], beside.at[side, :, before, :], place.tile(1, dc)))
        rims.append(wire.start(meas.at[:, b, first, :], beside.at[side, :, after, :], place.tile(-1, dc)))
    lax.fori_loop(0, STEPS, row_factor, 0)
    lax.fori_loop(0, NLB + 1, col_factor, 0)

    one.relay_second(0)
    two.relay_first(0)
    two.start_second(-1)
    two.relay_first(1)
    two.start_second(1)
    for copy in energy_copies:
        copy.wait_recv()
    energy[1] = energy[0] + energy_in[0] + energy_in[1] + energy_in[2]
    energy_copies = [wire.start(energy.at[1], energy_in.at[2 + d], place.tile(0, d)) for d in (1, 2, 3)]
    one.relay_first(0)
    one.start_second(-1)
    one.relay_first(1)
    one.start_second(1)
    two.end_first()
    two.start_second(2)
    two.relay_second(0)
    one.end_first()
    one.start_second(2)
    one.end_second(0)
    one.relay_second(-1)
    one.relay_second(1)
    two.relay_second(-1)
    two.relay_second(1)
    two.relay_second(2)
    one.relay_second(2)
    for da in (-1, 1, 2):
        one.end_second(da)
    for da in (0, -1, 1, 2):
        two.end_second(da)
    ends = [
        wire.start(planes.at[:, :, last, :], planes.at[:, :, before, :], place.tile(1, 0)),
        wire.start(planes.at[:, :, first, :], planes.at[:, :, after, :], place.tile(-1, 0)),
    ]
    for copy in energy_copies:
        copy.wait_recv()
    total = energy[1] + energy_in[3] + energy_in[4] + energy_in[5]
    mean = jnp.sum(total, keepdims=True) * (1.0 / (TOTAL_ROWS * TOTAL_COLS)) + EPS_ENERGY
    kappa = jnp.broadcast_to(2.0 / mean, (8, 128))
    for copy in rims + ends:
        copy.wait_recv()

    gc8 = col_of(NLB)
    col_in = jnp.where((gc8 >= 0) & (gc8 < TOTAL_COLS), 1.0, 0.0)
    lane9 = lanes_of((NLB + 1, 8, 128))

    def scaled(m, amount):
        k = rowm[m] * amount
        return jnp.concatenate([jnp.broadcast_to(k[None], (NLB, 8, 128)), (k * col_in)[None]], axis=0)

    def around(field, part, i):
        mid = field[part, i]
        right = pltpu.roll(mid, 1, 2)
        left = pltpu.roll(mid, 127, 2)
        right = jnp.where(lane9 == 0, jnp.concatenate([right[NLB:], right[:NLB]], axis=0), right)
        left = jnp.where(lane9 == 127, jnp.concatenate([left[1:], left[:1]], axis=0), left)
        return (field[part, i - 1] + field[part, i + 1]) + (right + left)

    def wrap(field):
        for part in (0, 1):
            field[part, 0] = pltpu.roll(field[part, STEPS], 1, 1)
            field[part, STEPS + 1] = pltpu.roll(field[part, 1], 7, 1)

    def add_around(base, field, i, amount):
        k = scaled(i - 1, amount)
        real = base[0, i] - k * around(field, 1, i)
        imag = base[1, i] + k * around(field, 0, i)
        return real, imag

    def sweep(body):
        lax.fori_loop(1, STEPS + 1, lambda i, carry: (body(i), carry)[1], 0)

    def enter(i):
        m = i - 1
        si, co = sincos(planes[0, :, strided(m), :])
        fr, fi = rowf[0, m], rowf[1, m]
        cr, ci = colf[0], colf[1]
        ur = fr[None] * cr - fi[None] * ci
        ui = fr[None] * ci + fi[None] * cr
        w0[0, i] = ur * co - ui * si
        w0[1, i] = ur * si + ui * co

    def first_sweep(base, amount):
        def body(i):
            rim[0, i], rim[1, i] = add_around(base, base, i, amount)

        sweep(body)
        wrap(rim)

    sweep(enter)
    wrap(w0)
    first_sweep(w0, 0.5)

    def between(i):
        ur, ui = add_around(w0, rim, i, 0.2)
        si, co = sincos(planes[1, :, strided(i - 1), :])
        turn[0, i - 1] = co
        turn[1, i - 1] = si
        w1[0, i] = ur * co - ui * si
        w1[1, i] = ur * si + ui * co

    sweep(between)
    wrap(w1)
    first_sweep(w1, 0.5)

    def compare(i):
        m = i - 1
        ur, ui = add_around(w1, rim, i, 0.2)
        k = scaled(m, kappa)
        for part, u in ((0, ur), (1, ui)):
            side = jnp.where(lane < 64, beside[0, part, strided(m), :], beside[1, part, strided(m), :])
            seen = jnp.concatenate([meas[part, :, strided(m), :], side[None]], axis=0)
            adj[part, i] = k * (u - seen)

    sweep(compare)
    wrap(adj)
    first_sweep(adj, -0.5)

    def back(i):
        m = i - 1
        gr, gi = add_around(adj, rim, i, -0.2)
        grad = gi * w1[0, i] - gr * w1[1, i]
        grads[1, :, strided(m), :] = grad[:NLB]
        co, si = turn[0, m], turn[1, m]
        adj[0, i] = gr * co + gi * si
        adj[1, i] = gi * co - gr * si

    sweep(back)
    wrap(adj)
    first_sweep(adj, -0.5)

    def finish(i):
        gr, gi = add_around(adj, rim, i, -0.2)
        grad = gi * w0[0, i] - gr * w0[1, i]
        grads[0, :, strided(i - 1), :] = grad[:NLB]

    sweep(finish)

    bufs = ((t1a, t2a, suma, t3a, t4a), (t1b, t2b, sumb, t3b, t4b))
    sums = [Scatter(wire, place, grads, unit, b) for unit, b in zip(RS_UNITS, bufs)]
    for s in sums:
        s.start_first()
    for s in sums:
        s.middle_first()
    for s in sums:
        s.start_second()
    for s in sums:
        s.middle_second()
    for s in sums:
        s.end_second(out)
    for copy in wire.all:
        copy.wait_send()


def per_device(phase_delay, angles, measured):
    f32 = jnp.float32
    field = pltpu.VMEM((2, STEPS + 2, NLB + 1, 8, 128), f32)
    scratch = [
        pltpu.VMEM((2, NLB + 1, EXT, 128), f32),
        pltpu.VMEM((2, 2, 8, 128), f32),
        pltpu.VMEM((2, ROWS, COLS), jnp.bfloat16),
        pltpu.VMEM((2, NLB, EXT, 128), f32),
        pltpu.VMEM((2, 2, EXT, 128), f32),
        field,
        field,
        field,
        field,
        pltpu.VMEM((2, STEPS, NLB + 1, 8, 128), f32),
        pltpu.VMEM((2, STEPS, 8, 128), f32),
        pltpu.VMEM((2, NLB + 1, 8, 128), f32),
        pltpu.VMEM((STEPS, 8, 128), f32),
        pltpu.VMEM((2, 8, 128), f32),
        pltpu.VMEM((6, 8, 128), f32),
        pltpu.VMEM((2, NLB, EXT, 128), f32),
    ]
    for b0, b1, _ in RS_UNITS:
        n = b1 - b0
        scratch += [
            pltpu.VMEM((2, 4, n, 8, 128), f32),
            pltpu.VMEM((2, 4, 2, n, 8, 128), f32),
            pltpu.VMEM((4, 2, n, 8, 128), f32),
            pltpu.VMEM((2, n, 8, 128), f32),
            pltpu.VMEM((2, 2, n, 8, 128), f32),
        ]
    scratch += [
        pltpu.SemaphoreType.DMA((NLB + 1,)),
        pltpu.SemaphoreType.DMA((N_SEM,)),
        pltpu.SemaphoreType.DMA((N_SEM,)),
    ]
    return pl.pallas_call(
        kernel,
        out_shape=jax.ShapeDtypeStruct(phase_delay.shape, f32),
        in_specs=[
            pl.BlockSpec(memory_space=pl.ANY),
            pl.BlockSpec(memory_space=pltpu.SMEM),
            pl.BlockSpec(memory_space=pl.ANY),
        ],
        out_specs=pl.BlockSpec(memory_space=pltpu.VMEM),
        scratch_shapes=scratch,
        compiler_params=pltpu.CompilerParams(
            collective_id=0, has_side_effects=True, vmem_limit_bytes=56 << 20
        ),
        name="tomography",
    )(phase_delay, angles, measured)


def solution(mesh):
    placed = (P(None, ("row", "illum"), "col"), P("illum", None), P(None, "illum", "row", "col"))
    return jax.shard_map(
        per_device,
        mesh=mesh,
        in_specs=placed,
        out_specs=P(None, ("row", "illum"), "col"),
        check_vma=False,
    )
```

```python
import math

import jax
import jax.numpy as jnp
from jax import lax
from jax.experimental import pallas as pl
from jax.experimental.pallas import tpu as pltpu
from jax.sharding import PartitionSpec as P

ROWS, COLS, NLB = 128, 1024, 8
EXT, STEPS = 144, 18
TOTAL_ROWS, TOTAL_COLS = 512, 4096
EPS_ENERGY = 1e-06
MESH = pl.DeviceIdType.MESH
AG_UNITS = ((0, 7, "zx"), (7, 9, "xz"))
RS_UNITS = ((0, 6, "xz"), (6, 8, "zx"))
N_SEM = 60
UNROLL = 3
SPAN = 720


def sincos(x):
    t = x * x
    s = 0.008333314069458244 + t * (-0.00019835866408867098 + t * 2.6937597583896155e-06)
    s = x * (0.9999999999519255 + t * (-0.1666666642612366 + t * s))
    c = 0.04166645537534636 + t * (-0.0013882960343216638 + t * 2.4121201083497457e-05)
    c = 0.9999999994728761 + t * (-0.4999999736217199 + t * c)
    return s, c


class Place:
    def __init__(self):
        illum = lax.axis_index("illum")
        self.zh, self.x = illum // 4, lax.rem(illum, 4)
        self.y, self.c = lax.axis_index("row"), lax.axis_index("col")

    def block(self, dz, dx):
        return lax.rem(self.zh + dz + 4, 4) * 4 + lax.rem(self.x + dx + 4, 4)

    def rows(self, dz, dx):
        return pl.ds(pl.multiple_of(8 * self.block(dz, dx), 8), 8)

    def illum(self, dz, dx):
        return {"illum": self.block(dz, dx)}

    def tile(self, dy, dc):
        return {"row": lax.rem(self.y + dy + 4, 4), "col": lax.rem(self.c + dc + 4, 4)}


class Wire:
    def __init__(self, send, recv, span):
        self.send, self.recv, self.span = send, recv, span
        self.sent, self.groups = 0, []

    def group(self):
        self.groups.append(0)
        return len(self.groups) - 1

    def start(self, src, dst, device, group):
        tiles = math.prod(src.shape) // 1024
        self.sent += tiles
        self.groups[group] += tiles
        pltpu.make_async_remote_copy(
            src_ref=src,
            dst_ref=dst,
            send_sem=self.send.at[0],
            recv_sem=self.recv.at[group],
            device_id=device,
            device_id_type=MESH,
        ).start()

    def wait_for(self, sem, tiles):
        part = self.span.at[:tiles]
        pltpu.make_async_copy(part, part, sem).wait()

    def arrived(self, group):
        self.wait_for(self.recv.at[group], self.groups[group])

    def all_sent(self):
        self.wait_for(self.send.at[0], self.sent)


class Gather:
    def __init__(self, wire, place, planes, trig, unit, own):
        self.w, self.p, self.planes, self.trig, self.own = wire, place, planes, trig, own
        self.b0, self.b1, self.order = unit
        self.lanes = slice(128 * self.b0, 128 * self.b1)
        self.first = [wire.group() for _ in range(3)]
        self.second = {da: [wire.group() for _ in range(2)] for da in (0, -1, 1, 2)}
        self.last = wire.group()

    def pos(self, da, db):
        return (da, db) if self.order == "zx" else (db, da)

    def send(self, da, db, step, group, plane=None):
        rows = self.p.rows(*self.pos(da, db))
        lead = slice(None) if plane is None else plane
        dst = self.planes.at[lead, rows, self.lanes]
        src = dst
        if (da, db) == (0, 0) and self.own is not None:
            src = self.own.at[lead, :, self.lanes]
        self.w.start(src, dst, self.p.illum(*self.pos(*step)), group)

    def start_first(self):
        self.send(0, 0, (1, 0), self.first[0])
        self.send(0, 0, (-1, 0), self.first[1])

    def relay_first(self, way):
        self.w.arrived(self.first[way])
        if way == 0:
            self.send(-1, 0, (1, 0), self.first[2], 0)
        else:
            self.send(1, 0, (-1, 0), self.first[2], 1)

    def end_first(self):
        self.w.arrived(self.first[2])

    def start_second(self, da):
        self.send(da, 0, (0, 1), self.second[da][0])
        self.send(da, 0, (0, -1), self.second[da][1])

    def relay_second(self, da):
        self.w.arrived(self.second[da][0])
        self.send(da, -1, (0, 1), self.last, 0)
        self.w.arrived(self.second[da][1])
        self.send(da, 1, (0, -1), self.last, 1)

    def end(self):
        self.w.arrived(self.last)

    def turn(self, da, *dbs):
        for db in dbs:
            turn_rows(self.planes, self.trig, self.p.rows(*self.pos(da, db)), self.b0, self.b1)


def turn_rows(planes, trig, rows, b0, b1):
    s, c = sincos(planes[:, rows, 128 * b0 : 128 * b1])
    for b in range(b0, b1):
        at = slice(128 * (b - b0), 128 * (b - b0 + 1))
        for plane in (0, 1):
            trig[plane, 0, b, rows, :] = c[plane, :, at]
            trig[plane, 1, b, rows, :] = s[plane, :, at]


class Scatter:
    def __init__(self, wire, place, grads, unit, bufs):
        self.w, self.p, self.g = wire, place, grads
        self.b0, self.b1, self.order = unit
        self.t1, self.t2, self.sums, self.t3, self.t4 = bufs
        self.r1 = {dq: (wire.group(), wire.group()) for dq in range(4)}
        self.r2 = {dq: wire.group() for dq in range(4)}
        self.r3 = (wire.group(), wire.group())
        self.r4 = wire.group()

    def pos(self, da, db):
        return (da, db) if self.order == "zx" else (db, da)

    def part(self, da, dq, plane):
        return (plane, slice(self.b0, self.b1), self.p.rows(*self.pos(da, dq)), slice(None))

    def send(self, src, dst, da, db, group):
        self.w.start(src, dst, self.p.illum(*self.pos(da, db)), group)

    def start_first(self):
        for dq in (2, 1, 3, 0):
            self.send(self.g.at[self.part(2, dq, 0)], self.t1.at[0, dq], 1, 0, self.r1[dq][0])
            self.send(self.g.at[self.part(2, dq, 1)], self.t1.at[1, dq], -1, 0, self.r1[dq][1])
        for dq in (2, 1, 3, 0):
            self.send(self.g.at[self.part(1, dq, 1)], self.t2.at[0, dq, 1], 1, 0, self.r2[dq])
            self.send(self.g.at[self.part(-1, dq, 0)], self.t2.at[1, dq, 0], -1, 0, self.r2[dq])

    def middle_first(self):
        for dq in (2, 1, 3, 0):
            self.w.arrived(self.r1[dq][0])
            at = self.part(1, dq, 0)
            self.g[at] = self.g[at] + self.t1[0, dq]
            self.send(self.g.at[at], self.t2.at[0, dq, 0], 1, 0, self.r2[dq])
            self.w.arrived(self.r1[dq][1])
            at = self.part(-1, dq, 1)
            self.g[at] = self.g[at] + self.t1[1, dq]
            self.send(self.g.at[at], self.t2.at[1, dq, 1], -1, 0, self.r2[dq])

    def add_first(self, dq):
        self.w.arrived(self.r2[dq])
        for plane in (0, 1):
            own = self.g[self.part(0, dq, plane)]
            self.sums[dq, plane] = own + self.t2[0, dq, plane] + self.t2[1, dq, plane]

    def start_second(self):
        self.add_first(2)
        self.send(self.sums.at[2, 0], self.t3.at[0], 0, 1, self.r3[0])
        self.send(self.sums.at[2, 1], self.t3.at[1], 0, -1, self.r3[1])
        self.add_first(1)
        self.send(self.sums.at[1, 1], self.t4.at[0, 1], 0, 1, self.r4)
        self.add_first(3)
        self.send(self.sums.at[3, 0], self.t4.at[1, 0], 0, -1, self.r4)
        self.add_first(0)

    def middle_second(self):
        self.w.arrived(self.r3[0])
        self.sums[1, 0] = self.sums[1, 0] + self.t3[0]
        self.send(self.sums.at[1, 0], self.t4.at[0, 0], 0, 1, self.r4)
        self.w.arrived(self.r3[1])
        self.sums[3, 1] = self.sums[3, 1] + self.t3[1]
        self.send(self.sums.at[3, 1], self.t4.at[1, 1], 0, -1, self.r4)

    def end_second(self, out):
        self.w.arrived(self.r4)
        for plane in (0, 1):
            total = self.sums[0, plane] + self.t4[0, plane] + self.t4[1, plane]
            for b in range(self.b0, self.b1):
                out[plane, :, 128 * b : 128 * (b + 1)] = total[b - self.b0]


def strided(m):
    return pl.ds(m, 8, stride=STEPS)


def lanes_of(shape):
    return lax.broadcasted_iota(jnp.int32, shape, len(shape) - 1)


def kernel(
    phase_hbm, angles, meas_hbm, out,
    planes, trig, edges, raw, meas, beside, w0, w1, rim, adj, back1, rowf, colf, rowm, energy, energy_in,
    grads, span, t1a, t2a, suma, t3a, t4a, t1b, t2b, sumb, t3b, t4b,
    local, send, recv,
):
    place = Place()
    wire = Wire(send, recv, span)
    own = place.rows(0, 0)
    fetch = [
        pltpu.make_async_copy(phase_hbm, planes.at[:, own, :COLS], local.at[0]),
        pltpu.make_async_copy(meas_hbm.at[:, 0], raw, local.at[1]),
    ]
    partners = [place.illum(1, 0), place.illum(-1, 0), place.illum(0, 1), place.illum(0, -1)]
    partners += [place.tile(d, 0) for d in (1, 2, 3)] + [place.tile(0, d) for d in (1, 2, 3)]
    partners += [place.tile(d, e) for d in (1, -1) for e in (1, -1)]
    barrier = pltpu.get_barrier_semaphore()
    for device in partners:
        pl.semaphore_signal(barrier, inc=1, device_id=device, device_id_type=MESH)
    for copy in fetch:
        copy.start()
    pl.semaphore_wait(barrier, len(partners))

    edge_group = wire.group()
    wire.start(phase_hbm.at[:, :, :128], edges.at[0], place.tile(0, -1), edge_group)
    wire.start(phase_hbm.at[:, :, COLS - 128 :], edges.at[1], place.tile(0, 1), edge_group)
    one = Gather(wire, place, planes, trig, AG_UNITS[0], phase_hbm)
    two = Gather(wire, place, planes, trig, AG_UNITS[1], None)
    one.start_first()
    one.start_second(0)
    fetch[0].wait()
    one.turn(0, 0)
    wire.arrived(edge_group)
    lane = lanes_of((2, 8, 128))
    planes[:, own, COLS:] = jnp.where(lane < 64, edges[0], edges[1])
    two.start_first()
    two.start_second(0)
    two.turn(0, 0)

    fetch[1].wait()
    energy[0] = jnp.zeros((8, 128), jnp.float32)

    def widen(g, carry):
        rows = pl.ds(pl.multiple_of(16 * g, 16), 16)
        for part in (0, 1):
            x = raw[part, rows, :].astype(jnp.float32)
            squares = x * x
            for b in range(NLB):
                meas[part, b, rows, :] = x[:, 128 * b : 128 * (b + 1)]
            half = squares[:8] + squares[8:]
            total = half[:, :128]
            for b in range(1, NLB):
                total = total + half[:, 128 * b : 128 * (b + 1)]
            energy[0] = energy[0] + total
        return carry

    lax.fori_loop(0, ROWS // 16, widen, 0)

    step_a, step_b = angles[0, 0], angles[0, 1]
    sub = lax.broadcasted_iota(jnp.int32, (8, 128), 0)

    def row_factor(m, carry):
        r = sub * STEPS + m
        gr = place.y * ROWS + jnp.where(r < 136, r, r - EXT)
        inside = jnp.where((gr >= 0) & (gr < TOTAL_ROWS), 1.0, 0.0)
        turns = jnp.bitwise_and(step_a * gr, TOTAL_ROWS - 1).astype(jnp.float32)
        theta = turns * (2.0 * math.pi / TOTAL_ROWS)
        co, si = jnp.cos(theta), jnp.sin(theta)
        rowf[0, m] = inside * (-0.28 * co - 0.96 * si)
        rowf[1, m] = inside * (0.96 * co - 0.28 * si)
        rowm[m] = inside
        return carry

    lane = lanes_of((8, 128))

    def col_of(b):
        edge = jnp.where(lane < 64, COLS + lane, lane - 128)
        return place.c * COLS + jnp.where(b < NLB, 128 * b + lane, edge)

    def col_factor(b, carry):
        gc = col_of(b)
        inside = jnp.where((gc >= 0) & (gc < TOTAL_COLS), 1.0, 0.0)
        turns = jnp.bitwise_and(step_b * gc, TOTAL_COLS - 1).astype(jnp.float32)
        theta = turns * (2.0 * math.pi / TOTAL_COLS)
        colf[0, b] = inside * jnp.cos(theta)
        colf[1, b] = inside * jnp.sin(theta)
        return carry

    one.relay_second(0)
    one.turn(0, -1, 1)
    two.relay_first(0)
    two.start_second(-1)
    two.relay_first(1)
    two.start_second(1)
    lax.fori_loop(0, STEPS, row_factor, 0)
    lax.fori_loop(0, NLB + 1, col_factor, 0)
    one.relay_first(0)
    one.start_second(-1)
    one.relay_first(1)
    one.start_second(1)
    one.turn(-1, 0)
    one.turn(1, 0)
    two.turn(-1, 0)
    two.turn(1, 0)
    two.end_first()
    two.start_second(2)
    two.turn(2, 0)
    two.relay_second(0)
    two.turn(0, -1, 1)
    one.relay_second(-1)
    one.turn(-1, -1, 1)
    one.relay_second(1)
    one.turn(1, -1, 1)
    one.end_first()
    one.start_second(2)
    one.turn(2, 0)
    two.relay_second(-1)
    two.turn(-1, -1, 1)
    two.relay_second(1)
    two.turn(1, -1, 1)
    two.relay_second(2)
    two.turn(2, -1, 1)
    one.relay_second(2)
    one.turn(2, -1, 1)
    two.end()
    one.end()
    end_group = wire.group()
    last, first = slice(120, 128), slice(0, 8)
    after, before = slice(128, 136), slice(136, 144)
    wire.start(planes.at[:, last, :], planes.at[:, before, :], place.tile(1, 0), end_group)
    wire.start(planes.at[:, first, :], planes.at[:, after, :], place.tile(-1, 0), end_group)
    energy_group = wire.group()
    for d in (1, 2, 3):
        wire.start(energy.at[0], energy_in.at[d - 1], place.tile(d, 0), energy_group)
    rim_group = wire.group()
    tile_rows = slice(0, 128)
    wire.start(meas.at[:, :, last, :], meas.at[:, :, before, :], place.tile(1, 0), rim_group)
    wire.start(meas.at[:, :, first, :], meas.at[:, :, after, :], place.tile(-1, 0), rim_group)
    for side, b, dc in ((0, 0, -1), (1, NLB - 1, 1)):
        src, dst = meas.at[:, b], beside.at[side]
        wire.start(src.at[:, tile_rows, :], dst.at[:, tile_rows, :], place.tile(0, dc), rim_group)
        wire.start(src.at[:, last, :], dst.at[:, before, :], place.tile(1, dc), rim_group)
        wire.start(src.at[:, first, :], dst.at[:, after, :], place.tile(-1, dc), rim_group)
    for unit in (one, two):
        for da in (0, -1, 1, 2):
            unit.turn(da, 2)
    wire.arrived(end_group)
    turn_rows(planes, trig, after, 0, NLB + 1)
    turn_rows(planes, trig, before, 0, NLB + 1)

    gc8 = col_of(NLB)
    col_in = jnp.where((gc8 >= 0) & (gc8 < TOTAL_COLS), 1.0, 0.0)
    lane9 = lanes_of((NLB + 1, 8, 128))

    def scaled(m, amount):
        k = rowm[m] * amount
        return jnp.concatenate([jnp.broadcast_to(k[None], (NLB, 8, 128)), (k * col_in)[None]], axis=0)

    def around(field, part, i):
        mid = field[part, i]
        right = pltpu.roll(mid, 1, 2)
        left = pltpu.roll(mid, 127, 2)
        right = jnp.where(lane9 == 0, jnp.concatenate([right[NLB:], right[:NLB]], axis=0), right)
        left = jnp.where(lane9 == 127, jnp.concatenate([left[1:], left[:1]], axis=0), left)
        return (field[part, i - 1] + field[part, i + 1]) + (right + left)

    def wrap(field):
        for part in (0, 1):
            field[part, 0] = pltpu.roll(field[part, STEPS], 1, 1)
            field[part, STEPS + 1] = pltpu.roll(field[part, 1], 7, 1)

    def add_around(base, field, i, amount):
        k = scaled(i - 1, amount)
        real = base[0, i] - k * around(field, 1, i)
        imag = base[1, i] + k * around(field, 0, i)
        return real, imag

    def sweep(body):
        def several(t, carry):
            for k in range(UNROLL):
                body(UNROLL * t + k + 1)
            return carry

        lax.fori_loop(0, STEPS // UNROLL, several, 0)

    def enter(i):
        m = i - 1
        co, si = trig[0, 0, :, strided(m), :], trig[0, 1, :, strided(m), :]
        fr, fi = rowf[0, m], rowf[1, m]
        cr, ci = colf[0], colf[1]
        ur = fr[None] * cr - fi[None] * ci
        ui = fr[None] * ci + fi[None] * cr
        w0[0, i] = ur * co - ui * si
        w0[1, i] = ur * si + ui * co

    def first_sweep(base, amount):
        def body(i):
            rim[0, i], rim[1, i] = add_around(base, base, i, amount)

        sweep(body)
        wrap(rim)

    sweep(enter)
    wrap(w0)
    first_sweep(w0, 0.5)

    def between(i):
        ur, ui = add_around(w0, rim, i, 0.2)
        m = i - 1
        co, si = trig[1, 0, :, strided(m), :], trig[1, 1, :, strided(m), :]
        w1[0, i] = ur * co - ui * si
        w1[1, i] = ur * si + ui * co

    sweep(between)
    wire.arrived(energy_group)
    energy[1] = energy[0] + energy_in[0] + energy_in[1] + energy_in[2]
    energy_group = wire.group()
    for d in (1, 2, 3):
        wire.start(energy.at[1], energy_in.at[2 + d], place.tile(0, d), energy_group)
    wrap(w1)
    first_sweep(w1, 0.5)

    wire.arrived(energy_group)
    total = energy[1] + energy_in[3] + energy_in[4] + energy_in[5]
    mean = jnp.sum(total, keepdims=True) * (1.0 / (TOTAL_ROWS * TOTAL_COLS)) + EPS_ENERGY
    kappa = jnp.broadcast_to(2.0 / mean, (8, 128))
    wire.arrived(rim_group)

    def compare(i):
        m = i - 1
        ur, ui = add_around(w1, rim, i, 0.2)
        k = scaled(m, kappa)
        for part, u in ((0, ur), (1, ui)):
            side = jnp.where(lane < 64, beside[0, part, strided(m), :], beside[1, part, strided(m), :])
            seen = jnp.concatenate([meas[part, :, strided(m), :], side[None]], axis=0)
            adj[part, i] = k * (u - seen)

    sweep(compare)
    wrap(adj)
    first_sweep(adj, -0.5)

    def back(i):
        m = i - 1
        gr, gi = add_around(adj, rim, i, -0.2)
        grad = gi * w1[0, i] - gr * w1[1, i]
        grads[1, :, strided(m), :] = grad[:NLB]
        co, si = trig[1, 0, :, strided(m), :], trig[1, 1, :, strided(m), :]
        back1[0, i] = gr * co + gi * si
        back1[1, i] = gi * co - gr * si

    sweep(back)
    wrap(back1)
    first_sweep(back1, -0.5)

    def finish(i):
        gr, gi = add_around(back1, rim, i, -0.2)
        grad = gi * w0[0, i] - gr * w0[1, i]
        grads[0, :, strided(i - 1), :] = grad[:NLB]

    sweep(finish)

    bufs = ((t1a, t2a, suma, t3a, t4a), (t1b, t2b, sumb, t3b, t4b))
    sums = [Scatter(wire, place, grads, unit, b) for unit, b in zip(RS_UNITS, bufs)]
    for s in sums:
        s.start_first()
    for s in sums:
        s.middle_first()
    for s in sums:
        s.start_second()
    for s in sums:
        s.middle_second()
    for s in sums:
        s.end_second(out)
    wire.all_sent()


def per_device(phase_delay, angles, measured):
    f32 = jnp.float32
    field = pltpu.VMEM((2, STEPS + 2, NLB + 1, 8, 128), f32)
    scratch = [
        pltpu.VMEM((2, EXT, COLS + 128), f32),
        pltpu.VMEM((2, 2, NLB + 1, EXT, 128), f32),
        pltpu.VMEM((2, 2, 8, 128), f32),
        pltpu.VMEM((2, ROWS, COLS), jnp.bfloat16),
        pltpu.VMEM((2, NLB, EXT, 128), f32),
        pltpu.VMEM((2, 2, EXT, 128), f32),
        field,
        field,
        field,
        field,
        field,
        pltpu.VMEM((2, STEPS, 8, 128), f32),
        pltpu.VMEM((2, NLB + 1, 8, 128), f32),
        pltpu.VMEM((STEPS, 8, 128), f32),
        pltpu.VMEM((2, 8, 128), f32),
        pltpu.VMEM((6, 8, 128), f32),
        pltpu.VMEM((2, NLB, EXT, 128), f32),
        pltpu.VMEM((SPAN, 8, 128), f32),
    ]
    for b0, b1, _ in RS_UNITS:
        n = b1 - b0
        scratch += [
            pltpu.VMEM((2, 4, n, 8, 128), f32),
            pltpu.VMEM((2, 4, 2, n, 8, 128), f32),
            pltpu.VMEM((4, 2, n, 8, 128), f32),
            pltpu.VMEM((2, n, 8, 128), f32),
            pltpu.VMEM((2, 2, n, 8, 128), f32),
        ]
    scratch += [
        pltpu.SemaphoreType.DMA((2,)),
        pltpu.SemaphoreType.DMA((1,)),
        pltpu.SemaphoreType.DMA((N_SEM,)),
    ]
    return pl.pallas_call(
        kernel,
        out_shape=jax.ShapeDtypeStruct(phase_delay.shape, f32),
        in_specs=[
            pl.BlockSpec(memory_space=pl.ANY),
            pl.BlockSpec(memory_space=pltpu.SMEM),
            pl.BlockSpec(memory_space=pl.ANY),
        ],
        out_specs=pl.BlockSpec(memory_space=pltpu.VMEM),
        scratch_shapes=scratch,
        compiler_params=pltpu.CompilerParams(
            collective_id=0, has_side_effects=True, vmem_limit_bytes=56 << 20
        ),
        name="tomography",
    )(phase_delay, angles, measured)


def solution(mesh):
    placed = (P(None, ("row", "illum"), "col"), P("illum", None), P(None, "illum", "row", "col"))
    return jax.shard_map(
        per_device,
        mesh=mesh,
        in_specs=placed,
        out_specs=P(None, ("row", "illum"), "col"),
        check_vma=False,
    )
```

```python
import math

import jax
import jax.numpy as jnp
from jax import lax
from jax.experimental import pallas as pl
from jax.experimental.pallas import tpu as pltpu
from jax.sharding import PartitionSpec as P

ROWS, COLS, NLB = 128, 1024, 8
EXT, STEPS = 144, 18
TOTAL_ROWS, TOTAL_COLS = 512, 4096
EPS_ENERGY = 1e-06
MESH = pl.DeviceIdType.MESH
AG_UNITS = ((0, 7, "zx"), (7, 9, "xz"))
RS_UNITS = ((0, 6, "xz"), (6, 8, "zx"))
N_SEM = 60
UNROLL = 3
SPAN = 720


def sincos(x):
    t = x * x
    s = 0.008333314069458244 + t * (-0.00019835866408867098 + t * 2.6937597583896155e-06)
    s = x * (0.9999999999519255 + t * (-0.1666666642612366 + t * s))
    c = 0.04166645537534636 + t * (-0.0013882960343216638 + t * 2.4121201083497457e-05)
    c = 0.9999999994728761 + t * (-0.4999999736217199 + t * c)
    return s, c


class Place:
    def __init__(self):
        illum = lax.axis_index("illum")
        self.zh, self.x = illum // 4, lax.rem(illum, 4)
        self.y, self.c = lax.axis_index("row"), lax.axis_index("col")

    def block(self, dz, dx):
        return lax.rem(self.zh + dz + 4, 4) * 4 + lax.rem(self.x + dx + 4, 4)

    def rows(self, dz, dx):
        return pl.ds(pl.multiple_of(8 * self.block(dz, dx), 8), 8)

    def illum(self, dz, dx):
        return {"illum": self.block(dz, dx)}

    def tile(self, dy, dc):
        return {"row": lax.rem(self.y + dy + 4, 4), "col": lax.rem(self.c + dc + 4, 4)}


class Wire:
    def __init__(self, send, recv, span):
        self.send, self.recv, self.span = send, recv, span
        self.sent, self.groups = 0, []

    def group(self):
        self.groups.append(0)
        return len(self.groups) - 1

    def start(self, src, dst, device, group):
        tiles = math.prod(src.shape) // 1024
        self.sent += tiles
        self.groups[group] += tiles
        pltpu.make_async_remote_copy(
            src_ref=src,
            dst_ref=dst,
            send_sem=self.send.at[0],
            recv_sem=self.recv.at[group],
            device_id=device,
            device_id_type=MESH,
        ).start()

    def wait_for(self, sem, tiles):
        part = self.span.at[:tiles]
        pltpu.make_async_copy(part, part, sem).wait()

    def arrived(self, group):
        self.wait_for(self.recv.at[group], self.groups[group])

    def all_sent(self):
        self.wait_for(self.send.at[0], self.sent)


class Gather:
    def __init__(self, wire, place, planes, trig, unit):
        self.w, self.p, self.planes, self.trig = wire, place, planes, trig
        self.b0, self.b1, self.order = unit
        self.lanes = slice(128 * self.b0, 128 * self.b1)
        self.first = [wire.group() for _ in range(3)]
        self.second = {da: [wire.group() for _ in range(2)] for da in (0, -1, 1, 2)}
        self.last = wire.group()

    def pos(self, da, db):
        return (da, db) if self.order == "zx" else (db, da)

    def send(self, da, db, step, group, plane=None):
        rows = self.p.rows(*self.pos(da, db))
        lead = slice(None) if plane is None else plane
        ref = self.planes.at[lead, rows, self.lanes]
        self.w.start(ref, ref, self.p.illum(*self.pos(*step)), group)

    def start_first(self):
        self.send(0, 0, (1, 0), self.first[0])
        self.send(0, 0, (-1, 0), self.first[1])

    def relay_first(self, way):
        self.w.arrived(self.first[way])
        if way == 0:
            self.send(-1, 0, (1, 0), self.first[2], 0)
        else:
            self.send(1, 0, (-1, 0), self.first[2], 1)

    def end_first(self):
        self.w.arrived(self.first[2])

    def start_second(self, da):
        self.send(da, 0, (0, 1), self.second[da][0])
        self.send(da, 0, (0, -1), self.second[da][1])

    def relay_second(self, da):
        self.w.arrived(self.second[da][0])
        self.send(da, -1, (0, 1), self.last, 0)
        self.w.arrived(self.second[da][1])
        self.send(da, 1, (0, -1), self.last, 1)

    def end(self):
        self.w.arrived(self.last)

    def turn(self, da, *dbs):
        for db in dbs:
            turn_rows(self.planes, self.trig, self.p.rows(*self.pos(da, db)), self.b0, self.b1)


def turn_rows(planes, trig, rows, b0, b1):
    s, c = sincos(planes[:, rows, 128 * b0 : 128 * b1])
    for b in range(b0, b1):
        at = slice(128 * (b - b0), 128 * (b - b0 + 1))
        for plane in (0, 1):
            trig[plane, 0, b, rows, :] = c[plane, :, at]
            trig[plane, 1, b, rows, :] = s[plane, :, at]


class Scatter:
    def __init__(self, wire, place, grads, unit, bufs):
        self.w, self.p, self.g = wire, place, grads
        self.b0, self.b1, self.order = unit
        self.t1, self.t2, self.sums, self.t3, self.t4 = bufs
        self.r1 = {dq: (wire.group(), wire.group()) for dq in range(4)}
        self.r2 = {dq: wire.group() for dq in range(4)}
        self.r3 = (wire.group(), wire.group())
        self.r4 = wire.group()

    def pos(self, da, db):
        return (da, db) if self.order == "zx" else (db, da)

    def part(self, da, dq, plane):
        return (plane, slice(self.b0, self.b1), self.p.rows(*self.pos(da, dq)), slice(None))

    def send(self, src, dst, da, db, group):
        self.w.start(src, dst, self.p.illum(*self.pos(da, db)), group)

    def start_first(self):
        for dq in (2, 1, 3, 0):
            self.send(self.g.at[self.part(2, dq, 0)], self.t1.at[0, dq], 1, 0, self.r1[dq][0])
            self.send(self.g.at[self.part(2, dq, 1)], self.t1.at[1, dq], -1, 0, self.r1[dq][1])
        for dq in (2, 1, 3, 0):
            self.send(self.g.at[self.part(1, dq, 1)], self.t2.at[0, dq, 1], 1, 0, self.r2[dq])
            self.send(self.g.at[self.part(-1, dq, 0)], self.t2.at[1, dq, 0], -1, 0, self.r2[dq])

    def middle_first(self):
        for dq in (2, 1, 3, 0):
            self.w.arrived(self.r1[dq][0])
            at = self.part(1, dq, 0)
            self.g[at] = self.g[at] + self.t1[0, dq]
            self.send(self.g.at[at], self.t2.at[0, dq, 0], 1, 0, self.r2[dq])
            self.w.arrived(self.r1[dq][1])
            at = self.part(-1, dq, 1)
            self.g[at] = self.g[at] + self.t1[1, dq]
            self.send(self.g.at[at], self.t2.at[1, dq, 1], -1, 0, self.r2[dq])

    def add_first(self, dq):
        self.w.arrived(self.r2[dq])
        for plane in (0, 1):
            own = self.g[self.part(0, dq, plane)]
            self.sums[dq, plane] = own + self.t2[0, dq, plane] + self.t2[1, dq, plane]

    def start_second(self):
        self.add_first(2)
        self.send(self.sums.at[2, 0], self.t3.at[0], 0, 1, self.r3[0])
        self.send(self.sums.at[2, 1], self.t3.at[1], 0, -1, self.r3[1])
        self.add_first(1)
        self.send(self.sums.at[1, 1], self.t4.at[0, 1], 0, 1, self.r4)
        self.add_first(3)
        self.send(self.sums.at[3, 0], self.t4.at[1, 0], 0, -1, self.r4)
        self.add_first(0)

    def middle_second(self):
        self.w.arrived(self.r3[0])
        self.sums[1, 0] = self.sums[1, 0] + self.t3[0]
        self.send(self.sums.at[1, 0], self.t4.at[0, 0], 0, 1, self.r4)
        self.w.arrived(self.r3[1])
        self.sums[3, 1] = self.sums[3, 1] + self.t3[1]
        self.send(self.sums.at[3, 1], self.t4.at[1, 1], 0, -1, self.r4)

    def end_second(self, plane):
        total = self.sums[0, plane] + self.t4[0, plane] + self.t4[1, plane]
        return [total[b] for b in range(self.b1 - self.b0)]


def strided(m):
    return pl.ds(m, 8, stride=STEPS)


def swapped(blocks):
    blocks = list(blocks)
    lane = lanes_of(blocks[0].shape)
    last = lane.ndim - 1
    for k in (1, 2, 4):
        low = jnp.bitwise_and(lane, k) == 0
        for b in range(NLB):
            if not b & k:
                one, two = blocks[b], blocks[b | k]
                blocks[b] = jnp.where(low, one, pltpu.roll(two, k, last))
                blocks[b | k] = jnp.where(low, pltpu.roll(one, 128 - k, last), two)
    return blocks


def split(x):
    return [x[..., 128 * b : 128 * (b + 1)] for b in range(NLB)]


def lanes_of(shape):
    return lax.broadcasted_iota(jnp.int32, shape, len(shape) - 1)


def kernel(
    phase_hbm, angles, meas_hbm, out,
    planes, trig, fresh, edges, raw, meas, rims, beside, w0, w1, rim, adj, back1, rowf, colf, rowm, energy, energy_in,
    grads, span, t1a, t2a, suma, t3a, t4a, t1b, t2b, sumb, t3b, t4b,
    local, send, recv,
):
    place = Place()
    wire = Wire(send, recv, span)
    own = place.rows(0, 0)
    fetch = [
        pltpu.make_async_copy(phase_hbm, fresh, local.at[0]),
        pltpu.make_async_copy(meas_hbm.at[:, 0], raw, local.at[1]),
    ]
    partners = [place.illum(1, 0), place.illum(-1, 0), place.illum(0, 1), place.illum(0, -1)]
    partners += [place.tile(d, 0) for d in (1, 2, 3)] + [place.tile(0, d) for d in (1, 2, 3)]
    partners += [place.tile(d, e) for d in (1, -1) for e in (1, -1)]
    barrier = pltpu.get_barrier_semaphore()
    for device in partners:
        pl.semaphore_signal(barrier, inc=1, device_id=device, device_id_type=MESH)
    for copy in fetch:
        copy.start()
    pl.semaphore_wait(barrier, len(partners))

    edge_group = wire.group()
    wire.start(phase_hbm.at[:, :, :128], edges.at[0], place.tile(0, -1), edge_group)
    wire.start(phase_hbm.at[:, :, COLS - 128 :], edges.at[1], place.tile(0, 1), edge_group)
    one = Gather(wire, place, planes, trig, AG_UNITS[0])
    two = Gather(wire, place, planes, trig, AG_UNITS[1])
    fetch[0].wait()
    for b, block in enumerate(swapped(split(fresh[...]))):
        planes[:, own, 128 * b : 128 * (b + 1)] = block
    one.start_first()
    one.start_second(0)
    one.turn(0, 0)
    wire.arrived(edge_group)
    lane = lanes_of((2, 8, 128))
    planes[:, own, COLS:] = jnp.where(lane < 64, pltpu.roll(edges[0], 8, 2), pltpu.roll(edges[1], 120, 2))
    two.start_first()
    two.start_second(0)
    two.turn(0, 0)

    fetch[1].wait()
    energy[0] = jnp.zeros((8, 128), jnp.float32)

    def widen(g, carry):
        rows = pl.ds(pl.multiple_of(16 * g, 16), 16)
        for part in (0, 1):
            x = raw[part, rows, :].astype(jnp.float32)
            squares = x * x
            blocks = split(x)
            rims[0, part, rows, :] = pltpu.roll(blocks[0], 8, 1)
            rims[1, part, rows, :] = pltpu.roll(blocks[NLB - 1], 120, 1)
            for b, block in enumerate(swapped(blocks)):
                meas[part, b, rows, :] = block
            half = squares[:8] + squares[8:]
            total = half[:, :128]
            for b in range(1, NLB):
                total = total + half[:, 128 * b : 128 * (b + 1)]
            energy[0] = energy[0] + total
        return carry

    lax.fori_loop(0, ROWS // 16, widen, 0)

    step_a, step_b = angles[0, 0], angles[0, 1]
    sub = lax.broadcasted_iota(jnp.int32, (8, 128), 0)

    def row_factor(m, carry):
        r = sub * STEPS + m
        gr = place.y * ROWS + jnp.where(r < 136, r, r - EXT)
        inside = jnp.where((gr >= 0) & (gr < TOTAL_ROWS), 1.0, 0.0)
        turns = jnp.bitwise_and(step_a * gr, TOTAL_ROWS - 1).astype(jnp.float32)
        theta = turns * (2.0 * math.pi / TOTAL_ROWS)
        co, si = jnp.cos(theta), jnp.sin(theta)
        rowf[0, m] = inside * (-0.28 * co - 0.96 * si)
        rowf[1, m] = inside * (0.96 * co - 0.28 * si)
        rowm[m] = inside
        return carry

    lane = lanes_of((8, 128))

    def col_of(b):
        edge = jnp.where(lane < 64, COLS - 8 + lane, lane - 120)
        inner = 128 * jnp.bitwise_and(lane, 7) + jnp.bitwise_and(lane, -8) + b
        return place.c * COLS + jnp.where(b < NLB, inner, edge)

    def col_factor(b, carry):
        gc = col_of(b)
        inside = jnp.where((gc >= 0) & (gc < TOTAL_COLS), 1.0, 0.0)
        turns = jnp.bitwise_and(step_b * gc, TOTAL_COLS - 1).astype(jnp.float32)
        theta = turns * (2.0 * math.pi / TOTAL_COLS)
        colf[0, b] = inside * jnp.cos(theta)
        colf[1, b] = inside * jnp.sin(theta)
        return carry

    one.relay_second(0)
    one.turn(0, -1, 1)
    two.relay_first(0)
    two.start_second(-1)
    two.relay_first(1)
    two.start_second(1)
    lax.fori_loop(0, STEPS, row_factor, 0)
    lax.fori_loop(0, NLB + 1, col_factor, 0)
    one.relay_first(0)
    one.start_second(-1)
    one.relay_first(1)
    one.start_second(1)
    one.turn(-1, 0)
    one.turn(1, 0)
    two.turn(-1, 0)
    two.turn(1, 0)
    two.end_first()
    two.start_second(2)
    two.turn(2, 0)
    two.relay_second(0)
    two.turn(0, -1, 1)
    one.relay_second(-1)
    one.turn(-1, -1, 1)
    one.relay_second(1)
    one.turn(1, -1, 1)
    one.end_first()
    one.start_second(2)
    one.turn(2, 0)
    two.relay_second(-1)
    two.turn(-1, -1, 1)
    two.relay_second(1)
    two.turn(1, -1, 1)
    two.relay_second(2)
    two.turn(2, -1, 1)
    one.relay_second(2)
    one.turn(2, -1, 1)
    two.end()
    one.end()
    end_group = wire.group()
    last, first = slice(120, 128), slice(0, 8)
    after, before = slice(128, 136), slice(136, 144)
    wire.start(planes.at[:, last, :], planes.at[:, before, :], place.tile(1, 0), end_group)
    wire.start(planes.at[:, first, :], planes.at[:, after, :], place.tile(-1, 0), end_group)
    energy_group = wire.group()
    for d in (1, 2, 3):
        wire.start(energy.at[0], energy_in.at[d - 1], place.tile(d, 0), energy_group)
    rim_group = wire.group()
    tile_rows = slice(0, 128)
    wire.start(meas.at[:, :, last, :], meas.at[:, :, before, :], place.tile(1, 0), rim_group)
    wire.start(meas.at[:, :, first, :], meas.at[:, :, after, :], place.tile(-1, 0), rim_group)
    for side, dc in ((0, -1), (1, 1)):
        src, dst = rims.at[side], beside.at[side]
        wire.start(src.at[:, tile_rows, :], dst.at[:, tile_rows, :], place.tile(0, dc), rim_group)
        wire.start(src.at[:, last, :], dst.at[:, before, :], place.tile(1, dc), rim_group)
        wire.start(src.at[:, first, :], dst.at[:, after, :], place.tile(-1, dc), rim_group)
    for unit in (one, two):
        for da in (0, -1, 1, 2):
            unit.turn(da, 2)
    wire.arrived(end_group)
    turn_rows(planes, trig, after, 0, NLB + 1)
    turn_rows(planes, trig, before, 0, NLB + 1)

    gc8 = col_of(NLB)
    col_in = jnp.where((gc8 >= 0) & (gc8 < TOTAL_COLS), 1.0, 0.0)

    def scaled(m, amount):
        k = rowm[m] * amount
        return jnp.concatenate([jnp.broadcast_to(k[None], (NLB, 8, 128)), (k * col_in)[None]], axis=0)

    def around(field, part, i):
        mid = field[part, i]
        first, last, edge = mid[0], mid[NLB - 1], mid[NLB]
        ahead = pltpu.roll(jnp.where(lane == 8, edge, first), 119, 1)
        behind = pltpu.roll(jnp.where(lane == 119, edge, last), 9, 1)
        right_last = jnp.where(lane < 120, pltpu.roll(first, 120, 1), ahead)
        left_first = jnp.where(lane < 8, behind, pltpu.roll(last, 8, 1))
        right_edge = jnp.where(lane == 119, ahead, pltpu.roll(edge, 127, 1))
        left_edge = jnp.where(lane == 8, behind, pltpu.roll(edge, 1, 1))
        right = jnp.concatenate([mid[1:NLB], right_last[None], right_edge[None]], axis=0)
        left = jnp.concatenate([left_first[None], mid[: NLB - 1], left_edge[None]], axis=0)
        return (field[part, i - 1] + field[part, i + 1]) + (right + left)

    def wrap(field):
        for part in (0, 1):
            field[part, 0] = pltpu.roll(field[part, STEPS], 1, 1)
            field[part, STEPS + 1] = pltpu.roll(field[part, 1], 7, 1)

    def add_around(base, field, i, amount):
        k = scaled(i - 1, amount)
        real = base[0, i] - k * around(field, 1, i)
        imag = base[1, i] + k * around(field, 0, i)
        return real, imag

    def sweep(body):
        def several(t, carry):
            for k in range(UNROLL):
                body(UNROLL * t + k + 1)
            return carry

        lax.fori_loop(0, STEPS // UNROLL, several, 0)

    def enter(i):
        m = i - 1
        co, si = trig[0, 0, :, strided(m), :], trig[0, 1, :, strided(m), :]
        fr, fi = rowf[0, m], rowf[1, m]
        cr, ci = colf[0], colf[1]
        ur = fr[None] * cr - fi[None] * ci
        ui = fr[None] * ci + fi[None] * cr
        w0[0, i] = ur * co - ui * si
        w0[1, i] = ur * si + ui * co

    def first_sweep(base, amount):
        def body(i):
            rim[0, i], rim[1, i] = add_around(base, base, i, amount)

        sweep(body)
        wrap(rim)

    sweep(enter)
    wrap(w0)
    first_sweep(w0, 0.5)

    def between(i):
        ur, ui = add_around(w0, rim, i, 0.2)
        m = i - 1
        co, si = trig[1, 0, :, strided(m), :], trig[1, 1, :, strided(m), :]
        w1[0, i] = ur * co - ui * si
        w1[1, i] = ur * si + ui * co

    sweep(between)
    wire.arrived(energy_group)
    energy[1] = energy[0] + energy_in[0] + energy_in[1] + energy_in[2]
    energy_group = wire.group()
    for d in (1, 2, 3):
        wire.start(energy.at[1], energy_in.at[2 + d], place.tile(0, d), energy_group)
    wrap(w1)
    first_sweep(w1, 0.5)

    wire.arrived(energy_group)
    total = energy[1] + energy_in[3] + energy_in[4] + energy_in[5]
    mean = jnp.sum(total, keepdims=True) * (1.0 / (TOTAL_ROWS * TOTAL_COLS)) + EPS_ENERGY
    kappa = jnp.broadcast_to(2.0 / mean, (8, 128))
    wire.arrived(rim_group)

    def compare(i):
        m = i - 1
        ur, ui = add_around(w1, rim, i, 0.2)
        k = scaled(m, kappa)
        for part, u in ((0, ur), (1, ui)):
            side = jnp.where(lane < 64, beside[0, part, strided(m), :], beside[1, part, strided(m), :])
            seen = jnp.concatenate([meas[part, :, strided(m), :], side[None]], axis=0)
            adj[part, i] = k * (u - seen)

    sweep(compare)
    wrap(adj)
    first_sweep(adj, -0.5)

    def back(i):
        m = i - 1
        gr, gi = add_around(adj, rim, i, -0.2)
        grad = gi * w1[0, i] - gr * w1[1, i]
        grads[1, :, strided(m), :] = grad[:NLB]
        co, si = trig[1, 0, :, strided(m), :], trig[1, 1, :, strided(m), :]
        back1[0, i] = gr * co + gi * si
        back1[1, i] = gi * co - gr * si

    sweep(back)
    wrap(back1)
    first_sweep(back1, -0.5)

    def finish(i):
        gr, gi = add_around(back1, rim, i, -0.2)
        grad = gi * w0[0, i] - gr * w0[1, i]
        grads[0, :, strided(i - 1), :] = grad[:NLB]

    sweep(finish)

    bufs = ((t1a, t2a, suma, t3a, t4a), (t1b, t2b, sumb, t3b, t4b))
    sums = [Scatter(wire, place, grads, unit, b) for unit, b in zip(RS_UNITS, bufs)]
    for s in sums:
        s.start_first()
    for s in sums:
        s.middle_first()
    for s in sums:
        s.start_second()
    for s in sums:
        s.middle_second()
    for s in sums:
        wire.arrived(s.r4)
    for plane in (0, 1):
        blocks = sums[0].end_second(plane) + sums[1].end_second(plane)
        for b, block in enumerate(swapped(blocks)):
            out[plane, :, 128 * b : 128 * (b + 1)] = block
    wire.all_sent()


def per_device(phase_delay, angles, measured):
    f32 = jnp.float32
    field = pltpu.VMEM((2, STEPS + 2, NLB + 1, 8, 128), f32)
    scratch = [
        pltpu.VMEM((2, EXT, COLS + 128), f32),
        pltpu.VMEM((2, 2, NLB + 1, EXT, 128), f32),
        pltpu.VMEM((2, 8, COLS), f32),
        pltpu.VMEM((2, 2, 8, 128), f32),
        pltpu.VMEM((2, ROWS, COLS), jnp.bfloat16),
        pltpu.VMEM((2, NLB, EXT, 128), f32),
        pltpu.VMEM((2, 2, ROWS, 128), f32),
        pltpu.VMEM((2, 2, EXT, 128), f32),
        field,
        field,
        field,
        field,
        field,
        pltpu.VMEM((2, STEPS, 8, 128), f32),
        pltpu.VMEM((2, NLB + 1, 8, 128), f32),
        pltpu.VMEM((STEPS, 8, 128), f32),
        pltpu.VMEM((2, 8, 128), f32),
        pltpu.VMEM((6, 8, 128), f32),
        pltpu.VMEM((2, NLB, EXT, 128), f32),
        pltpu.VMEM((SPAN, 8, 128), f32),
    ]
    for b0, b1, _ in RS_UNITS:
        n = b1 - b0
        scratch += [
            pltpu.VMEM((2, 4, n, 8, 128), f32),
            pltpu.VMEM((2, 4, 2, n, 8, 128), f32),
            pltpu.VMEM((4, 2, n, 8, 128), f32),
            pltpu.VMEM((2, n, 8, 128), f32),
            pltpu.VMEM((2, 2, n, 8, 128), f32),
        ]
    scratch += [
        pltpu.SemaphoreType.DMA((2,)),
        pltpu.SemaphoreType.DMA((1,)),
        pltpu.SemaphoreType.DMA((N_SEM,)),
    ]
    return pl.pallas_call(
        kernel,
        out_shape=jax.ShapeDtypeStruct(phase_delay.shape, f32),
        in_specs=[
            pl.BlockSpec(memory_space=pl.ANY),
            pl.BlockSpec(memory_space=pltpu.SMEM),
            pl.BlockSpec(memory_space=pl.ANY),
        ],
        out_specs=pl.BlockSpec(memory_space=pltpu.VMEM),
        scratch_shapes=scratch,
        compiler_params=pltpu.CompilerParams(
            collective_id=0, has_side_effects=True, vmem_limit_bytes=56 << 20
        ),
        name="tomography",
    )(phase_delay, angles, measured)


def solution(mesh):
    placed = (P(None, ("row", "illum"), "col"), P("illum", None), P(None, "illum", "row", "col"))
    return jax.shard_map(
        per_device,
        mesh=mesh,
        in_specs=placed,
        out_specs=P(None, ("row", "illum"), "col"),
        check_vma=False,
    )
```

```python
import math

import jax
import jax.numpy as jnp
from jax import lax
from jax.experimental import pallas as pl
from jax.experimental.pallas import tpu as pltpu
from jax.sharding import PartitionSpec as P

ROWS, COLS, NLB = 128, 1024, 8
EXT, STEPS = 144, 18
TOTAL_ROWS, TOTAL_COLS = 512, 4096
EPS_ENERGY = 1e-06
MESH = pl.DeviceIdType.MESH
AG_UNITS = ((0, 7, "zx"), (7, 9, "xz"))
RS_UNITS = ((0, 6, "xz"), (6, 8, "zx"))
N_SEM = 60
UNROLL = 9
SPAN = 720


def sincos(x):
    t = x * x
    s = 0.008333314069458244 + t * (-0.00019835866408867098 + t * 2.6937597583896155e-06)
    s = x * (0.9999999999519255 + t * (-0.1666666642612366 + t * s))
    c = 0.04166645537534636 + t * (-0.0013882960343216638 + t * 2.4121201083497457e-05)
    c = 0.9999999994728761 + t * (-0.4999999736217199 + t * c)
    return s, c


class Place:
    def __init__(self):
        illum = lax.axis_index("illum")
        self.zh, self.x = illum // 4, lax.rem(illum, 4)
        self.y, self.c = lax.axis_index("row"), lax.axis_index("col")

    def block(self, dz, dx):
        return lax.rem(self.zh + dz + 4, 4) * 4 + lax.rem(self.x + dx + 4, 4)

    def rows(self, dz, dx):
        return pl.ds(pl.multiple_of(8 * self.block(dz, dx), 8), 8)

    def illum(self, dz, dx):
        return {"illum": self.block(dz, dx)}

    def tile(self, dy, dc):
        return {"row": lax.rem(self.y + dy + 4, 4), "col": lax.rem(self.c + dc + 4, 4)}


class Wire:
    def __init__(self, send, recv, span):
        self.send, self.recv, self.span = send, recv, span
        self.sent, self.groups = 0, []

    def group(self):
        self.groups.append(0)
        return len(self.groups) - 1

    def start(self, src, dst, device, group):
        tiles = math.prod(src.shape) // 1024
        self.sent += tiles
        self.groups[group] += tiles
        pltpu.make_async_remote_copy(
            src_ref=src,
            dst_ref=dst,
            send_sem=self.send.at[0],
            recv_sem=self.recv.at[group],
            device_id=device,
            device_id_type=MESH,
        ).start()

    def wait_for(self, sem, tiles):
        part = self.span.at[:tiles]
        pltpu.make_async_copy(part, part, sem).wait()

    def arrived(self, group):
        self.wait_for(self.recv.at[group], self.groups[group])

    def all_sent(self):
        self.wait_for(self.send.at[0], self.sent)


class Gather:
    def __init__(self, wire, place, planes, trig, plane, unit):
        self.w, self.p, self.planes, self.trig, self.plane = wire, place, planes, trig, plane
        self.b0, self.b1, self.order = unit
        self.mid = (self.b0 + self.b1) // 2
        self.first = [wire.group() for _ in range(2)]
        self.second = {da: wire.group() for da in (0, -1, 1, 2)}
        self.last = wire.group()

    def pos(self, da, db):
        return (da, db) if self.order == "zx" else (db, da)

    def send(self, da, db, step, group, half=None):
        rows = self.p.rows(*self.pos(da, db))
        b0, b1 = ((self.b0, self.b1), (self.b0, self.mid), (self.mid, self.b1))[half or 0]
        ref = self.planes.at[self.plane, rows, 128 * b0 : 128 * b1]
        self.w.start(ref, ref, self.p.illum(*self.pos(*step)), group)

    def start(self):
        self.send(0, 0, (1, 0), self.first[0])
        self.send(0, 0, (-1, 0), self.first[0])
        self.start_second(0)

    def relay_first(self):
        self.w.arrived(self.first[0])
        self.send(-1, 0, (1, 0), self.first[1], 1)
        self.send(1, 0, (-1, 0), self.first[1], 2)
        self.start_second(-1)
        self.start_second(1)

    def end_first(self):
        self.w.arrived(self.first[1])
        self.start_second(2)

    def start_second(self, da):
        self.send(da, 0, (0, 1), self.second[da])
        self.send(da, 0, (0, -1), self.second[da])

    def relay_second(self, *das):
        for da in das:
            self.w.arrived(self.second[da])
            self.send(da, -1, (0, 1), self.last, 1)
            self.send(da, 1, (0, -1), self.last, 2)

    def end(self):
        self.w.arrived(self.last)

    def turn(self, das, dbs):
        for da in das:
            for db in dbs:
                rows = self.p.rows(*self.pos(da, db))
                turn_rows(self.planes, self.trig, self.plane, rows, self.b0, self.b1)


def turn_rows(planes, trig, plane, rows, b0, b1):
    s, c = sincos(planes[plane, rows, 128 * b0 : 128 * b1])
    for b in range(b0, b1):
        at = slice(128 * (b - b0), 128 * (b - b0 + 1))
        trig[plane, 0, b, rows, :] = c[:, at]
        trig[plane, 1, b, rows, :] = s[:, at]


class Scatter:
    def __init__(self, wire, place, grads, plane, unit, bufs):
        self.w, self.p, self.g, self.plane = wire, place, grads, plane
        self.b0, self.b1, self.order = unit
        self.n, self.h = self.b1 - self.b0, (self.b1 - self.b0) // 2
        self.t1, self.t2, self.sums, self.t3, self.t4 = bufs
        one, two = (wire.group() for _ in range(2))
        self.r1 = {2: one, 1: one, 3: two, 0: two}
        one, two = (wire.group() for _ in range(2))
        self.r2 = {2: one, 1: one, 3: two, 0: two}
        self.r3, self.r4 = wire.group(), wire.group()

    def pos(self, da, db):
        return (da, db) if self.order == "zx" else (db, da)

    def part(self, da, dq, half=0):
        m = self.b0 + self.h
        lanes = (slice(self.b0, self.b1), slice(self.b0, m), slice(m, self.b1))[half]
        return (self.plane, lanes, self.p.rows(*self.pos(da, dq)), slice(None))

    def send(self, src, dst, da, db, group):
        self.w.start(src, dst, self.p.illum(*self.pos(da, db)), group)

    def start_first(self):
        for dq in (2, 1, 3, 0):
            self.send(self.g.at[self.part(2, dq, 1)], self.t1.at[0, dq], 1, 0, self.r1[dq])
            self.send(self.g.at[self.part(2, dq, 2)], self.t1.at[1, dq], -1, 0, self.r1[dq])

    def early_first(self):
        for dq in (2, 1, 3, 0):
            self.send(self.g.at[self.part(1, dq, 2)], self.t2.at[0, dq, self.h :], 1, 0, self.r2[dq])
            self.send(self.g.at[self.part(-1, dq, 1)], self.t2.at[1, dq, : self.h], -1, 0, self.r2[dq])

    def middle_first(self):
        for dq in (2, 1, 3, 0):
            if dq in (2, 3):
                self.w.arrived(self.r1[dq])
            at = self.part(1, dq, 1)
            self.g[at] = self.g[at] + self.t1[0, dq]
            at = self.part(-1, dq, 2)
            self.g[at] = self.g[at] + self.t1[1, dq]
        for dq in (2, 1, 3, 0):
            self.send(self.g.at[self.part(1, dq, 1)], self.t2.at[0, dq, : self.h], 1, 0, self.r2[dq])
            self.send(self.g.at[self.part(-1, dq, 2)], self.t2.at[1, dq, self.h :], -1, 0, self.r2[dq])

    def add_first(self, dq):
        self.sums[dq] = self.g[self.part(0, dq)] + self.t2[0, dq] + self.t2[1, dq]

    def start_second(self):
        h = self.h
        self.w.arrived(self.r2[2])
        self.add_first(2)
        self.add_first(1)
        self.send(self.sums.at[2, :h], self.t3.at[0], 0, 1, self.r3)
        self.send(self.sums.at[2, h:], self.t3.at[1], 0, -1, self.r3)
        self.w.arrived(self.r2[3])
        self.add_first(3)
        self.send(self.sums.at[1, h:], self.t4.at[0, h:], 0, 1, self.r4)
        self.send(self.sums.at[3, :h], self.t4.at[1, :h], 0, -1, self.r4)
        self.add_first(0)

    def middle_second(self):
        h = self.h
        self.w.arrived(self.r3)
        self.sums[1, :h] = self.sums[1, :h] + self.t3[0]
        self.sums[3, h:] = self.sums[3, h:] + self.t3[1]
        self.send(self.sums.at[1, :h], self.t4.at[0, :h], 0, 1, self.r4)
        self.send(self.sums.at[3, h:], self.t4.at[1, h:], 0, -1, self.r4)

    def end_second(self):
        self.w.arrived(self.r4)
        total = self.sums[0] + self.t4[0] + self.t4[1]
        return [total[b] for b in range(self.n)]


def strided(m):
    return pl.ds(m, 8, stride=STEPS)


def swapped(blocks):
    blocks = list(blocks)
    lane = lanes_of(blocks[0].shape)
    last = lane.ndim - 1
    for k in (1, 2, 4):
        low = jnp.bitwise_and(lane, k) == 0
        for b in range(NLB):
            if not b & k:
                one, two = blocks[b], blocks[b | k]
                blocks[b] = jnp.where(low, one, pltpu.roll(two, k, last))
                blocks[b | k] = jnp.where(low, pltpu.roll(one, 128 - k, last), two)
    return blocks


def split(x):
    return [x[..., 128 * b : 128 * (b + 1)] for b in range(NLB)]


def lanes_of(shape):
    return lax.broadcasted_iota(jnp.int32, shape, len(shape) - 1)


def kernel(
    phase_hbm, angles, meas_hbm, out,
    planes, trig, fresh, edges, raw, meas, rims, beside, w0, w1, rim, adj, back1, rowf, colf, rowm, energy, energy_in,
    grads, span, *rest,
):
    *bufs, local, send, recv = rest
    place = Place()
    wire = Wire(send, recv, span)
    own = place.rows(0, 0)
    fetch = [
        pltpu.make_async_copy(phase_hbm, fresh, local.at[0]),
        pltpu.make_async_copy(meas_hbm.at[:, 0], raw, local.at[1]),
    ]
    partners = [place.illum(1, 0), place.illum(-1, 0), place.illum(0, 1), place.illum(0, -1)]
    partners += [place.tile(d, 0) for d in (1, 2, 3)] + [place.tile(0, d) for d in (1, 2, 3)]
    partners += [place.tile(d, e) for d in (1, -1) for e in (1, -1)]
    barrier = pltpu.get_barrier_semaphore()
    for device in partners:
        pl.semaphore_signal(barrier, inc=1, device_id=device, device_id_type=MESH)
    for copy in fetch:
        copy.start()
    pl.semaphore_wait(barrier, len(partners))

    edge_group = wire.group()
    wire.start(phase_hbm.at[:, :, :128], edges.at[0], place.tile(0, -1), edge_group)
    wire.start(phase_hbm.at[:, :, COLS - 128 :], edges.at[1], place.tile(0, 1), edge_group)
    units = [[Gather(wire, place, planes, trig, plane, u) for u in AG_UNITS] for plane in (0, 1)]
    (main0, side0), (main1, side1) = units
    fetch[0].wait()
    for b, block in enumerate(swapped(split(fresh[...]))):
        planes[:, own, 128 * b : 128 * (b + 1)] = block
    main0.start()
    main1.start()
    wire.arrived(edge_group)
    lane = lanes_of((2, 8, 128))
    planes[:, own, COLS:] = jnp.where(lane < 64, pltpu.roll(edges[0], 8, 2), pltpu.roll(edges[1], 120, 2))
    side0.start()
    side1.start()
    main0.turn((0,), (0,))
    main1.turn((0,), (0,))

    fetch[1].wait()
    energy[0] = jnp.zeros((8, 128), jnp.float32)

    def widen(g, carry):
        rows = pl.ds(pl.multiple_of(16 * g, 16), 16)
        for part in (0, 1):
            x = raw[part, rows, :].astype(jnp.float32)
            squares = x * x
            blocks = split(x)
            rims[0, part, rows, :] = pltpu.roll(blocks[0], 8, 1)
            rims[1, part, rows, :] = pltpu.roll(blocks[NLB - 1], 120, 1)
            for b, block in enumerate(swapped(blocks)):
                meas[part, b, rows, :] = block
            half = squares[:8] + squares[8:]
            total = half[:, :128]
            for b in range(1, NLB):
                total = total + half[:, 128 * b : 128 * (b + 1)]
            energy[0] = energy[0] + total
        return carry

    lax.fori_loop(0, ROWS // 16, widen, 0)

    step_a, step_b = angles[0, 0], angles[0, 1]
    lane = lanes_of((8, 128))

    def circle(steps, period):
        turns = jnp.bitwise_and(steps + period // 2, period - 1) - period // 2
        s, c = sincos(turns.astype(jnp.float32) * (0.5 * math.pi / period))
        s, c = 2.0 * s * c, 1.0 - 2.0 * s * s
        return 2.0 * s * c, 1.0 - 2.0 * s * s

    def col_of(b):
        edge = jnp.where(lane < 64, COLS - 8 + lane, lane - 120)
        inner = 128 * jnp.bitwise_and(lane, 7) + jnp.bitwise_and(lane, -8) + b
        return place.c * COLS + (inner if b < NLB else edge)

    def factors():
        shape = (STEPS, 8, 128)
        r = lax.broadcasted_iota(jnp.int32, shape, 1) * STEPS + lax.broadcasted_iota(jnp.int32, shape, 0)
        gr = place.y * ROWS + jnp.where(r < 136, r, r - EXT)
        inside = jnp.where((gr >= 0) & (gr < TOTAL_ROWS), 1.0, 0.0)
        si, co = circle(step_a * gr, TOTAL_ROWS)
        rowf[0] = inside * (-0.28 * co - 0.96 * si)
        rowf[1] = inside * (0.96 * co - 0.28 * si)
        rowm[...] = inside
        gc = jnp.stack([col_of(b) for b in range(NLB + 1)])
        inside = jnp.where((gc >= 0) & (gc < TOTAL_COLS), 1.0, 0.0)
        si, co = circle(step_b * gc, TOTAL_COLS)
        colf[0] = inside * co
        colf[1] = inside * si

    main0.relay_second(0)
    side0.relay_first()
    main1.relay_second(0)
    side1.relay_first()
    main0.relay_first()
    side0.end_first()
    side1.end_first()
    main0.turn((0,), (-1, 1))
    main0.turn((-1, 1), (0,))
    factors()
    main1.relay_first()
    side0.relay_second(0)
    main0.end_first()
    main0.relay_second(-1, 1)
    side1.relay_second(0)
    side0.relay_second(-1, 1)
    main1.end_first()
    main0.turn((-1, 1), (-1, 1))
    main0.turn((2,), (0,))
    side0.relay_second(2)
    main0.relay_second(2)
    main1.relay_second(-1, 1)
    side0.turn((0, -1, 1, 2), (0, -1, 1))
    side1.relay_second(-1, 1, 2)

    last, first = slice(120, 128), slice(0, 8)
    after, before = slice(128, 136), slice(136, 144)
    end_groups = [wire.group(), wire.group()]

    def share_ends(plane):
        ref = planes.at[plane]
        for unit in units[plane]:
            unit.end()
        wire.start(ref.at[last, :], ref.at[before, :], place.tile(1, 0), end_groups[plane])
        wire.start(ref.at[first, :], ref.at[after, :], place.tile(-1, 0), end_groups[plane])

    def turn_ends(plane):
        wire.arrived(end_groups[plane])
        turn_rows(planes, trig, plane, slice(128, 144), 0, NLB + 1)

    share_ends(0)
    main1.relay_second(2)
    energy_group = wire.group()
    for d in (1, 2, 3):
        wire.start(energy.at[0], energy_in.at[d - 1], place.tile(d, 0), energy_group)
    rim_group = wire.group()
    tile_rows = slice(0, 128)
    wire.start(meas.at[:, :, last, :], meas.at[:, :, before, :], place.tile(1, 0), rim_group)
    wire.start(meas.at[:, :, first, :], meas.at[:, :, after, :], place.tile(-1, 0), rim_group)
    for side, dc in ((0, -1), (1, 1)):
        src, dst = rims.at[side], beside.at[side]
        wire.start(src.at[:, tile_rows, :], dst.at[:, tile_rows, :], place.tile(0, dc), rim_group)
        wire.start(src.at[:, last, :], dst.at[:, before, :], place.tile(1, dc), rim_group)
        wire.start(src.at[:, first, :], dst.at[:, after, :], place.tile(-1, dc), rim_group)
    main0.turn((2,), (-1, 1))
    main0.turn((0, -1, 1, 2), (2,))
    side0.turn((0, -1, 1, 2), (2,))
    main1.turn((0,), (-1, 1))
    main1.turn((-1, 1), (-1, 0, 1))
    main1.turn((2,), (0,))
    side1.turn((0, -1, 1, 2), (0, -1, 1))
    turn_ends(0)

    gc8 = col_of(NLB)
    col_in = jnp.where((gc8 >= 0) & (gc8 < TOTAL_COLS), 1.0, 0.0)

    def scaled(m, amount):
        k = rowm[m] * amount
        return jnp.concatenate([jnp.broadcast_to(k[None], (NLB, 8, 128)), (k * col_in)[None]], axis=0)

    def around(field, part, i):
        mid = field[part, i]
        first, last, edge = mid[0], mid[NLB - 1], mid[NLB]
        ahead = pltpu.roll(jnp.where(lane == 8, edge, first), 119, 1)
        behind = pltpu.roll(jnp.where(lane == 119, edge, last), 9, 1)
        right_last = jnp.where(lane < 120, pltpu.roll(first, 120, 1), ahead)
        left_first = jnp.where(lane < 8, behind, pltpu.roll(last, 8, 1))
        right_edge = jnp.where(lane == 119, ahead, pltpu.roll(edge, 127, 1))
        left_edge = jnp.where(lane == 8, behind, pltpu.roll(edge, 1, 1))
        right = jnp.concatenate([mid[1:NLB], right_last[None], right_edge[None]], axis=0)
        left = jnp.concatenate([left_first[None], mid[: NLB - 1], left_edge[None]], axis=0)
        return (field[part, i - 1] + field[part, i + 1]) + (right + left)

    def wrap(field):
        for part in (0, 1):
            field[part, 0] = pltpu.roll(field[part, STEPS], 1, 1)
            field[part, STEPS + 1] = pltpu.roll(field[part, 1], 7, 1)

    def add_around(base, field, i, amount):
        k = scaled(i - 1, amount)
        real = base[0, i] - k * around(field, 1, i)
        imag = base[1, i] + k * around(field, 0, i)
        return real, imag

    def sweep(body):
        def several(t, carry):
            for k in range(UNROLL):
                body(UNROLL * t + k + 1)
            return carry

        lax.fori_loop(0, STEPS // UNROLL, several, 0)

    def enter(i):
        m = i - 1
        co, si = trig[0, 0, :, strided(m), :], trig[0, 1, :, strided(m), :]
        fr, fi = rowf[0, m], rowf[1, m]
        cr, ci = colf[0], colf[1]
        ur = fr[None] * cr - fi[None] * ci
        ui = fr[None] * ci + fi[None] * cr
        w0[0, i] = ur * co - ui * si
        w0[1, i] = ur * si + ui * co

    def first_sweep(base, amount):
        def body(i):
            rim[0, i], rim[1, i] = add_around(base, base, i, amount)

        sweep(body)
        wrap(rim)

    sweep(enter)
    share_ends(1)
    wrap(w0)
    first_sweep(w0, 0.5)
    main1.turn((2,), (-1, 1))
    main1.turn((0, -1, 1, 2), (2,))
    side1.turn((0, -1, 1, 2), (2,))
    turn_ends(1)

    def between(i):
        ur, ui = add_around(w0, rim, i, 0.2)
        m = i - 1
        co, si = trig[1, 0, :, strided(m), :], trig[1, 1, :, strided(m), :]
        w1[0, i] = ur * co - ui * si
        w1[1, i] = ur * si + ui * co

    sweep(between)
    wire.arrived(energy_group)
    energy[1] = energy[0] + energy_in[0] + energy_in[1] + energy_in[2]
    energy_group = wire.group()
    for d in (1, 2, 3):
        wire.start(energy.at[1], energy_in.at[2 + d], place.tile(0, d), energy_group)
    wrap(w1)
    first_sweep(w1, 0.5)

    wire.arrived(energy_group)
    total = energy[1] + energy_in[3] + energy_in[4] + energy_in[5]
    mean = jnp.sum(total, keepdims=True) * (1.0 / (TOTAL_ROWS * TOTAL_COLS)) + EPS_ENERGY
    kappa = jnp.broadcast_to(2.0 / mean, (8, 128))
    wire.arrived(rim_group)

    def compare(i):
        m = i - 1
        ur, ui = add_around(w1, rim, i, 0.2)
        k = scaled(m, kappa)
        for part, u in ((0, ur), (1, ui)):
            side = jnp.where(lane < 64, beside[0, part, strided(m), :], beside[1, part, strided(m), :])
            seen = jnp.concatenate([meas[part, :, strided(m), :], side[None]], axis=0)
            adj[part, i] = k * (u - seen)

    sweep(compare)
    wrap(adj)
    first_sweep(adj, -0.5)

    def back(i):
        m = i - 1
        gr, gi = add_around(adj, rim, i, -0.2)
        grad = gi * w1[0, i] - gr * w1[1, i]
        grads[1, :, strided(m), :] = grad[:NLB]
        co, si = trig[1, 0, :, strided(m), :], trig[1, 1, :, strided(m), :]
        back1[0, i] = gr * co + gi * si
        back1[1, i] = gi * co - gr * si

    sweep(back)
    late, early = (
        [Scatter(wire, place, grads, plane, u, bufs[5 * k : 5 * k + 5]) for k, u in pairs]
        for plane, pairs in ((0, tuple(enumerate(RS_UNITS))), (1, tuple(enumerate(RS_UNITS, 2))))
    )
    for s in early:
        s.start_first()
    for s in early:
        s.early_first()
    wrap(back1)
    first_sweep(back1, -0.5)

    def finish(i):
        gr, gi = add_around(back1, rim, i, -0.2)
        grad = gi * w0[0, i] - gr * w0[1, i]
        grads[0, :, strided(i - 1), :] = grad[:NLB]

    sweep(finish)

    for s in late:
        s.start_first()
    for s in early:
        s.middle_first()
    for s in late:
        s.early_first()
    for s in late:
        s.middle_first()
    for s in early:
        s.start_second()
    for s in late:
        s.start_second()
    for s in early:
        s.middle_second()
    for s in late:
        s.middle_second()
    for plane, parts in ((1, early), (0, late)):
        blocks = [block for s in parts for block in s.end_second()]
        for b, block in enumerate(swapped(blocks)):
            out[plane, :, 128 * b : 128 * (b + 1)] = block
    wire.all_sent()


def per_device(phase_delay, angles, measured):
    f32 = jnp.float32
    field = pltpu.VMEM((2, STEPS + 2, NLB + 1, 8, 128), f32)
    scratch = [
        pltpu.VMEM((2, EXT, COLS + 128), f32),
        pltpu.VMEM((2, 2, NLB + 1, EXT, 128), f32),
        pltpu.VMEM((2, 8, COLS), f32),
        pltpu.VMEM((2, 2, 8, 128), f32),
        pltpu.VMEM((2, ROWS, COLS), jnp.bfloat16),
        pltpu.VMEM((2, NLB, EXT, 128), f32),
        pltpu.VMEM((2, 2, ROWS, 128), f32),
        pltpu.VMEM((2, 2, EXT, 128), f32),
        field,
        field,
        field,
        field,
        field,
        pltpu.VMEM((2, STEPS, 8, 128), f32),
        pltpu.VMEM((2, NLB + 1, 8, 128), f32),
        pltpu.VMEM((STEPS, 8, 128), f32),
        pltpu.VMEM((2, 8, 128), f32),
        pltpu.VMEM((6, 8, 128), f32),
        pltpu.VMEM((2, NLB, EXT, 128), f32),
        pltpu.VMEM((SPAN, 8, 128), f32),
    ]
    for b0, b1, _ in RS_UNITS * 2:
        n = b1 - b0
        scratch += [
            pltpu.VMEM((2, 4, n // 2, 8, 128), f32),
            pltpu.VMEM((2, 4, n, 8, 128), f32),
            pltpu.VMEM((4, n, 8, 128), f32),
            pltpu.VMEM((2, n // 2, 8, 128), f32),
            pltpu.VMEM((2, n, 8, 128), f32),
        ]
    scratch += [
        pltpu.SemaphoreType.DMA((2,)),
        pltpu.SemaphoreType.DMA((1,)),
        pltpu.SemaphoreType.DMA((N_SEM,)),
    ]
    return pl.pallas_call(
        kernel,
        out_shape=jax.ShapeDtypeStruct(phase_delay.shape, f32),
        in_specs=[
            pl.BlockSpec(memory_space=pl.ANY),
            pl.BlockSpec(memory_space=pltpu.SMEM),
            pl.BlockSpec(memory_space=pl.ANY),
        ],
        out_specs=pl.BlockSpec(memory_space=pltpu.VMEM),
        scratch_shapes=scratch,
        compiler_params=pltpu.CompilerParams(
            collective_id=0, has_side_effects=True, vmem_limit_bytes=56 << 20
        ),
        name="tomography",
    )(phase_delay, angles, measured)


def solution(mesh):
    placed = (P(None, ("row", "illum"), "col"), P("illum", None), P(None, "illum", "row", "col"))
    return jax.shard_map(
        per_device,
        mesh=mesh,
        in_specs=placed,
        out_specs=P(None, ("row", "illum"), "col"),
        check_vma=False,
    )
```

```python
import math

import jax
import jax.numpy as jnp
from jax import lax
from jax.experimental import pallas as pl
from jax.experimental.pallas import tpu as pltpu
from jax.sharding import PartitionSpec as P

ROWS, COLS, NLB = 128, 1024, 8
EXT, STEPS = 144, 18
TOTAL_ROWS, TOTAL_COLS = 512, 4096
EPS_ENERGY = 1e-06
MESH = pl.DeviceIdType.MESH
AG_UNITS = ((0, 6, "zx", True, True), (6, 8, "xz", False, True))
HALO_UNIT = (8, 9, "zx", False, False)
RS_UNITS = ((0, 6, "xz"), (6, 8, "zx"))
N_SEM = 62
UNROLL = 9
SPAN = 720


def sincos(x):
    t = x * x
    s = 0.008333314069458244 + t * (-0.00019835866408867098 + t * 2.6937597583896155e-06)
    s = x * (0.9999999999519255 + t * (-0.1666666642612366 + t * s))
    c = 0.04166645537534636 + t * (-0.0013882960343216638 + t * 2.4121201083497457e-05)
    c = 0.9999999994728761 + t * (-0.4999999736217199 + t * c)
    return s, c


class Place:
    def __init__(self):
        illum = lax.axis_index("illum")
        self.zh, self.x = illum // 4, lax.rem(illum, 4)
        self.y, self.c = lax.axis_index("row"), lax.axis_index("col")

    def block(self, dz, dx):
        return lax.rem(self.zh + dz + 4, 4) * 4 + lax.rem(self.x + dx + 4, 4)

    def rows(self, dz, dx):
        return pl.ds(pl.multiple_of(8 * self.block(dz, dx), 8), 8)

    def illum(self, dz, dx):
        return {"illum": self.block(dz, dx)}

    def tile(self, dy, dc):
        return {"row": lax.rem(self.y + dy + 4, 4), "col": lax.rem(self.c + dc + 4, 4)}


class Wire:
    def __init__(self, send, recv, span):
        self.send, self.recv, self.span = send, recv, span
        self.sent, self.groups = 0, []

    def group(self):
        self.groups.append(0)
        return len(self.groups) - 1

    def start(self, src, dst, device, group):
        tiles = math.prod(src.shape) // 1024
        self.sent += tiles
        self.groups[group] += tiles
        pltpu.make_async_remote_copy(
            src_ref=src,
            dst_ref=dst,
            send_sem=self.send.at[0],
            recv_sem=self.recv.at[group],
            device_id=device,
            device_id_type=MESH,
        ).start()

    def wait_for(self, sem, tiles):
        part = self.span.at[:tiles]
        pltpu.make_async_copy(part, part, sem).wait()

    def arrived(self, group):
        self.wait_for(self.recv.at[group], self.groups[group])

    def all_sent(self):
        self.wait_for(self.send.at[0], self.sent)


class Gather:
    def __init__(self, wire, place, planes, trig, plane, unit):
        self.w, self.p, self.planes, self.trig, self.plane = wire, place, planes, trig, plane
        self.b0, self.b1, self.order, *self.relays = unit
        self.mid = (self.b0 + self.b1) // 2
        self.first = [wire.group() for _ in range(1 + self.relays[0])]
        self.second = {da: wire.group() for da in (0, -1, 1, 2)}
        if self.relays[1]:
            self.last = wire.group()

    def pos(self, da, db):
        return (da, db) if self.order == "zx" else (db, da)

    def send(self, da, db, step, group, half=None):
        rows = self.p.rows(*self.pos(da, db))
        b0, b1 = ((self.b0, self.b1), (self.b0, self.mid), (self.mid, self.b1))[half or 0]
        lead = slice(None) if self.plane is None else self.plane
        ref = self.planes.at[lead, rows, 128 * b0 : 128 * b1]
        self.w.start(ref, ref, self.p.illum(*self.pos(*step)), group)

    def start(self):
        self.send(0, 0, (1, 0), self.first[0])
        self.send(0, 0, (-1, 0), self.first[0])
        if not self.relays[0]:
            self.send(0, 0, (2, 0), self.first[0])
        self.start_second(0)

    def relay_first(self):
        self.w.arrived(self.first[0])
        if self.relays[0]:
            self.send(-1, 0, (1, 0), self.first[1], 1)
            self.send(1, 0, (-1, 0), self.first[1], 2)
        else:
            self.start_second(2)
        self.start_second(-1)
        self.start_second(1)

    def end_first(self):
        self.w.arrived(self.first[1])
        self.start_second(2)

    def start_second(self, da):
        self.send(da, 0, (0, 1), self.second[da])
        self.send(da, 0, (0, -1), self.second[da])
        if not self.relays[1]:
            self.send(da, 0, (0, 2), self.second[da])

    def relay_second(self, *das):
        for da in das:
            self.w.arrived(self.second[da])
            if self.relays[1]:
                self.send(da, -1, (0, 1), self.last, 1)
                self.send(da, 1, (0, -1), self.last, 2)

    def end(self):
        self.w.arrived(self.last)

    def turn(self, das, dbs):
        for da in das:
            for db in dbs:
                rows = self.p.rows(*self.pos(da, db))
                for plane in (0, 1) if self.plane is None else (self.plane,):
                    turn_rows(self.planes, self.trig, plane, rows, self.b0, self.b1)


def turn_rows(planes, trig, plane, rows, b0, b1):
    s, c = sincos(planes[plane, rows, 128 * b0 : 128 * b1])
    for b in range(b0, b1):
        at = slice(128 * (b - b0), 128 * (b - b0 + 1))
        trig[plane, 0, b, rows, :] = c[:, at]
        trig[plane, 1, b, rows, :] = s[:, at]


class Scatter:
    def __init__(self, wire, place, grads, plane, unit, bufs):
        self.w, self.p, self.g, self.plane = wire, place, grads, plane
        self.b0, self.b1, self.order = unit
        self.n, self.h = self.b1 - self.b0, (self.b1 - self.b0) // 2
        self.t1, self.t2, self.sums, self.t3, self.t4 = bufs
        one, two = (wire.group() for _ in range(2))
        self.r1 = {2: one, 1: one, 3: two, 0: two}
        one, two = (wire.group() for _ in range(2))
        self.r2 = {2: one, 1: one, 3: two, 0: two}
        self.r3, self.r4 = wire.group(), wire.group()

    def pos(self, da, db):
        return (da, db) if self.order == "zx" else (db, da)

    def part(self, da, dq, half=0):
        m = self.b0 + self.h
        lanes = (slice(self.b0, self.b1), slice(self.b0, m), slice(m, self.b1))[half]
        return (self.plane, lanes, self.p.rows(*self.pos(da, dq)), slice(None))

    def send(self, src, dst, da, db, group):
        self.w.start(src, dst, self.p.illum(*self.pos(da, db)), group)

    def start_first(self):
        for dq in (2, 1, 3, 0):
            self.send(self.g.at[self.part(2, dq, 1)], self.t1.at[0, dq], 1, 0, self.r1[dq])
            self.send(self.g.at[self.part(2, dq, 2)], self.t1.at[1, dq], -1, 0, self.r1[dq])

    def early_first(self):
        for dq in (2, 1, 3, 0):
            self.send(self.g.at[self.part(1, dq, 2)], self.t2.at[0, dq, self.h :], 1, 0, self.r2[dq])
            self.send(self.g.at[self.part(-1, dq, 1)], self.t2.at[1, dq, : self.h], -1, 0, self.r2[dq])

    def middle_first(self):
        for dq in (2, 1, 3, 0):
            if dq in (2, 3):
                self.w.arrived(self.r1[dq])
            at = self.part(1, dq, 1)
            self.g[at] = self.g[at] + self.t1[0, dq]
            at = self.part(-1, dq, 2)
            self.g[at] = self.g[at] + self.t1[1, dq]
        for dq in (2, 1, 3, 0):
            self.send(self.g.at[self.part(1, dq, 1)], self.t2.at[0, dq, : self.h], 1, 0, self.r2[dq])
            self.send(self.g.at[self.part(-1, dq, 2)], self.t2.at[1, dq, self.h :], -1, 0, self.r2[dq])

    def add_first(self, dq):
        self.sums[dq] = self.g[self.part(0, dq)] + self.t2[0, dq] + self.t2[1, dq]

    def start_second(self):
        h = self.h
        self.w.arrived(self.r2[2])
        self.add_first(2)
        self.add_first(1)
        self.send(self.sums.at[2, :h], self.t3.at[0], 0, 1, self.r3)
        self.send(self.sums.at[2, h:], self.t3.at[1], 0, -1, self.r3)
        self.w.arrived(self.r2[3])
        self.add_first(3)
        self.send(self.sums.at[1, h:], self.t4.at[0, h:], 0, 1, self.r4)
        self.send(self.sums.at[3, :h], self.t4.at[1, :h], 0, -1, self.r4)
        self.add_first(0)

    def middle_second(self):
        h = self.h
        self.w.arrived(self.r3)
        self.sums[1, :h] = self.sums[1, :h] + self.t3[0]
        self.sums[3, h:] = self.sums[3, h:] + self.t3[1]
        self.send(self.sums.at[1, :h], self.t4.at[0, :h], 0, 1, self.r4)
        self.send(self.sums.at[3, h:], self.t4.at[1, h:], 0, -1, self.r4)

    def end_second(self):
        self.w.arrived(self.r4)
        total = self.sums[0] + self.t4[0] + self.t4[1]
        return [total[b] for b in range(self.n)]


def strided(m):
    return pl.ds(m, 8, stride=STEPS)


def swapped(blocks):
    blocks = list(blocks)
    lane = lanes_of(blocks[0].shape)
    last = lane.ndim - 1
    for k in (1, 2, 4):
        low = jnp.bitwise_and(lane, k) == 0
        for b in range(NLB):
            if not b & k:
                one, two = blocks[b], blocks[b | k]
                blocks[b] = jnp.where(low, one, pltpu.roll(two, k, last))
                blocks[b | k] = jnp.where(low, pltpu.roll(one, 128 - k, last), two)
    return blocks


def split(x):
    return [x[..., 128 * b : 128 * (b + 1)] for b in range(NLB)]


def lanes_of(shape):
    return lax.broadcasted_iota(jnp.int32, shape, len(shape) - 1)


def kernel(
    phase_hbm, angles, meas_hbm, out,
    planes, trig, fresh, edges, raw, meas, rims, beside, w0, w1, rim, adj, back1, rowf, colf, rowm, energy, energy_in,
    grads, span, *rest,
):
    *bufs, local, send, recv = rest
    place = Place()
    wire = Wire(send, recv, span)
    own = place.rows(0, 0)
    fetch = [
        pltpu.make_async_copy(phase_hbm, fresh, local.at[0]),
        pltpu.make_async_copy(meas_hbm.at[:, 0], raw, local.at[1]),
    ]
    partners = [place.illum(1, 0), place.illum(-1, 0), place.illum(0, 1), place.illum(0, -1)]
    partners += [place.illum(2, 0), place.illum(0, 2)]
    partners += [place.tile(d, 0) for d in (1, 2, 3)] + [place.tile(0, d) for d in (1, 2, 3)]
    partners += [place.tile(d, e) for d in (1, -1) for e in (1, -1)]
    barrier = pltpu.get_barrier_semaphore()
    for device in partners:
        pl.semaphore_signal(barrier, inc=1, device_id=device, device_id_type=MESH)
    for copy in fetch:
        copy.start()
    pl.semaphore_wait(barrier, len(partners))

    edge_group = wire.group()
    wire.start(phase_hbm.at[:, :, :128], edges.at[0], place.tile(0, -1), edge_group)
    wire.start(phase_hbm.at[:, :, COLS - 128 :], edges.at[1], place.tile(0, 1), edge_group)
    units = [[Gather(wire, place, planes, trig, plane, u) for u in AG_UNITS] for plane in (0, 1)]
    (main0, side0), (main1, side1) = units
    halo = Gather(wire, place, planes, trig, None, HALO_UNIT)
    fetch[0].wait()
    for b, block in enumerate(swapped(split(fresh[...]))):
        planes[:, own, 128 * b : 128 * (b + 1)] = block
    main0.start()
    side0.start()
    main1.start()
    side1.start()
    wire.arrived(edge_group)
    lane = lanes_of((2, 8, 128))
    planes[:, own, COLS:] = jnp.where(lane < 64, pltpu.roll(edges[0], 8, 2), pltpu.roll(edges[1], 120, 2))
    halo.start()

    fetch[1].wait()
    energy[0] = jnp.zeros((8, 128), jnp.float32)

    def widen(g, carry):
        rows = pl.ds(pl.multiple_of(16 * g, 16), 16)
        for part in (0, 1):
            x = raw[part, rows, :].astype(jnp.float32)
            squares = x * x
            blocks = split(x)
            rims[0, part, rows, :] = pltpu.roll(blocks[0], 8, 1)
            rims[1, part, rows, :] = pltpu.roll(blocks[NLB - 1], 120, 1)
            for b, block in enumerate(swapped(blocks)):
                meas[part, b, rows, :] = block
            half = squares[:8] + squares[8:]
            total = half[:, :128]
            for b in range(1, NLB):
                total = total + half[:, 128 * b : 128 * (b + 1)]
            energy[0] = energy[0] + total
        return carry

    lax.fori_loop(0, ROWS // 16, widen, 0)
    energy_group = wire.group()
    for d in (1, 2, 3):
        wire.start(energy.at[0], energy_in.at[d - 1], place.tile(d, 0), energy_group)

    step_a, step_b = angles[0, 0], angles[0, 1]
    lane = lanes_of((8, 128))

    def circle(steps, period):
        turns = jnp.bitwise_and(steps + period // 2, period - 1) - period // 2
        s, c = sincos(turns.astype(jnp.float32) * (0.5 * math.pi / period))
        s, c = 2.0 * s * c, 1.0 - 2.0 * s * s
        return 2.0 * s * c, 1.0 - 2.0 * s * s

    def col_of(b):
        edge = jnp.where(lane < 64, COLS - 8 + lane, lane - 120)
        inner = 128 * jnp.bitwise_and(lane, 7) + jnp.bitwise_and(lane, -8) + b
        return place.c * COLS + (inner if b < NLB else edge)

    def factors():
        shape = (STEPS, 8, 128)
        r = lax.broadcasted_iota(jnp.int32, shape, 1) * STEPS + lax.broadcasted_iota(jnp.int32, shape, 0)
        gr = place.y * ROWS + jnp.where(r < 136, r, r - EXT)
        inside = jnp.where((gr >= 0) & (gr < TOTAL_ROWS), 1.0, 0.0)
        si, co = circle(step_a * gr, TOTAL_ROWS)
        rowf[0] = inside * (-0.28 * co - 0.96 * si)
        rowf[1] = inside * (0.96 * co - 0.28 * si)
        rowm[...] = inside
        gc = jnp.stack([col_of(b) for b in range(NLB + 1)])
        inside = jnp.where((gc >= 0) & (gc < TOTAL_COLS), 1.0, 0.0)
        si, co = circle(step_b * gc, TOTAL_COLS)
        colf[0] = inside * co
        colf[1] = inside * si

    every, near = (0, -1, 1, 2), (0, -1, 1)
    main0.relay_second(0)
    side0.relay_first()
    main1.relay_second(0)
    side1.relay_first()
    main0.turn((0,), near)
    main0.relay_first()
    halo.turn((0,), (0,))
    halo.relay_first()
    side0.turn(every, (0,))
    main1.relay_first()
    wire.arrived(energy_group)
    energy[1] = energy[0] + energy_in[0] + energy_in[1] + energy_in[2]
    energy_group = wire.group()
    for d in (1, 2, 3):
        wire.start(energy.at[1], energy_in.at[2 + d], place.tile(0, d), energy_group)
    factors()
    main0.turn((-1, 1), (0,))
    side0.relay_second(0)
    main0.end_first()
    side0.relay_second(-1, 1)
    main0.relay_second(-1, 1)
    side1.relay_second(0)
    main1.end_first()
    side0.relay_second(2)
    side1.relay_second(-1, 1)
    main0.turn((-1, 1), (-1, 1))
    main0.turn((2,), (0,))
    main0.relay_second(2)
    main1.relay_second(-1, 1)
    side1.relay_second(2)
    side0.turn(every, (-1, 1))
    halo.relay_second(*every)

    last, first = slice(120, 128), slice(0, 8)
    after, before = slice(128, 136), slice(136, 144)
    end_groups = [wire.group(), wire.group()]

    def share_ends(plane):
        ref = planes.at[plane]
        for unit in units[plane]:
            unit.end()
        wire.start(ref.at[last, :], ref.at[before, :], place.tile(1, 0), end_groups[plane])
        wire.start(ref.at[first, :], ref.at[after, :], place.tile(-1, 0), end_groups[plane])

    def turn_ends(plane):
        wire.arrived(end_groups[plane])
        turn_rows(planes, trig, plane, slice(128, 144), 0, NLB + 1)

    share_ends(0)
    main1.relay_second(2)
    rim_group = wire.group()
    tile_rows = slice(0, 128)
    wire.start(meas.at[:, :, last, :], meas.at[:, :, before, :], place.tile(1, 0), rim_group)
    wire.start(meas.at[:, :, first, :], meas.at[:, :, after, :], place.tile(-1, 0), rim_group)
    for side, dc in ((0, -1), (1, 1)):
        src, dst = rims.at[side], beside.at[side]
        wire.start(src.at[:, tile_rows, :], dst.at[:, tile_rows, :], place.tile(0, dc), rim_group)
        wire.start(src.at[:, last, :], dst.at[:, before, :], place.tile(1, dc), rim_group)
        wire.start(src.at[:, first, :], dst.at[:, after, :], place.tile(-1, dc), rim_group)
    main0.turn((2,), (-1, 1))
    main0.turn(every, (2,))
    side0.turn(every, (2,))
    halo.turn((0,), (-1, 1, 2))
    halo.turn((-1, 1, 2), every)
    main1.turn(near, near)
    main1.turn((2,), (0,))
    side1.turn(every, near)
    turn_ends(0)

    gc8 = col_of(NLB)
    col_in = jnp.where((gc8 >= 0) & (gc8 < TOTAL_COLS), 1.0, 0.0)

    def scaled(m, amount):
        k = rowm[m] * amount
        return jnp.concatenate([jnp.broadcast_to(k[None], (NLB, 8, 128)), (k * col_in)[None]], axis=0)

    def around(field, part, i):
        mid = field[part, i]
        first, last, edge = mid[0], mid[NLB - 1], mid[NLB]
        ahead = pltpu.roll(jnp.where(lane == 8, edge, first), 119, 1)
        behind = pltpu.roll(jnp.where(lane == 119, edge, last), 9, 1)
        right_last = jnp.where(lane < 120, pltpu.roll(first, 120, 1), ahead)
        left_first = jnp.where(lane < 8, behind, pltpu.roll(last, 8, 1))
        right_edge = jnp.where(lane == 119, ahead, pltpu.roll(edge, 127, 1))
        left_edge = jnp.where(lane == 8, behind, pltpu.roll(edge, 1, 1))
        right = jnp.concatenate([mid[1:NLB], right_last[None], right_edge[None]], axis=0)
        left = jnp.concatenate([left_first[None], mid[: NLB - 1], left_edge[None]], axis=0)
        return (field[part, i - 1] + field[part, i + 1]) + (right + left)

    def wrap(field):
        for part in (0, 1):
            field[part, 0] = pltpu.roll(field[part, STEPS], 1, 1)
            field[part, STEPS + 1] = pltpu.roll(field[part, 1], 7, 1)

    def add_around(base, field, i, amount):
        k = scaled(i - 1, amount)
        real = base[0, i] - k * around(field, 1, i)
        imag = base[1, i] + k * around(field, 0, i)
        return real, imag

    def sweep(body):
        def several(t, carry):
            for k in range(UNROLL):
                body(UNROLL * t + k + 1)
            return carry

        lax.fori_loop(0, STEPS // UNROLL, several, 0)

    def enter(i):
        m = i - 1
        co, si = trig[0, 0, :, strided(m), :], trig[0, 1, :, strided(m), :]
        fr, fi = rowf[0, m], rowf[1, m]
        cr, ci = colf[0], colf[1]
        ur = fr[None] * cr - fi[None] * ci
        ui = fr[None] * ci + fi[None] * cr
        w0[0, i] = ur * co - ui * si
        w0[1, i] = ur * si + ui * co

    def first_sweep(base, amount):
        def body(i):
            rim[0, i], rim[1, i] = add_around(base, base, i, amount)

        sweep(body)
        wrap(rim)

    sweep(enter)
    share_ends(1)
    wrap(w0)
    first_sweep(w0, 0.5)
    main1.turn((2,), (-1, 1))
    main1.turn(every, (2,))
    side1.turn(every, (2,))
    turn_ends(1)

    def between(i):
        ur, ui = add_around(w0, rim, i, 0.2)
        m = i - 1
        co, si = trig[1, 0, :, strided(m), :], trig[1, 1, :, strided(m), :]
        w1[0, i] = ur * co - ui * si
        w1[1, i] = ur * si + ui * co

    sweep(between)
    wrap(w1)
    first_sweep(w1, 0.5)

    wire.arrived(energy_group)
    total = energy[1] + energy_in[3] + energy_in[4] + energy_in[5]
    mean = jnp.sum(total, keepdims=True) * (1.0 / (TOTAL_ROWS * TOTAL_COLS)) + EPS_ENERGY
    kappa = jnp.broadcast_to(2.0 / mean, (8, 128))
    wire.arrived(rim_group)

    def compare(i):
        m = i - 1
        ur, ui = add_around(w1, rim, i, 0.2)
        k = scaled(m, kappa)
        for part, u in ((0, ur), (1, ui)):
            side = jnp.where(lane < 64, beside[0, part, strided(m), :], beside[1, part, strided(m), :])
            seen = jnp.concatenate([meas[part, :, strided(m), :], side[None]], axis=0)
            adj[part, i] = k * (u - seen)

    sweep(compare)
    wrap(adj)
    first_sweep(adj, -0.5)

    def back(i):
        m = i - 1
        gr, gi = add_around(adj, rim, i, -0.2)
        grad = gi * w1[0, i] - gr * w1[1, i]
        grads[1, :, strided(m), :] = grad[:NLB]
        co, si = trig[1, 0, :, strided(m), :], trig[1, 1, :, strided(m), :]
        back1[0, i] = gr * co + gi * si
        back1[1, i] = gi * co - gr * si

    sweep(back)
    late, early = (
        [Scatter(wire, place, grads, plane, u, bufs[5 * k : 5 * k + 5]) for k, u in pairs]
        for plane, pairs in ((0, tuple(enumerate(RS_UNITS))), (1, tuple(enumerate(RS_UNITS, 2))))
    )
    for s in early:
        s.start_first()
    for s in early:
        s.early_first()
    wrap(back1)
    first_sweep(back1, -0.5)

    def finish(i):
        gr, gi = add_around(back1, rim, i, -0.2)
        grad = gi * w0[0, i] - gr * w0[1, i]
        grads[0, :, strided(i - 1), :] = grad[:NLB]

    sweep(finish)

    for s in late:
        s.start_first()
    for s in early:
        s.middle_first()
    for s in late:
        s.early_first()
    for s in late:
        s.middle_first()
    for s in early:
        s.start_second()
    for s in late:
        s.start_second()
    for s in early:
        s.middle_second()
    for s in late:
        s.middle_second()
    for plane, parts in ((1, early), (0, late)):
        blocks = [block for s in parts for block in s.end_second()]
        for b, block in enumerate(swapped(blocks)):
            out[plane, :, 128 * b : 128 * (b + 1)] = block
    wire.all_sent()
    assert len(wire.groups) <= N_SEM


def per_device(phase_delay, angles, measured):
    f32 = jnp.float32
    field = pltpu.VMEM((2, STEPS + 2, NLB + 1, 8, 128), f32)
    scratch = [
        pltpu.VMEM((2, EXT, COLS + 128), f32),
        pltpu.VMEM((2, 2, NLB + 1, EXT, 128), f32),
        pltpu.VMEM((2, 8, COLS), f32),
        pltpu.VMEM((2, 2, 8, 128), f32),
        pltpu.VMEM((2, ROWS, COLS), jnp.bfloat16),
        pltpu.VMEM((2, NLB, EXT, 128), f32),
        pltpu.VMEM((2, 2, ROWS, 128), f32),
        pltpu.VMEM((2, 2, EXT, 128), f32),
        field,
        field,
        field,
        field,
        field,
        pltpu.VMEM((2, STEPS, 8, 128), f32),
        pltpu.VMEM((2, NLB + 1, 8, 128), f32),
        pltpu.VMEM((STEPS, 8, 128), f32),
        pltpu.VMEM((2, 8, 128), f32),
        pltpu.VMEM((6, 8, 128), f32),
        pltpu.VMEM((2, NLB, EXT, 128), f32),
        pltpu.VMEM((SPAN, 8, 128), f32),
    ]
    for b0, b1, _ in RS_UNITS * 2:
        n = b1 - b0
        scratch += [
            pltpu.VMEM((2, 4, n // 2, 8, 128), f32),
            pltpu.VMEM((2, 4, n, 8, 128), f32),
            pltpu.VMEM((4, n, 8, 128), f32),
            pltpu.VMEM((2, n // 2, 8, 128), f32),
            pltpu.VMEM((2, n, 8, 128), f32),
        ]
    scratch += [
        pltpu.SemaphoreType.DMA((2,)),
        pltpu.SemaphoreType.DMA((1,)),
        pltpu.SemaphoreType.DMA((N_SEM,)),
    ]
    return pl.pallas_call(
        kernel,
        out_shape=jax.ShapeDtypeStruct(phase_delay.shape, f32),
        in_specs=[
            pl.BlockSpec(memory_space=pl.ANY),
            pl.BlockSpec(memory_space=pltpu.SMEM),
            pl.BlockSpec(memory_space=pl.ANY),
        ],
        out_specs=pl.BlockSpec(memory_space=pltpu.VMEM),
        scratch_shapes=scratch,
        compiler_params=pltpu.CompilerParams(
            collective_id=0, has_side_effects=True, vmem_limit_bytes=56 << 20
        ),
        name="tomography",
    )(phase_delay, angles, measured)


def solution(mesh):
    placed = (P(None, ("row", "illum"), "col"), P("illum", None), P(None, "illum", "row", "col"))
    return jax.shard_map(
        per_device,
        mesh=mesh,
        in_specs=placed,
        out_specs=P(None, ("row", "illum"), "col"),
        check_vma=False,
    )
```

```python
import math

import jax
import jax.numpy as jnp
from jax import lax
from jax.experimental import pallas as pl
from jax.experimental.pallas import tpu as pltpu
from jax.sharding import PartitionSpec as P

ROWS, COLS, NLB = 128, 1024, 8
EXT, STEPS = 144, 18
TOTAL_ROWS, TOTAL_COLS = 512, 4096
EPS_ENERGY = 1e-06
MESH = pl.DeviceIdType.MESH
AG_UNITS = ((0, 6, "zx", True, True), (6, 8, "xz", False, True))
HALO_UNIT = (8, 9, "zx", True, False)
RS_UNITS = ((0, 6, "xz"), (6, 8, "zx"))
N_SEM = 64
UNROLL = 9
SPAN = 720


def sincos(x):
    t = x * x
    s = 0.008333314069458244 + t * (-0.00019835866408867098 + t * 2.6937597583896155e-06)
    s = x * (0.9999999999519255 + t * (-0.1666666642612366 + t * s))
    c = 0.04166645537534636 + t * (-0.0013882960343216638 + t * 2.4121201083497457e-05)
    c = 0.9999999994728761 + t * (-0.4999999736217199 + t * c)
    return s, c


class Place:
    def __init__(self):
        illum = lax.axis_index("illum")
        self.zh, self.x = illum // 4, lax.rem(illum, 4)
        self.y, self.c = lax.axis_index("row"), lax.axis_index("col")

    def block(self, dz, dx):
        return lax.rem(self.zh + dz + 4, 4) * 4 + lax.rem(self.x + dx + 4, 4)

    def rows(self, dz, dx):
        return pl.ds(pl.multiple_of(8 * self.block(dz, dx), 8), 8)

    def illum(self, dz, dx):
        return {"illum": self.block(dz, dx)}

    def tile(self, dy, dc):
        return {"row": lax.rem(self.y + dy + 4, 4), "col": lax.rem(self.c + dc + 4, 4)}


class Wire:
    def __init__(self, send, recv, span):
        self.send, self.recv, self.span = send, recv, span
        self.sent, self.groups = 0, []

    def group(self):
        self.groups.append(0)
        return len(self.groups) - 1

    def start(self, src, dst, device, group):
        tiles = math.prod(src.shape) // 1024
        self.sent += tiles
        self.groups[group] += tiles
        pltpu.make_async_remote_copy(
            src_ref=src,
            dst_ref=dst,
            send_sem=self.send.at[0],
            recv_sem=self.recv.at[group],
            device_id=device,
            device_id_type=MESH,
        ).start()

    def wait_for(self, sem, tiles):
        part = self.span.at[:tiles]
        pltpu.make_async_copy(part, part, sem).wait()

    def arrived(self, group):
        self.wait_for(self.recv.at[group], self.groups[group])

    def all_sent(self):
        self.wait_for(self.send.at[0], self.sent)


class Gather:
    def __init__(self, wire, place, planes, trig, plane, unit):
        self.w, self.p, self.planes, self.trig, self.plane = wire, place, planes, trig, plane
        self.b0, self.b1, self.order, *self.relays = unit
        self.mid = (self.b0 + self.b1) // 2
        self.first = [wire.group() for _ in range(1 + self.relays[0])]
        self.second = {da: wire.group() for da in (0, -1, 1, 2)}
        if self.relays[1]:
            self.last = wire.group()

    def pos(self, da, db):
        return (da, db) if self.order == "zx" else (db, da)

    def send(self, da, db, step, group, half=None):
        rows = self.p.rows(*self.pos(da, db))
        b0, b1 = ((self.b0, self.b1), (self.b0, self.mid), (self.mid, self.b1))[half or 0]
        lead = self.plane
        if lead is None:
            lead, b0, b1 = (half - 1 if half else slice(None)), self.b0, self.b1
        ref = self.planes.at[lead, rows, 128 * b0 : 128 * b1]
        self.w.start(ref, ref, self.p.illum(*self.pos(*step)), group)

    def start(self):
        self.send(0, 0, (1, 0), self.first[0])
        self.send(0, 0, (-1, 0), self.first[0])
        if not self.relays[0]:
            self.send(0, 0, (2, 0), self.first[0])
        self.start_second(0)

    def relay_first(self):
        self.w.arrived(self.first[0])
        if self.relays[0]:
            self.send(-1, 0, (1, 0), self.first[1], 1)
            self.send(1, 0, (-1, 0), self.first[1], 2)
        else:
            self.start_second(2)
        self.start_second(-1)
        self.start_second(1)

    def end_first(self):
        self.w.arrived(self.first[1])
        self.start_second(2)

    def start_second(self, da):
        self.send(da, 0, (0, 1), self.second[da])
        self.send(da, 0, (0, -1), self.second[da])
        if not self.relays[1]:
            self.send(da, 0, (0, 2), self.second[da])

    def relay_second(self, *das):
        for da in das:
            self.w.arrived(self.second[da])
            if self.relays[1]:
                self.send(da, -1, (0, 1), self.last, 1)
                self.send(da, 1, (0, -1), self.last, 2)

    def end(self):
        self.w.arrived(self.last)

    def turn(self, das, dbs):
        for da in das:
            for db in dbs:
                rows = self.p.rows(*self.pos(da, db))
                for plane in (0, 1) if self.plane is None else (self.plane,):
                    turn_rows(self.planes, self.trig, plane, rows, self.b0, self.b1)


def turn_rows(planes, trig, plane, rows, b0, b1):
    s, c = sincos(planes[plane, rows, 128 * b0 : 128 * b1])
    for b in range(b0, b1):
        at = slice(128 * (b - b0), 128 * (b - b0 + 1))
        trig[plane, 0, b, rows, :] = c[:, at]
        trig[plane, 1, b, rows, :] = s[:, at]


class Scatter:
    def __init__(self, wire, place, grads, plane, unit, bufs):
        self.w, self.p, self.g, self.plane = wire, place, grads, plane
        self.b0, self.b1, self.order = unit
        self.n, self.h = self.b1 - self.b0, (self.b1 - self.b0) // 2
        self.t1, self.t2, self.sums, self.t3, self.t4 = bufs
        one, two = (wire.group() for _ in range(2))
        self.r1 = {2: one, 1: one, 3: two, 0: two}
        one, two = (wire.group() for _ in range(2))
        self.r2 = {2: one, 1: one, 3: two, 0: two}
        self.r3, self.r4 = wire.group(), wire.group()

    def pos(self, da, db):
        return (da, db) if self.order == "zx" else (db, da)

    def part(self, da, dq, half=0):
        m = self.b0 + self.h
        lanes = (slice(self.b0, self.b1), slice(self.b0, m), slice(m, self.b1))[half]
        return (self.plane, lanes, self.p.rows(*self.pos(da, dq)), slice(None))

    def send(self, src, dst, da, db, group):
        self.w.start(src, dst, self.p.illum(*self.pos(da, db)), group)

    def start_first(self):
        for dq in (2, 1, 3, 0):
            self.send(self.g.at[self.part(2, dq, 1)], self.t1.at[0, dq], 1, 0, self.r1[dq])
            self.send(self.g.at[self.part(2, dq, 2)], self.t1.at[1, dq], -1, 0, self.r1[dq])

    def early_first(self):
        for dq in (2, 1, 3, 0):
            self.send(self.g.at[self.part(1, dq, 2)], self.t2.at[0, dq, self.h :], 1, 0, self.r2[dq])
            self.send(self.g.at[self.part(-1, dq, 1)], self.t2.at[1, dq, : self.h], -1, 0, self.r2[dq])

    def middle_first(self):
        for dq in (2, 1, 3, 0):
            if dq in (2, 3):
                self.w.arrived(self.r1[dq])
            at = self.part(1, dq, 1)
            self.g[at] = self.g[at] + self.t1[0, dq]
            at = self.part(-1, dq, 2)
            self.g[at] = self.g[at] + self.t1[1, dq]
        for dq in (2, 1, 3, 0):
            self.send(self.g.at[self.part(1, dq, 1)], self.t2.at[0, dq, : self.h], 1, 0, self.r2[dq])
            self.send(self.g.at[self.part(-1, dq, 2)], self.t2.at[1, dq, self.h :], -1, 0, self.r2[dq])

    def add_first(self, dq):
        self.sums[dq] = self.g[self.part(0, dq)] + self.t2[0, dq] + self.t2[1, dq]

    def start_second(self):
        h = self.h
        self.w.arrived(self.r2[2])
        self.add_first(2)
        self.add_first(1)
        self.send(self.sums.at[2, :h], self.t3.at[0], 0, 1, self.r3)
        self.send(self.sums.at[2, h:], self.t3.at[1], 0, -1, self.r3)
        self.w.arrived(self.r2[3])
        self.add_first(3)
        self.send(self.sums.at[1, h:], self.t4.at[0, h:], 0, 1, self.r4)
        self.send(self.sums.at[3, :h], self.t4.at[1, :h], 0, -1, self.r4)
        self.add_first(0)

    def middle_second(self):
        h = self.h
        self.w.arrived(self.r3)
        self.sums[1, :h] = self.sums[1, :h] + self.t3[0]
        self.sums[3, h:] = self.sums[3, h:] + self.t3[1]
        self.send(self.sums.at[1, :h], self.t4.at[0, :h], 0, 1, self.r4)
        self.send(self.sums.at[3, h:], self.t4.at[1, h:], 0, -1, self.r4)

    def end_second(self):
        self.w.arrived(self.r4)
        total = self.sums[0] + self.t4[0] + self.t4[1]
        return [total[b] for b in range(self.n)]


def strided(m):
    return pl.ds(m, 8, stride=STEPS)


def swapped(blocks):
    blocks = list(blocks)
    lane = lanes_of(blocks[0].shape)
    last = lane.ndim - 1
    for k in (1, 2, 4):
        low = jnp.bitwise_and(lane, k) == 0
        for b in range(NLB):
            if not b & k:
                one, two = blocks[b], blocks[b | k]
                blocks[b] = jnp.where(low, one, pltpu.roll(two, k, last))
                blocks[b | k] = jnp.where(low, pltpu.roll(one, 128 - k, last), two)
    return blocks


def split(x):
    return [x[..., 128 * b : 128 * (b + 1)] for b in range(NLB)]


def lanes_of(shape):
    return lax.broadcasted_iota(jnp.int32, shape, len(shape) - 1)


def kernel(
    phase_hbm, angles, meas_hbm, out,
    planes, trig, fresh, edges, raw, meas, rims, beside, w0, w1, rim, adj, back1, rowf, colf, rowm, energy, energy_in,
    grads, span, *rest,
):
    *bufs, local, send, recv = rest
    place = Place()
    wire = Wire(send, recv, span)
    own = place.rows(0, 0)
    fetch = [
        pltpu.make_async_copy(phase_hbm, fresh, local.at[0]),
        pltpu.make_async_copy(meas_hbm.at[:, 0], raw, local.at[1]),
    ]
    partners = [place.illum(1, 0), place.illum(-1, 0), place.illum(0, 1), place.illum(0, -1)]
    partners.append(place.illum(0, 2))
    partners += [place.tile(d, 0) for d in (1, -1)] + [place.tile(0, d) for d in (1, 2, 3)]
    partners += [place.tile(d, e) for d in (1, -1) for e in (1, -1)]
    barrier = pltpu.get_barrier_semaphore()
    for device in partners:
        pl.semaphore_signal(barrier, inc=1, device_id=device, device_id_type=MESH)
    for copy in fetch:
        copy.start()
    pl.semaphore_wait(barrier, len(partners))

    edge_group = wire.group()
    wire.start(phase_hbm.at[:, :, :128], edges.at[0], place.tile(0, -1), edge_group)
    wire.start(phase_hbm.at[:, :, COLS - 128 :], edges.at[1], place.tile(0, 1), edge_group)
    units = [[Gather(wire, place, planes, trig, plane, u) for u in AG_UNITS] for plane in (0, 1)]
    (main0, side0), (main1, side1) = units
    halo = Gather(wire, place, planes, trig, None, HALO_UNIT)
    fetch[0].wait()
    for b, block in enumerate(swapped(split(fresh[...]))):
        planes[:, own, 128 * b : 128 * (b + 1)] = block
    main0.start()
    side0.start()
    main1.start()
    side1.start()
    wire.arrived(edge_group)
    lane = lanes_of((2, 8, 128))
    planes[:, own, COLS:] = jnp.where(lane < 64, pltpu.roll(edges[0], 8, 2), pltpu.roll(edges[1], 120, 2))
    halo.start()

    fetch[1].wait()
    energy[0] = jnp.zeros((8, 128), jnp.float32)

    def widen(g, carry):
        rows = pl.ds(pl.multiple_of(16 * g, 16), 16)
        for part in (0, 1):
            x = raw[part, rows, :].astype(jnp.float32)
            squares = x * x
            blocks = split(x)
            rims[0, part, rows, :] = pltpu.roll(blocks[0], 8, 1)
            rims[1, part, rows, :] = pltpu.roll(blocks[NLB - 1], 120, 1)
            for b, block in enumerate(swapped(blocks)):
                meas[part, b, rows, :] = block
            half = squares[:8] + squares[8:]
            total = half[:, :128]
            for b in range(1, NLB):
                total = total + half[:, 128 * b : 128 * (b + 1)]
            energy[0] = energy[0] + total
        return carry

    lax.fori_loop(0, ROWS // 16, widen, 0)
    energy_group = wire.group()
    wire.start(energy.at[0], energy_in.at[0], place.tile(1, 0), energy_group)
    wire.start(energy.at[0], energy_in.at[1], place.tile(-1, 0), energy_group)
    rim_group = wire.group()
    tile_rows, last, first = slice(0, 128), slice(120, 128), slice(0, 8)
    after, before = slice(128, 136), slice(136, 144)
    wire.start(meas.at[:, :, last, :], meas.at[:, :, before, :], place.tile(1, 0), rim_group)
    wire.start(meas.at[:, :, first, :], meas.at[:, :, after, :], place.tile(-1, 0), rim_group)

    step_a, step_b = angles[0, 0], angles[0, 1]
    lane = lanes_of((8, 128))

    def circle(steps, period):
        turns = jnp.bitwise_and(steps + period // 2, period - 1) - period // 2
        s, c = sincos(turns.astype(jnp.float32) * (0.5 * math.pi / period))
        s, c = 2.0 * s * c, 1.0 - 2.0 * s * s
        return 2.0 * s * c, 1.0 - 2.0 * s * s

    def col_of(b):
        edge = jnp.where(lane < 64, COLS - 8 + lane, lane - 120)
        inner = 128 * jnp.bitwise_and(lane, 7) + jnp.bitwise_and(lane, -8) + b
        return place.c * COLS + (inner if b < NLB else edge)

    def factors():
        shape = (STEPS, 8, 128)
        r = lax.broadcasted_iota(jnp.int32, shape, 1) * STEPS + lax.broadcasted_iota(jnp.int32, shape, 0)
        gr = place.y * ROWS + jnp.where(r < 136, r, r - EXT)
        inside = jnp.where((gr >= 0) & (gr < TOTAL_ROWS), 1.0, 0.0)
        si, co = circle(step_a * gr, TOTAL_ROWS)
        rowf[0] = inside * (-0.28 * co - 0.96 * si)
        rowf[1] = inside * (0.96 * co - 0.28 * si)
        rowm[...] = inside
        gc = jnp.stack([col_of(b) for b in range(NLB + 1)])
        inside = jnp.where((gc >= 0) & (gc < TOTAL_COLS), 1.0, 0.0)
        si, co = circle(step_b * gc, TOTAL_COLS)
        colf[0] = inside * co
        colf[1] = inside * si

    every, near = (0, -1, 1, 2), (0, -1, 1)
    every, near = (0, -1, 1, 2), (0, -1, 1)
    main0.relay_second(0)
    main0.turn((0,), near)
    main0.relay_first()
    side0.relay_first()
    main1.relay_second(0)
    wire.arrived(energy_group)
    far_group = wire.group()
    wire.start(energy_in.at[0], energy_in.at[2], place.tile(1, 0), far_group)
    halo.turn((0,), (0,))
    main1.relay_first()
    side1.relay_first()
    main0.turn((-1, 1), (0,))
    halo.relay_first()
    factors()
    side0.turn(every, (0,))
    side0.relay_second(0)
    main0.end_first()
    main0.relay_second(-1, 1)
    side1.relay_second(0)
    halo.end_first()
    main1.end_first()
    side0.relay_second(-1, 1)
    main1.relay_second(-1, 1)
    wire.arrived(far_group)
    energy[1] = energy[0] + energy_in[0] + energy_in[1] + energy_in[2]
    energy_group = wire.group()
    for d in (1, 2, 3):
        wire.start(energy.at[1], energy_in.at[2 + d], place.tile(0, d), energy_group)
    side0.relay_second(2)
    side1.relay_second(-1, 1)
    main0.turn((-1, 1), (-1, 1))
    main0.turn((2,), (0,))
    main0.relay_second(2)
    side1.relay_second(2)
    main1.relay_second(2)
    side0.turn(every, (-1, 1))
    halo.relay_second(*every)

    end_groups = [wire.group(), wire.group()]

    def share_ends(plane):
        ref = planes.at[plane]
        for unit in units[plane]:
            unit.end()
        wire.start(ref.at[last, :], ref.at[before, :], place.tile(1, 0), end_groups[plane])
        wire.start(ref.at[first, :], ref.at[after, :], place.tile(-1, 0), end_groups[plane])

    def turn_ends(plane):
        wire.arrived(end_groups[plane])
        turn_rows(planes, trig, plane, slice(128, 144), 0, NLB + 1)

    share_ends(0)
    for side, dc in ((0, -1), (1, 1)):
        src, dst = rims.at[side], beside.at[side]
        wire.start(src.at[:, tile_rows, :], dst.at[:, tile_rows, :], place.tile(0, dc), rim_group)
        wire.start(src.at[:, last, :], dst.at[:, before, :], place.tile(1, dc), rim_group)
        wire.start(src.at[:, first, :], dst.at[:, after, :], place.tile(-1, dc), rim_group)
    main0.turn((2,), (-1, 1))
    main0.turn(every, (2,))
    side0.turn(every, (2,))
    halo.turn((0,), (-1, 1, 2))
    halo.turn((-1, 1, 2), every)
    main1.turn(near, near)
    main1.turn((2,), (0,))
    side1.turn(every, near)
    turn_ends(0)

    gc8 = col_of(NLB)
    col_in = jnp.where((gc8 >= 0) & (gc8 < TOTAL_COLS), 1.0, 0.0)

    def scaled(m, amount):
        k = rowm[m] * amount
        return jnp.concatenate([jnp.broadcast_to(k[None], (NLB, 8, 128)), (k * col_in)[None]], axis=0)

    def around(field, part, i):
        mid = field[part, i]
        first, last, edge = mid[0], mid[NLB - 1], mid[NLB]
        ahead = pltpu.roll(jnp.where(lane == 8, edge, first), 119, 1)
        behind = pltpu.roll(jnp.where(lane == 119, edge, last), 9, 1)
        right_last = jnp.where(lane < 120, pltpu.roll(first, 120, 1), ahead)
        left_first = jnp.where(lane < 8, behind, pltpu.roll(last, 8, 1))
        right_edge = jnp.where(lane == 119, ahead, pltpu.roll(edge, 127, 1))
        left_edge = jnp.where(lane == 8, behind, pltpu.roll(edge, 1, 1))
        right = jnp.concatenate([mid[1:NLB], right_last[None], right_edge[None]], axis=0)
        left = jnp.concatenate([left_first[None], mid[: NLB - 1], left_edge[None]], axis=0)
        return (field[part, i - 1] + field[part, i + 1]) + (right + left)

    def wrap(field):
        for part in (0, 1):
            field[part, 0] = pltpu.roll(field[part, STEPS], 1, 1)
            field[part, STEPS + 1] = pltpu.roll(field[part, 1], 7, 1)

    def add_around(base, field, i, amount):
        k = scaled(i - 1, amount)
        real = base[0, i] - k * around(field, 1, i)
        imag = base[1, i] + k * around(field, 0, i)
        return real, imag

    def sweep(body):
        def several(t, carry):
            for k in range(UNROLL):
                body(UNROLL * t + k + 1)
            return carry

        lax.fori_loop(0, STEPS // UNROLL, several, 0)

    def enter(i):
        m = i - 1
        co, si = trig[0, 0, :, strided(m), :], trig[0, 1, :, strided(m), :]
        fr, fi = rowf[0, m], rowf[1, m]
        cr, ci = colf[0], colf[1]
        ur = fr[None] * cr - fi[None] * ci
        ui = fr[None] * ci + fi[None] * cr
        w0[0, i] = ur * co - ui * si
        w0[1, i] = ur * si + ui * co

    def first_sweep(base, amount):
        def body(i):
            rim[0, i], rim[1, i] = add_around(base, base, i, amount)

        sweep(body)
        wrap(rim)

    sweep(enter)
    share_ends(1)
    wrap(w0)
    first_sweep(w0, 0.5)
    main1.turn((2,), (-1, 1))
    main1.turn(every, (2,))
    side1.turn(every, (2,))
    turn_ends(1)

    def between(i):
        ur, ui = add_around(w0, rim, i, 0.2)
        m = i - 1
        co, si = trig[1, 0, :, strided(m), :], trig[1, 1, :, strided(m), :]
        w1[0, i] = ur * co - ui * si
        w1[1, i] = ur * si + ui * co

    sweep(between)
    wrap(w1)
    first_sweep(w1, 0.5)

    wire.arrived(energy_group)
    total = energy[1] + energy_in[3] + energy_in[4] + energy_in[5]
    mean = jnp.sum(total, keepdims=True) * (1.0 / (TOTAL_ROWS * TOTAL_COLS)) + EPS_ENERGY
    kappa = jnp.broadcast_to(2.0 / mean, (8, 128))
    wire.arrived(rim_group)

    def compare(i):
        m = i - 1
        ur, ui = add_around(w1, rim, i, 0.2)
        k = scaled(m, kappa)
        for part, u in ((0, ur), (1, ui)):
            side = jnp.where(lane < 64, beside[0, part, strided(m), :], beside[1, part, strided(m), :])
            seen = jnp.concatenate([meas[part, :, strided(m), :], side[None]], axis=0)
            adj[part, i] = k * (u - seen)

    sweep(compare)
    wrap(adj)
    first_sweep(adj, -0.5)

    def back(i):
        m = i - 1
        gr, gi = add_around(adj, rim, i, -0.2)
        grad = gi * w1[0, i] - gr * w1[1, i]
        grads[1, :, strided(m), :] = grad[:NLB]
        co, si = trig[1, 0, :, strided(m), :], trig[1, 1, :, strided(m), :]
        back1[0, i] = gr * co + gi * si
        back1[1, i] = gi * co - gr * si

    sweep(back)
    late, early = (
        [Scatter(wire, place, grads, plane, u, bufs[5 * k : 5 * k + 5]) for k, u in pairs]
        for plane, pairs in ((0, tuple(enumerate(RS_UNITS))), (1, tuple(enumerate(RS_UNITS, 2))))
    )
    for s in early:
        s.start_first()
    for s in early:
        s.early_first()
    wrap(back1)
    first_sweep(back1, -0.5)

    def finish(i):
        gr, gi = add_around(back1, rim, i, -0.2)
        grad = gi * w0[0, i] - gr * w0[1, i]
        grads[0, :, strided(i - 1), :] = grad[:NLB]

    sweep(finish)

    for s in late:
        s.start_first()
    for s in early:
        s.middle_first()
    for s in late:
        s.early_first()
    for s in late:
        s.middle_first()
    for s in early:
        s.start_second()
    for s in late:
        s.start_second()
    for s in early:
        s.middle_second()
    for s in late:
        s.middle_second()
    for plane, parts in ((1, early), (0, late)):
        blocks = [block for s in parts for block in s.end_second()]
        for b, block in enumerate(swapped(blocks)):
            out[plane, :, 128 * b : 128 * (b + 1)] = block
    wire.all_sent()
    assert len(wire.groups) <= N_SEM


def per_device(phase_delay, angles, measured):
    f32 = jnp.float32
    field = pltpu.VMEM((2, STEPS + 2, NLB + 1, 8, 128), f32)
    scratch = [
        pltpu.VMEM((2, EXT, COLS + 128), f32),
        pltpu.VMEM((2, 2, NLB + 1, EXT, 128), f32),
        pltpu.VMEM((2, 8, COLS), f32),
        pltpu.VMEM((2, 2, 8, 128), f32),
        pltpu.VMEM((2, ROWS, COLS), jnp.bfloat16),
        pltpu.VMEM((2, NLB, EXT, 128), f32),
        pltpu.VMEM((2, 2, ROWS, 128), f32),
        pltpu.VMEM((2, 2, EXT, 128), f32),
        field,
        field,
        field,
        field,
        field,
        pltpu.VMEM((2, STEPS, 8, 128), f32),
        pltpu.VMEM((2, NLB + 1, 8, 128), f32),
        pltpu.VMEM((STEPS, 8, 128), f32),
        pltpu.VMEM((2, 8, 128), f32),
        pltpu.VMEM((6, 8, 128), f32),
        pltpu.VMEM((2, NLB, EXT, 128), f32),
        pltpu.VMEM((SPAN, 8, 128), f32),
    ]
    for b0, b1, _ in RS_UNITS * 2:
        n = b1 - b0
        scratch += [
            pltpu.VMEM((2, 4, n // 2, 8, 128), f32),
            pltpu.VMEM((2, 4, n, 8, 128), f32),
            pltpu.VMEM((4, n, 8, 128), f32),
            pltpu.VMEM((2, n // 2, 8, 128), f32),
            pltpu.VMEM((2, n, 8, 128), f32),
        ]
    scratch += [
        pltpu.SemaphoreType.DMA((2,)),
        pltpu.SemaphoreType.DMA((1,)),
        pltpu.SemaphoreType.DMA((N_SEM,)),
    ]
    return pl.pallas_call(
        kernel,
        out_shape=jax.ShapeDtypeStruct(phase_delay.shape, f32),
        in_specs=[
            pl.BlockSpec(memory_space=pl.ANY),
            pl.BlockSpec(memory_space=pltpu.SMEM),
            pl.BlockSpec(memory_space=pl.ANY),
        ],
        out_specs=pl.BlockSpec(memory_space=pltpu.VMEM),
        scratch_shapes=scratch,
        compiler_params=pltpu.CompilerParams(
            collective_id=0, has_side_effects=True, vmem_limit_bytes=56 << 20
        ),
        name="tomography",
    )(phase_delay, angles, measured)


def solution(mesh):
    placed = (P(None, ("row", "illum"), "col"), P("illum", None), P(None, "illum", "row", "col"))
    return jax.shard_map(
        per_device,
        mesh=mesh,
        in_specs=placed,
        out_specs=P(None, ("row", "illum"), "col"),
        check_vma=False,
    )
```

```python
import math

import jax
import jax.numpy as jnp
from jax import lax
from jax.experimental import pallas as pl
from jax.experimental.pallas import tpu as pltpu
from jax.sharding import PartitionSpec as P

ROWS, COLS, NLB = 128, 1024, 8
EXT, STEPS = 144, 18
TOTAL_ROWS, TOTAL_COLS = 512, 4096
EPS_ENERGY = 1e-06
MESH = pl.DeviceIdType.MESH
AG_UNITS = ((0, 6, "zx", True, True), (6, 8, "xz", False, True))
HALO_UNIT = (8, 9, "zx", True, False)
RS_UNITS = ((0, 5, "xz"), (5, 8, "zx"))
N_SEM = 64
UNROLL = 18
SPAN = 720


def sincos(x):
    t = x * x
    s = 0.008333314069458244 + t * (-0.00019835866408867098 + t * 2.6937597583896155e-06)
    s = x * (0.9999999999519255 + t * (-0.1666666642612366 + t * s))
    c = 0.04166645537534636 + t * (-0.0013882960343216638 + t * 2.4121201083497457e-05)
    c = 0.9999999994728761 + t * (-0.4999999736217199 + t * c)
    return s, c


class Place:
    def __init__(self):
        illum = lax.axis_index("illum")
        self.zh, self.x = illum // 4, lax.rem(illum, 4)
        self.y, self.c = lax.axis_index("row"), lax.axis_index("col")

    def block(self, dz, dx):
        return lax.rem(self.zh + dz + 4, 4) * 4 + lax.rem(self.x + dx + 4, 4)

    def rows(self, dz, dx):
        return pl.ds(pl.multiple_of(8 * self.block(dz, dx), 8), 8)

    def illum(self, dz, dx):
        return {"illum": self.block(dz, dx)}

    def tile(self, dy, dc):
        return {"row": lax.rem(self.y + dy + 4, 4), "col": lax.rem(self.c + dc + 4, 4)}


class Wire:
    def __init__(self, send, recv, span):
        self.send, self.recv, self.span = send, recv, span
        self.sent, self.groups = 0, []

    def group(self):
        self.groups.append(0)
        return len(self.groups) - 1

    def start(self, src, dst, device, group):
        tiles = math.prod(src.shape) // 1024
        self.sent += tiles
        self.groups[group] += tiles
        pltpu.make_async_remote_copy(
            src_ref=src,
            dst_ref=dst,
            send_sem=self.send.at[0],
            recv_sem=self.recv.at[group],
            device_id=device,
            device_id_type=MESH,
        ).start()

    def wait_for(self, sem, tiles):
        part = self.span.at[:tiles]
        pltpu.make_async_copy(part, part, sem).wait()

    def arrived(self, group):
        self.wait_for(self.recv.at[group], self.groups[group])

    def all_sent(self):
        self.wait_for(self.send.at[0], self.sent)


class Gather:
    def __init__(self, wire, place, planes, trig, plane, unit):
        self.w, self.p, self.planes, self.trig, self.plane = wire, place, planes, trig, plane
        self.b0, self.b1, self.order, *self.relays = unit
        self.mid = (self.b0 + self.b1) // 2
        self.first = [wire.group() for _ in range(1 + self.relays[0])]
        self.second = {da: wire.group() for da in (0, -1, 1, 2)}
        if self.relays[1]:
            self.last = wire.group()

    def pos(self, da, db):
        return (da, db) if self.order == "zx" else (db, da)

    def send(self, da, db, step, group, half=None):
        rows = self.p.rows(*self.pos(da, db))
        b0, b1 = ((self.b0, self.b1), (self.b0, self.mid), (self.mid, self.b1))[half or 0]
        lead = self.plane
        if lead is None:
            lead, b0, b1 = (half - 1 if half else slice(None)), self.b0, self.b1
        ref = self.planes.at[lead, rows, 128 * b0 : 128 * b1]
        self.w.start(ref, ref, self.p.illum(*self.pos(*step)), group)

    def start(self):
        self.send(0, 0, (1, 0), self.first[0])
        self.send(0, 0, (-1, 0), self.first[0])
        if not self.relays[0]:
            self.send(0, 0, (2, 0), self.first[0])
        self.start_second(0)

    def relay_first(self):
        self.w.arrived(self.first[0])
        if self.relays[0]:
            self.send(-1, 0, (1, 0), self.first[1], 1)
            self.send(1, 0, (-1, 0), self.first[1], 2)
        else:
            self.start_second(2)
        self.start_second(-1)
        self.start_second(1)

    def end_first(self):
        self.w.arrived(self.first[1])
        self.start_second(2)

    def start_second(self, da):
        self.send(da, 0, (0, 1), self.second[da])
        self.send(da, 0, (0, -1), self.second[da])
        if not self.relays[1]:
            self.send(da, 0, (0, 2), self.second[da])

    def relay_second(self, *das):
        for da in das:
            self.w.arrived(self.second[da])
            if self.relays[1]:
                self.send(da, -1, (0, 1), self.last, 1)
                self.send(da, 1, (0, -1), self.last, 2)

    def end(self):
        self.w.arrived(self.last)

    def turn(self, das, dbs):
        for da in das:
            for db in dbs:
                rows = self.p.rows(*self.pos(da, db))
                for plane in (0, 1) if self.plane is None else (self.plane,):
                    turn_rows(self.planes, self.trig, plane, rows, self.b0, self.b1)


def turn_rows(planes, trig, plane, rows, b0, b1):
    s, c = sincos(planes[plane, rows, 128 * b0 : 128 * b1])
    for b in range(b0, b1):
        at = slice(128 * (b - b0), 128 * (b - b0 + 1))
        trig[plane, 0, b, rows, :] = c[:, at]
        trig[plane, 1, b, rows, :] = s[:, at]


class Scatter:
    def __init__(self, wire, place, grads, plane, unit, bufs):
        self.w, self.p, self.g, self.plane = wire, place, grads, plane
        self.b0, self.b1, self.order = unit
        self.n, self.h = self.b1 - self.b0, (self.b1 - self.b0) // 2
        self.t1, self.t2, self.sums, self.t3, self.t4 = bufs
        one, two = (wire.group() for _ in range(2))
        self.r1 = {2: one, 1: one, 3: two, 0: two}
        one, two = (wire.group() for _ in range(2))
        self.r2 = {2: one, 1: one, 3: two, 0: two}
        self.r3, self.r4 = wire.group(), wire.group()

    def pos(self, da, db):
        return (da, db) if self.order == "zx" else (db, da)

    def part(self, da, dq, half=0):
        m = self.b0 + self.h
        lanes = (slice(self.b0, self.b1), slice(self.b0, m), slice(m, self.b1))[half]
        return (self.plane, lanes, self.p.rows(*self.pos(da, dq)), slice(None))

    def send(self, src, dst, da, db, group):
        self.w.start(src, dst, self.p.illum(*self.pos(da, db)), group)

    def start_first(self):
        for dq in (2, 1, 3, 0):
            self.send(self.g.at[self.part(2, dq, 1)], self.t1.at[0, dq, : self.h], 1, 0, self.r1[dq])
            self.send(self.g.at[self.part(2, dq, 2)], self.t1.at[1, dq, : self.n - self.h], -1, 0, self.r1[dq])

    def early_first(self):
        for dq in (2, 1, 3, 0):
            self.send(self.g.at[self.part(1, dq, 2)], self.t2.at[0, dq, self.h :], 1, 0, self.r2[dq])
            self.send(self.g.at[self.part(-1, dq, 1)], self.t2.at[1, dq, : self.h], -1, 0, self.r2[dq])

    def middle_first(self):
        for dq in (2, 1, 3, 0):
            if dq in (2, 3):
                self.w.arrived(self.r1[dq])
            at = self.part(1, dq, 1)
            self.g[at] = self.g[at] + self.t1[0, dq, : self.h]
            at = self.part(-1, dq, 2)
            self.g[at] = self.g[at] + self.t1[1, dq, : self.n - self.h]
        for dq in (2, 1, 3, 0):
            self.send(self.g.at[self.part(1, dq, 1)], self.t2.at[0, dq, : self.h], 1, 0, self.r2[dq])
            self.send(self.g.at[self.part(-1, dq, 2)], self.t2.at[1, dq, self.h :], -1, 0, self.r2[dq])

    def add_first(self, dq):
        self.sums[dq] = self.g[self.part(0, dq)] + self.t2[0, dq] + self.t2[1, dq]

    def start_second(self):
        h = self.h
        self.w.arrived(self.r2[2])
        self.add_first(2)
        self.add_first(1)
        self.send(self.sums.at[2, :h], self.t3.at[0, :h], 0, 1, self.r3)
        self.send(self.sums.at[2, h:], self.t3.at[1, : self.n - h], 0, -1, self.r3)
        self.w.arrived(self.r2[3])
        self.add_first(3)
        self.send(self.sums.at[1, h:], self.t4.at[0, h:], 0, 1, self.r4)
        self.send(self.sums.at[3, :h], self.t4.at[1, :h], 0, -1, self.r4)
        self.add_first(0)

    def middle_second(self):
        h = self.h
        self.w.arrived(self.r3)
        self.sums[1, :h] = self.sums[1, :h] + self.t3[0, :h]
        self.sums[3, h:] = self.sums[3, h:] + self.t3[1, : self.n - h]
        self.send(self.sums.at[1, :h], self.t4.at[0, :h], 0, 1, self.r4)
        self.send(self.sums.at[3, h:], self.t4.at[1, h:], 0, -1, self.r4)

    def end_second(self):
        self.w.arrived(self.r4)
        total = self.sums[0] + self.t4[0] + self.t4[1]
        return [total[b] for b in range(self.n)]


def strided(m):
    return pl.ds(m, 8, stride=STEPS)


def swapped(blocks):
    blocks = list(blocks)
    lane = lanes_of(blocks[0].shape)
    last = lane.ndim - 1
    for k in (1, 2, 4):
        low = jnp.bitwise_and(lane, k) == 0
        for b in range(NLB):
            if not b & k:
                one, two = blocks[b], blocks[b | k]
                blocks[b] = jnp.where(low, one, pltpu.roll(two, k, last))
                blocks[b | k] = jnp.where(low, pltpu.roll(one, 128 - k, last), two)
    return blocks


def split(x):
    return [x[..., 128 * b : 128 * (b + 1)] for b in range(NLB)]


def lanes_of(shape):
    return lax.broadcasted_iota(jnp.int32, shape, len(shape) - 1)


def kernel(
    phase_hbm, angles, meas_hbm, out,
    planes, trig, fresh, edges, raw, meas, rims, beside, w0, w1, rim, adj, back1, rowf, colf, rowm, energy, energy_in,
    grads, span, *rest,
):
    *bufs, local, send, recv = rest
    place = Place()
    wire = Wire(send, recv, span)
    own = place.rows(0, 0)
    fetch = [
        pltpu.make_async_copy(phase_hbm, fresh, local.at[0]),
        pltpu.make_async_copy(meas_hbm.at[:, 0], raw, local.at[1]),
    ]
    partners = [place.illum(1, 0), place.illum(-1, 0), place.illum(0, 1), place.illum(0, -1)]
    partners.append(place.illum(0, 2))
    partners += [place.tile(d, 0) for d in (1, -1)] + [place.tile(0, d) for d in (1, 2, 3)]
    partners += [place.tile(d, e) for d in (1, -1) for e in (1, -1)]
    barrier = pltpu.get_barrier_semaphore()
    for device in partners:
        pl.semaphore_signal(barrier, inc=1, device_id=device, device_id_type=MESH)
    for copy in fetch:
        copy.start()
    pl.semaphore_wait(barrier, len(partners))

    edge_group = wire.group()
    wire.start(phase_hbm.at[:, :, :128], edges.at[0], place.tile(0, -1), edge_group)
    wire.start(phase_hbm.at[:, :, COLS - 128 :], edges.at[1], place.tile(0, 1), edge_group)
    units = [[Gather(wire, place, planes, trig, plane, u) for u in AG_UNITS] for plane in (0, 1)]
    (main0, side0), (main1, side1) = units
    halo = Gather(wire, place, planes, trig, None, HALO_UNIT)
    fetch[0].wait()
    for b, block in enumerate(swapped(split(fresh[...]))):
        planes[:, own, 128 * b : 128 * (b + 1)] = block
    main0.start()
    side0.start()
    main1.start()
    side1.start()
    wire.arrived(edge_group)
    lane = lanes_of((2, 8, 128))
    planes[:, own, COLS:] = jnp.where(lane < 64, pltpu.roll(edges[0], 8, 2), pltpu.roll(edges[1], 120, 2))
    halo.start()

    fetch[1].wait()
    energy[0] = jnp.zeros((8, 128), jnp.float32)

    def widen(g, carry):
        rows = pl.ds(pl.multiple_of(16 * g, 16), 16)
        for part in (0, 1):
            x = raw[part, rows, :].astype(jnp.float32)
            squares = x * x
            blocks = split(x)
            rims[0, part, rows, :] = pltpu.roll(blocks[0], 8, 1)
            rims[1, part, rows, :] = pltpu.roll(blocks[NLB - 1], 120, 1)
            for b, block in enumerate(swapped(blocks)):
                meas[part, b, rows, :] = block
            half = squares[:8] + squares[8:]
            total = half[:, :128]
            for b in range(1, NLB):
                total = total + half[:, 128 * b : 128 * (b + 1)]
            energy[0] = energy[0] + total
        return carry

    lax.fori_loop(0, ROWS // 16, widen, 0)
    energy_group = wire.group()
    wire.start(energy.at[0], energy_in.at[0], place.tile(1, 0), energy_group)
    wire.start(energy.at[0], energy_in.at[1], place.tile(-1, 0), energy_group)
    rim_group = wire.group()
    tile_rows, last, first = slice(0, 128), slice(120, 128), slice(0, 8)
    after, before = slice(128, 136), slice(136, 144)
    wire.start(meas.at[:, :, last, :], meas.at[:, :, before, :], place.tile(1, 0), rim_group)
    wire.start(meas.at[:, :, first, :], meas.at[:, :, after, :], place.tile(-1, 0), rim_group)

    step_a, step_b = angles[0, 0], angles[0, 1]
    lane = lanes_of((8, 128))

    def circle(steps, period):
        turns = jnp.bitwise_and(steps + period // 2, period - 1) - period // 2
        s, c = sincos(turns.astype(jnp.float32) * (0.5 * math.pi / period))
        s, c = 2.0 * s * c, 1.0 - 2.0 * s * s
        return 2.0 * s * c, 1.0 - 2.0 * s * s

    def col_of(b):
        edge = jnp.where(lane < 64, COLS - 8 + lane, lane - 120)
        inner = 128 * jnp.bitwise_and(lane, 7) + jnp.bitwise_and(lane, -8) + b
        return place.c * COLS + (inner if b < NLB else edge)

    def factors():
        shape = (STEPS, 8, 128)
        r = lax.broadcasted_iota(jnp.int32, shape, 1) * STEPS + lax.broadcasted_iota(jnp.int32, shape, 0)
        gr = place.y * ROWS + jnp.where(r < 136, r, r - EXT)
        inside = jnp.where((gr >= 0) & (gr < TOTAL_ROWS), 1.0, 0.0)
        si, co = circle(step_a * gr, TOTAL_ROWS)
        rowf[0] = inside * (-0.28 * co - 0.96 * si)
        rowf[1] = inside * (0.96 * co - 0.28 * si)
        rowm[...] = inside
        gc = jnp.stack([col_of(b) for b in range(NLB + 1)])
        inside = jnp.where((gc >= 0) & (gc < TOTAL_COLS), 1.0, 0.0)
        si, co = circle(step_b * gc, TOTAL_COLS)
        colf[0] = inside * co
        colf[1] = inside * si

    every, near = (0, -1, 1, 2), (0, -1, 1)
    every, near = (0, -1, 1, 2), (0, -1, 1)
    main0.relay_second(0)
    main0.turn((0,), near)
    main0.relay_first()
    side0.relay_first()
    main1.relay_second(0)
    wire.arrived(energy_group)
    far_group = wire.group()
    wire.start(energy_in.at[0], energy_in.at[2], place.tile(1, 0), far_group)
    halo.turn((0,), (0,))
    main1.relay_first()
    side1.relay_first()
    main0.turn((-1, 1), (0,))
    halo.relay_first()
    factors()
    side0.turn(every, (0,))
    side0.relay_second(0)
    main0.end_first()
    main0.relay_second(-1, 1)
    side1.relay_second(0)
    halo.end_first()
    main1.end_first()
    side0.relay_second(-1, 1)
    main1.relay_second(-1, 1)
    wire.arrived(far_group)
    energy[1] = energy[0] + energy_in[0] + energy_in[1] + energy_in[2]
    energy_group = wire.group()
    for d in (1, 2, 3):
        wire.start(energy.at[1], energy_in.at[2 + d], place.tile(0, d), energy_group)
    side0.relay_second(2)
    side1.relay_second(-1, 1)
    main0.turn((-1, 1), (-1, 1))
    main0.turn((2,), (0,))
    main0.relay_second(2)
    side1.relay_second(2)
    main1.relay_second(2)
    side0.turn(every, (-1, 1))
    halo.relay_second(*every)

    end_groups = [wire.group(), wire.group()]

    def share_ends(plane):
        ref = planes.at[plane]
        for unit in units[plane]:
            unit.end()
        wire.start(ref.at[last, :], ref.at[before, :], place.tile(1, 0), end_groups[plane])
        wire.start(ref.at[first, :], ref.at[after, :], place.tile(-1, 0), end_groups[plane])

    def turn_ends(plane):
        wire.arrived(end_groups[plane])
        turn_rows(planes, trig, plane, slice(128, 144), 0, NLB + 1)

    share_ends(0)
    for side, dc in ((0, -1), (1, 1)):
        src, dst = rims.at[side], beside.at[side]
        wire.start(src.at[:, tile_rows, :], dst.at[:, tile_rows, :], place.tile(0, dc), rim_group)
        wire.start(src.at[:, last, :], dst.at[:, before, :], place.tile(1, dc), rim_group)
        wire.start(src.at[:, first, :], dst.at[:, after, :], place.tile(-1, dc), rim_group)
    main0.turn((2,), (-1, 1))
    main0.turn(every, (2,))
    side0.turn(every, (2,))
    halo.turn((0,), (-1, 1, 2))
    halo.turn((-1, 1, 2), every)
    main1.turn(near, near)
    main1.turn((2,), (0,))
    side1.turn(every, near)
    turn_ends(0)

    gc8 = col_of(NLB)
    col_in = jnp.where((gc8 >= 0) & (gc8 < TOTAL_COLS), 1.0, 0.0)

    def scaled(m, amount):
        k = rowm[m] * amount
        return jnp.concatenate([jnp.broadcast_to(k[None], (NLB, 8, 128)), (k * col_in)[None]], axis=0)

    def around(field, part, i):
        mid = field[part, i]
        first, last, edge = mid[0], mid[NLB - 1], mid[NLB]
        ahead = pltpu.roll(jnp.where(lane == 8, edge, first), 119, 1)
        behind = pltpu.roll(jnp.where(lane == 119, edge, last), 9, 1)
        right_last = jnp.where(lane < 120, pltpu.roll(first, 120, 1), ahead)
        left_first = jnp.where(lane < 8, behind, pltpu.roll(last, 8, 1))
        right_edge = jnp.where(lane == 119, ahead, pltpu.roll(edge, 127, 1))
        left_edge = jnp.where(lane == 8, behind, pltpu.roll(edge, 1, 1))
        right = jnp.concatenate([mid[1:NLB], right_last[None], right_edge[None]], axis=0)
        left = jnp.concatenate([left_first[None], mid[: NLB - 1], left_edge[None]], axis=0)
        return (field[part, i - 1] + field[part, i + 1]) + (right + left)

    def wrap(field):
        for part in (0, 1):
            field[part, 0] = pltpu.roll(field[part, STEPS], 1, 1)
            field[part, STEPS + 1] = pltpu.roll(field[part, 1], 7, 1)

    def add_around(base, field, i, amount):
        k = scaled(i - 1, amount)
        real = base[0, i] - k * around(field, 1, i)
        imag = base[1, i] + k * around(field, 0, i)
        return real, imag

    def sweep(body):
        def several(t, carry):
            for k in range(UNROLL):
                body(UNROLL * t + k + 1)
            return carry

        lax.fori_loop(0, STEPS // UNROLL, several, 0)

    def enter(i):
        m = i - 1
        co, si = trig[0, 0, :, strided(m), :], trig[0, 1, :, strided(m), :]
        fr, fi = rowf[0, m], rowf[1, m]
        cr, ci = colf[0], colf[1]
        ur = fr[None] * cr - fi[None] * ci
        ui = fr[None] * ci + fi[None] * cr
        w0[0, i] = ur * co - ui * si
        w0[1, i] = ur * si + ui * co

    def first_sweep(base, amount):
        def body(i):
            rim[0, i], rim[1, i] = add_around(base, base, i, amount)

        sweep(body)
        wrap(rim)

    sweep(enter)
    share_ends(1)
    wrap(w0)
    first_sweep(w0, 0.5)
    main1.turn((2,), (-1, 1))
    main1.turn(every, (2,))
    side1.turn(every, (2,))
    turn_ends(1)

    def between(i):
        ur, ui = add_around(w0, rim, i, 0.2)
        m = i - 1
        co, si = trig[1, 0, :, strided(m), :], trig[1, 1, :, strided(m), :]
        w1[0, i] = ur * co - ui * si
        w1[1, i] = ur * si + ui * co

    sweep(between)
    wrap(w1)
    first_sweep(w1, 0.5)

    wire.arrived(energy_group)
    total = energy[1] + energy_in[3] + energy_in[4] + energy_in[5]
    mean = jnp.sum(total, keepdims=True) * (1.0 / (TOTAL_ROWS * TOTAL_COLS)) + EPS_ENERGY
    kappa = jnp.broadcast_to(2.0 / mean, (8, 128))
    wire.arrived(rim_group)

    def compare(i):
        m = i - 1
        ur, ui = add_around(w1, rim, i, 0.2)
        k = scaled(m, kappa)
        for part, u in ((0, ur), (1, ui)):
            side = jnp.where(lane < 64, beside[0, part, strided(m), :], beside[1, part, strided(m), :])
            seen = jnp.concatenate([meas[part, :, strided(m), :], side[None]], axis=0)
            adj[part, i] = k * (u - seen)

    sweep(compare)
    wrap(adj)
    first_sweep(adj, -0.5)

    def back(i):
        m = i - 1
        gr, gi = add_around(adj, rim, i, -0.2)
        grad = gi * w1[0, i] - gr * w1[1, i]
        grads[1, :, strided(m), :] = grad[:NLB]
        co, si = trig[1, 0, :, strided(m), :], trig[1, 1, :, strided(m), :]
        back1[0, i] = gr * co + gi * si
        back1[1, i] = gi * co - gr * si

    sweep(back)
    late, early = (
        [Scatter(wire, place, grads, plane, u, bufs[5 * k : 5 * k + 5]) for k, u in pairs]
        for plane, pairs in ((0, tuple(enumerate(RS_UNITS))), (1, tuple(enumerate(RS_UNITS, 2))))
    )
    for s in early:
        s.start_first()
    for s in early:
        s.early_first()
    wrap(back1)
    first_sweep(back1, -0.5)

    def finish(i):
        gr, gi = add_around(back1, rim, i, -0.2)
        grad = gi * w0[0, i] - gr * w0[1, i]
        grads[0, :, strided(i - 1), :] = grad[:NLB]

    sweep(finish)

    for s in late:
        s.start_first()
    for s in early:
        s.middle_first()
    for s in late:
        s.early_first()
    for s in late:
        s.middle_first()
    for s in early:
        s.start_second()
    for s in late:
        s.start_second()
    for s in early:
        s.middle_second()
    for s in late:
        s.middle_second()
    for plane, parts in ((1, early), (0, late)):
        blocks = [block for s in parts for block in s.end_second()]
        for b, block in enumerate(swapped(blocks)):
            out[plane, :, 128 * b : 128 * (b + 1)] = block
    wire.all_sent()
    assert len(wire.groups) <= N_SEM


def per_device(phase_delay, angles, measured):
    f32 = jnp.float32
    field = pltpu.VMEM((2, STEPS + 2, NLB + 1, 8, 128), f32)
    scratch = [
        pltpu.VMEM((2, EXT, COLS + 128), f32),
        pltpu.VMEM((2, 2, NLB + 1, EXT, 128), f32),
        pltpu.VMEM((2, 8, COLS), f32),
        pltpu.VMEM((2, 2, 8, 128), f32),
        pltpu.VMEM((2, ROWS, COLS), jnp.bfloat16),
        pltpu.VMEM((2, NLB, EXT, 128), f32),
        pltpu.VMEM((2, 2, ROWS, 128), f32),
        pltpu.VMEM((2, 2, EXT, 128), f32),
        field,
        field,
        field,
        field,
        field,
        pltpu.VMEM((2, STEPS, 8, 128), f32),
        pltpu.VMEM((2, NLB + 1, 8, 128), f32),
        pltpu.VMEM((STEPS, 8, 128), f32),
        pltpu.VMEM((2, 8, 128), f32),
        pltpu.VMEM((6, 8, 128), f32),
        pltpu.VMEM((2, NLB, EXT, 128), f32),
        pltpu.VMEM((SPAN, 8, 128), f32),
    ]
    for b0, b1, _ in RS_UNITS * 2:
        n = b1 - b0
        scratch += [
            pltpu.VMEM((2, 4, n - n // 2, 8, 128), f32),
            pltpu.VMEM((2, 4, n, 8, 128), f32),
            pltpu.VMEM((4, n, 8, 128), f32),
            pltpu.VMEM((2, n - n // 2, 8, 128), f32),
            pltpu.VMEM((2, n, 8, 128), f32),
        ]
    scratch += [
        pltpu.SemaphoreType.DMA((2,)),
        pltpu.SemaphoreType.DMA((1,)),
        pltpu.SemaphoreType.DMA((N_SEM,)),
    ]
    return pl.pallas_call(
        kernel,
        out_shape=jax.ShapeDtypeStruct(phase_delay.shape, f32),
        in_specs=[
            pl.BlockSpec(memory_space=pl.ANY),
            pl.BlockSpec(memory_space=pltpu.SMEM),
            pl.BlockSpec(memory_space=pl.ANY),
        ],
        out_specs=pl.BlockSpec(memory_space=pltpu.VMEM),
        scratch_shapes=scratch,
        compiler_params=pltpu.CompilerParams(
            collective_id=0, has_side_effects=True, vmem_limit_bytes=56 << 20
        ),
        name="tomography",
    )(phase_delay, angles, measured)


def solution(mesh):
    placed = (P(None, ("row", "illum"), "col"), P("illum", None), P(None, "illum", "row", "col"))
    return jax.shard_map(
        per_device,
        mesh=mesh,
        in_specs=placed,
        out_specs=P(None, ("row", "illum"), "col"),
        check_vma=False,
    )
```

```python
import math

import jax
import jax.numpy as jnp
from jax import lax
from jax.experimental import pallas as pl
from jax.experimental.pallas import tpu as pltpu
from jax.sharding import PartitionSpec as P

ROWS, COLS, NLB = 128, 1024, 8
EXT, STEPS = 144, 18
TOTAL_ROWS, TOTAL_COLS = 512, 4096
EPS_ENERGY = 1e-06
MESH = pl.DeviceIdType.MESH
AG_UNITS = ((0, 6, "zx", True, True), (6, 8, "xz", False, True))
HALO_UNIT = (8, 9, "zx", True, False)
RS_UNITS = ((0, 5, "xz"), (5, 8, "zx"))
N_SEM = 64
UNROLL = 9
SPAN = 720


def sincos(x):
    t = x * x
    s = 0.008333314069458244 + t * (-0.00019835866408867098 + t * 2.6937597583896155e-06)
    s = x * (0.9999999999519255 + t * (-0.1666666642612366 + t * s))
    c = 0.04166645537534636 + t * (-0.0013882960343216638 + t * 2.4121201083497457e-05)
    c = 0.9999999994728761 + t * (-0.4999999736217199 + t * c)
    return s, c


class Place:
    def __init__(self):
        illum = lax.axis_index("illum")
        self.zh, self.x = illum // 4, lax.rem(illum, 4)
        self.y, self.c = lax.axis_index("row"), lax.axis_index("col")

    def block(self, dz, dx):
        return lax.rem(self.zh + dz + 4, 4) * 4 + lax.rem(self.x + dx + 4, 4)

    def rows(self, dz, dx):
        return pl.ds(pl.multiple_of(8 * self.block(dz, dx), 8), 8)

    def illum(self, dz, dx):
        return {"illum": self.block(dz, dx)}

    def tile(self, dy, dc):
        return {"row": lax.rem(self.y + dy + 4, 4), "col": lax.rem(self.c + dc + 4, 4)}


class Wire:
    def __init__(self, send, recv, span):
        self.send, self.recv, self.span = send, recv, span
        self.sent, self.groups = 0, []

    def group(self):
        self.groups.append(0)
        return len(self.groups) - 1

    def start(self, src, dst, device, group):
        tiles = math.prod(src.shape) // 1024
        self.sent += tiles
        self.groups[group] += tiles
        pltpu.make_async_remote_copy(
            src_ref=src,
            dst_ref=dst,
            send_sem=self.send.at[0],
            recv_sem=self.recv.at[group],
            device_id=device,
            device_id_type=MESH,
        ).start()

    def wait_for(self, sem, tiles):
        part = self.span.at[:tiles]
        pltpu.make_async_copy(part, part, sem).wait()

    def arrived(self, group):
        self.wait_for(self.recv.at[group], self.groups[group])

    def all_sent(self):
        self.wait_for(self.send.at[0], self.sent)


class Gather:
    def __init__(self, wire, place, planes, trig, plane, unit):
        self.w, self.p, self.planes, self.trig, self.plane = wire, place, planes, trig, plane
        self.b0, self.b1, self.order, *self.relays = unit
        self.mid = (self.b0 + self.b1) // 2
        self.first = [wire.group() for _ in range(1 + self.relays[0])]
        self.second = {da: wire.group() for da in (0, -1, 1, 2)}
        if self.relays[1]:
            self.last = wire.group()

    def pos(self, da, db):
        return (da, db) if self.order == "zx" else (db, da)

    def send(self, da, db, step, group, half=None):
        rows = self.p.rows(*self.pos(da, db))
        b0, b1 = ((self.b0, self.b1), (self.b0, self.mid), (self.mid, self.b1))[half or 0]
        lead = self.plane
        if lead is None:
            lead, b0, b1 = (half - 1 if half else slice(None)), self.b0, self.b1
        ref = self.planes.at[lead, rows, 128 * b0 : 128 * b1]
        self.w.start(ref, ref, self.p.illum(*self.pos(*step)), group)

    def start(self):
        self.send(0, 0, (1, 0), self.first[0])
        self.send(0, 0, (-1, 0), self.first[0])
        if not self.relays[0]:
            self.send(0, 0, (2, 0), self.first[0])
        self.start_second(0)

    def relay_first(self):
        self.w.arrived(self.first[0])
        if self.relays[0]:
            self.send(-1, 0, (1, 0), self.first[1], 1)
            self.send(1, 0, (-1, 0), self.first[1], 2)
        else:
            self.start_second(2)
        self.start_second(-1)
        self.start_second(1)

    def end_first(self):
        self.w.arrived(self.first[1])
        self.start_second(2)

    def start_second(self, da):
        self.send(da, 0, (0, 1), self.second[da])
        self.send(da, 0, (0, -1), self.second[da])
        if not self.relays[1]:
            self.send(da, 0, (0, 2), self.second[da])

    def relay_second(self, *das):
        for da in das:
            self.w.arrived(self.second[da])
            if self.relays[1]:
                self.send(da, -1, (0, 1), self.last, 1)
                self.send(da, 1, (0, -1), self.last, 2)

    def end(self):
        self.w.arrived(self.last)

    def turn(self, das, dbs):
        for da in das:
            for db in dbs:
                rows = self.p.rows(*self.pos(da, db))
                for plane in (0, 1) if self.plane is None else (self.plane,):
                    turn_rows(self.planes, self.trig, plane, rows, self.b0, self.b1)


def turn_rows(planes, trig, plane, rows, b0, b1):
    s, c = sincos(planes[plane, rows, 128 * b0 : 128 * b1])
    for b in range(b0, b1):
        at = slice(128 * (b - b0), 128 * (b - b0 + 1))
        trig[plane, 0, b, rows, :] = c[:, at]
        trig[plane, 1, b, rows, :] = s[:, at]


class Scatter:
    def __init__(self, wire, place, grads, plane, unit, bufs):
        self.w, self.p, self.g, self.plane = wire, place, grads, plane
        self.b0, self.b1, self.order = unit
        self.n, self.h = self.b1 - self.b0, (self.b1 - self.b0) // 2
        self.t1, self.t2, self.sums, self.t3, self.t4 = bufs
        one, two = (wire.group() for _ in range(2))
        self.r1 = {2: one, 1: one, 3: two, 0: two}
        one, two = (wire.group() for _ in range(2))
        self.r2 = {2: one, 1: one, 3: two, 0: two}
        self.r3, self.r4 = wire.group(), wire.group()

    def pos(self, da, db):
        return (da, db) if self.order == "zx" else (db, da)

    def part(self, da, dq, half=0):
        m = self.b0 + self.h
        lanes = (slice(self.b0, self.b1), slice(self.b0, m), slice(m, self.b1))[half]
        return (self.plane, lanes, self.p.rows(*self.pos(da, dq)), slice(None))

    def send(self, src, dst, da, db, group):
        self.w.start(src, dst, self.p.illum(*self.pos(da, db)), group)

    def start_first(self):
        for dq in (2, 1, 3, 0):
            self.send(self.g.at[self.part(2, dq, 1)], self.t1.at[0, dq, : self.h], 1, 0, self.r1[dq])
            self.send(self.g.at[self.part(2, dq, 2)], self.t1.at[1, dq, : self.n - self.h], -1, 0, self.r1[dq])

    def early_first(self):
        for dq in (2, 1, 3, 0):
            self.send(self.g.at[self.part(1, dq, 2)], self.t2.at[0, dq, self.h :], 1, 0, self.r2[dq])
            self.send(self.g.at[self.part(-1, dq, 1)], self.t2.at[1, dq, : self.h], -1, 0, self.r2[dq])

    def middle_first(self):
        for dq in (2, 1, 3, 0):
            if dq in (2, 3):
                self.w.arrived(self.r1[dq])
            at = self.part(1, dq, 1)
            self.g[at] = self.g[at] + self.t1[0, dq, : self.h]
            at = self.part(-1, dq, 2)
            self.g[at] = self.g[at] + self.t1[1, dq, : self.n - self.h]
        for dq in (2, 1, 3, 0):
            self.send(self.g.at[self.part(1, dq, 1)], self.t2.at[0, dq, : self.h], 1, 0, self.r2[dq])
            self.send(self.g.at[self.part(-1, dq, 2)], self.t2.at[1, dq, self.h :], -1, 0, self.r2[dq])

    def add_first(self, dq):
        self.sums[dq] = self.g[self.part(0, dq)] + self.t2[0, dq] + self.t2[1, dq]

    def start_second(self):
        h = self.h
        self.w.arrived(self.r2[2])
        self.add_first(2)
        self.add_first(1)
        self.send(self.sums.at[2, :h], self.t3.at[0, :h], 0, 1, self.r3)
        self.send(self.sums.at[2, h:], self.t3.at[1, : self.n - h], 0, -1, self.r3)
        self.w.arrived(self.r2[3])
        self.add_first(3)
        self.send(self.sums.at[1, h:], self.t4.at[0, h:], 0, 1, self.r4)
        self.send(self.sums.at[3, :h], self.t4.at[1, :h], 0, -1, self.r4)
        self.add_first(0)

    def middle_second(self):
        h = self.h
        self.w.arrived(self.r3)
        self.sums[1, :h] = self.sums[1, :h] + self.t3[0, :h]
        self.sums[3, h:] = self.sums[3, h:] + self.t3[1, : self.n - h]
        self.send(self.sums.at[1, :h], self.t4.at[0, :h], 0, 1, self.r4)
        self.send(self.sums.at[3, h:], self.t4.at[1, h:], 0, -1, self.r4)

    def end_second(self):
        self.w.arrived(self.r4)
        total = self.sums[0] + self.t4[0] + self.t4[1]
        return [total[b] for b in range(self.n)]


def strided(m):
    return pl.ds(m, 8, stride=STEPS)


def swapped(blocks):
    blocks = list(blocks)
    lane = lanes_of(blocks[0].shape)
    last = lane.ndim - 1
    for k in (1, 2, 4):
        low = jnp.bitwise_and(lane, k) == 0
        for b in range(NLB):
            if not b & k:
                one, two = blocks[b], blocks[b | k]
                blocks[b] = jnp.where(low, one, pltpu.roll(two, k, last))
                blocks[b | k] = jnp.where(low, pltpu.roll(one, 128 - k, last), two)
    return blocks


def split(x):
    return [x[..., 128 * b : 128 * (b + 1)] for b in range(NLB)]


def lanes_of(shape):
    return lax.broadcasted_iota(jnp.int32, shape, len(shape) - 1)


def kernel(
    phase_hbm, angles, meas_hbm, out,
    planes, trig, fresh, edges, raw, meas, rims, beside, w0, w1, rim, adj, back1, rowf, colf, rowm, energy, energy_in,
    grads, span, *rest,
):
    *bufs, local, send, recv = rest
    place = Place()
    wire = Wire(send, recv, span)
    own = place.rows(0, 0)
    fetch = [
        pltpu.make_async_copy(phase_hbm, fresh, local.at[0]),
        pltpu.make_async_copy(meas_hbm.at[:, 0], raw, local.at[1]),
    ]
    partners = [place.illum(1, 0), place.illum(-1, 0), place.illum(0, 1), place.illum(0, -1)]
    partners.append(place.illum(0, 2))
    partners += [place.tile(d, 0) for d in (1, -1)] + [place.tile(0, d) for d in (1, 2, 3)]
    partners += [place.tile(d, e) for d in (1, -1) for e in (1, -1)]
    barrier = pltpu.get_barrier_semaphore()
    for device in partners:
        pl.semaphore_signal(barrier, inc=1, device_id=device, device_id_type=MESH)
    for copy in fetch:
        copy.start()
    pl.semaphore_wait(barrier, len(partners))

    edge_group = wire.group()
    wire.start(phase_hbm.at[:, :, :128], edges.at[0], place.tile(0, -1), edge_group)
    wire.start(phase_hbm.at[:, :, COLS - 128 :], edges.at[1], place.tile(0, 1), edge_group)
    units = [[Gather(wire, place, planes, trig, plane, u) for u in AG_UNITS] for plane in (0, 1)]
    (main0, side0), (main1, side1) = units
    halo = Gather(wire, place, planes, trig, None, HALO_UNIT)
    fetch[0].wait()
    for b, block in enumerate(swapped(split(fresh[...]))):
        planes[:, own, 128 * b : 128 * (b + 1)] = block
    main0.start()
    side0.start()
    main1.start()
    side1.start()
    wire.arrived(edge_group)
    lane = lanes_of((2, 8, 128))
    planes[:, own, COLS:] = jnp.where(lane < 64, pltpu.roll(edges[0], 8, 2), pltpu.roll(edges[1], 120, 2))
    halo.start()

    fetch[1].wait()
    energy[0] = jnp.zeros((8, 128), jnp.float32)

    def widen(g, carry):
        rows = pl.ds(pl.multiple_of(16 * g, 16), 16)
        for part in (0, 1):
            x = raw[part, rows, :].astype(jnp.float32)
            squares = x * x
            blocks = split(x)
            rims[0, part, rows, :] = pltpu.roll(blocks[0], 8, 1)
            rims[1, part, rows, :] = pltpu.roll(blocks[NLB - 1], 120, 1)
            for b, block in enumerate(swapped(blocks)):
                meas[part, b, rows, :] = block
            half = squares[:8] + squares[8:]
            total = half[:, :128]
            for b in range(1, NLB):
                total = total + half[:, 128 * b : 128 * (b + 1)]
            energy[0] = energy[0] + total
        return carry

    lax.fori_loop(0, ROWS // 16, widen, 0)
    energy_group = wire.group()
    wire.start(energy.at[0], energy_in.at[0], place.tile(1, 0), energy_group)
    wire.start(energy.at[0], energy_in.at[1], place.tile(-1, 0), energy_group)
    rim_group = wire.group()
    tile_rows, last, first = slice(0, 128), slice(120, 128), slice(0, 8)
    after, before = slice(128, 136), slice(136, 144)
    wire.start(meas.at[:, :, last, :], meas.at[:, :, before, :], place.tile(1, 0), rim_group)
    wire.start(meas.at[:, :, first, :], meas.at[:, :, after, :], place.tile(-1, 0), rim_group)

    step_a, step_b = angles[0, 0], angles[0, 1]
    lane = lanes_of((8, 128))

    def circle(steps, period):
        turns = jnp.bitwise_and(steps + period // 2, period - 1) - period // 2
        s, c = sincos(turns.astype(jnp.float32) * (0.5 * math.pi / period))
        s, c = 2.0 * s * c, 1.0 - 2.0 * s * s
        return 2.0 * s * c, 1.0 - 2.0 * s * s

    def col_of(b):
        edge = jnp.where(lane < 64, COLS - 8 + lane, lane - 120)
        inner = 128 * jnp.bitwise_and(lane, 7) + jnp.bitwise_and(lane, -8) + b
        return place.c * COLS + (inner if b < NLB else edge)

    def factors():
        shape = (STEPS, 8, 128)
        r = lax.broadcasted_iota(jnp.int32, shape, 1) * STEPS + lax.broadcasted_iota(jnp.int32, shape, 0)
        gr = place.y * ROWS + jnp.where(r < 136, r, r - EXT)
        inside = jnp.where((gr >= 0) & (gr < TOTAL_ROWS), 1.0, 0.0)
        si, co = circle(step_a * gr, TOTAL_ROWS)
        rowf[0] = inside * (-0.28 * co - 0.96 * si)
        rowf[1] = inside * (0.96 * co - 0.28 * si)
        rowm[...] = inside
        gc = jnp.stack([col_of(b) for b in range(NLB + 1)])
        inside = jnp.where((gc >= 0) & (gc < TOTAL_COLS), 1.0, 0.0)
        si, co = circle(step_b * gc, TOTAL_COLS)
        colf[0] = inside * co
        colf[1] = inside * si

    every, near = (0, -1, 1, 2), (0, -1, 1)
    every, near = (0, -1, 1, 2), (0, -1, 1)
    main0.relay_second(0)
    main0.turn((0,), near)
    main0.relay_first()
    side0.relay_first()
    main1.relay_second(0)
    wire.arrived(energy_group)
    far_group = wire.group()
    wire.start(energy_in.at[0], energy_in.at[2], place.tile(1, 0), far_group)
    halo.turn((0,), (0,))
    main1.relay_first()
    side1.relay_first()
    main0.turn((-1, 1), (0,))
    halo.relay_first()
    factors()
    side0.turn(every, (0,))
    side0.relay_second(0)
    main0.end_first()
    main0.relay_second(-1, 1)
    side1.relay_second(0)
    halo.end_first()
    main1.end_first()
    side0.relay_second(-1, 1)
    main1.relay_second(-1, 1)
    wire.arrived(far_group)
    energy[1] = energy[0] + energy_in[0] + energy_in[1] + energy_in[2]
    energy_group = wire.group()
    for d in (1, 2, 3):
        wire.start(energy.at[1], energy_in.at[2 + d], place.tile(0, d), energy_group)
    side0.relay_second(2)
    side1.relay_second(-1, 1)
    main0.turn((-1, 1), (-1, 1))
    main0.turn((2,), (0,))
    main0.relay_second(2)
    side1.relay_second(2)
    main1.relay_second(2)
    side0.turn(every, (-1, 1))
    halo.relay_second(*every)

    end_groups = [wire.group(), wire.group()]

    def share_ends(plane):
        ref = planes.at[plane]
        for unit in units[plane]:
            unit.end()
        wire.start(ref.at[last, :], ref.at[before, :], place.tile(1, 0), end_groups[plane])
        wire.start(ref.at[first, :], ref.at[after, :], place.tile(-1, 0), end_groups[plane])

    def turn_ends(plane):
        wire.arrived(end_groups[plane])
        turn_rows(planes, trig, plane, slice(128, 144), 0, NLB + 1)

    share_ends(0)
    for side, dc in ((0, -1), (1, 1)):
        src, dst = rims.at[side], beside.at[side]
        wire.start(src.at[:, tile_rows, :], dst.at[:, tile_rows, :], place.tile(0, dc), rim_group)
        wire.start(src.at[:, last, :], dst.at[:, before, :], place.tile(1, dc), rim_group)
        wire.start(src.at[:, first, :], dst.at[:, after, :], place.tile(-1, dc), rim_group)
    main0.turn((2,), (-1, 1))
    main0.turn(every, (2,))
    side0.turn(every, (2,))
    halo.turn((0,), (-1, 1, 2))
    halo.turn((-1, 1, 2), every)
    main1.turn(near, near)
    main1.turn((2,), (0,))
    side1.turn(every, near)
    turn_ends(0)

    gc8 = col_of(NLB)
    col_in = jnp.where((gc8 >= 0) & (gc8 < TOTAL_COLS), 1.0, 0.0)

    def scaled(m, amount):
        k = rowm[m] * amount
        return jnp.concatenate([jnp.broadcast_to(k[None], (NLB, 8, 128)), (k * col_in)[None]], axis=0)

    def around(field, part, i):
        mid = field[part, i]
        first, last, edge = mid[0], mid[NLB - 1], mid[NLB]
        ahead = pltpu.roll(jnp.where(lane == 8, edge, first), 119, 1)
        behind = pltpu.roll(jnp.where(lane == 119, edge, last), 9, 1)
        right_last = jnp.where(lane < 120, pltpu.roll(first, 120, 1), ahead)
        left_first = jnp.where(lane < 8, behind, pltpu.roll(last, 8, 1))
        right_edge = jnp.where(lane == 119, ahead, pltpu.roll(edge, 127, 1))
        left_edge = jnp.where(lane == 8, behind, pltpu.roll(edge, 1, 1))
        right = jnp.concatenate([mid[1:NLB], right_last[None], right_edge[None]], axis=0)
        left = jnp.concatenate([left_first[None], mid[: NLB - 1], left_edge[None]], axis=0)
        return (field[part, i - 1] + field[part, i + 1]) + (right + left)

    def wrap(field):
        for part in (0, 1):
            field[part, 0] = pltpu.roll(field[part, STEPS], 1, 1)
            field[part, STEPS + 1] = pltpu.roll(field[part, 1], 7, 1)

    def add_around(base, field, i, amount):
        k = scaled(i - 1, amount)
        real = base[0, i] - k * around(field, 1, i)
        imag = base[1, i] + k * around(field, 0, i)
        return real, imag

    def sweep(body):
        def several(t, carry):
            for k in range(UNROLL):
                body(UNROLL * t + k + 1)
            return carry

        lax.fori_loop(0, STEPS // UNROLL, several, 0)

    def enter(i):
        m = i - 1
        co, si = trig[0, 0, :, strided(m), :], trig[0, 1, :, strided(m), :]
        fr, fi = rowf[0, m], rowf[1, m]
        cr, ci = colf[0], colf[1]
        ur = fr[None] * cr - fi[None] * ci
        ui = fr[None] * ci + fi[None] * cr
        w0[0, i] = ur * co - ui * si
        w0[1, i] = ur * si + ui * co

    def first_sweep(base, amount):
        def body(i):
            rim[0, i], rim[1, i] = add_around(base, base, i, amount)

        sweep(body)
        wrap(rim)

    sweep(enter)
    share_ends(1)
    wrap(w0)
    first_sweep(w0, 0.5)
    main1.turn((2,), (-1, 1))
    main1.turn(every, (2,))
    side1.turn(every, (2,))
    turn_ends(1)

    def between(i):
        ur, ui = add_around(w0, rim, i, 0.2)
        m = i - 1
        co, si = trig[1, 0, :, strided(m), :], trig[1, 1, :, strided(m), :]
        w1[0, i] = ur * co - ui * si
        w1[1, i] = ur * si + ui * co

    sweep(between)
    wrap(w1)
    first_sweep(w1, 0.5)

    wire.arrived(energy_group)
    total = energy[1] + energy_in[3] + energy_in[4] + energy_in[5]
    mean = jnp.sum(total, keepdims=True) * (1.0 / (TOTAL_ROWS * TOTAL_COLS)) + EPS_ENERGY
    kappa = jnp.broadcast_to(2.0 / mean, (8, 128))
    wire.arrived(rim_group)

    def compare(i):
        m = i - 1
        ur, ui = add_around(w1, rim, i, 0.2)
        k = scaled(m, kappa)
        for part, u in ((0, ur), (1, ui)):
            side = jnp.where(lane < 64, beside[0, part, strided(m), :], beside[1, part, strided(m), :])
            seen = jnp.concatenate([meas[part, :, strided(m), :], side[None]], axis=0)
            adj[part, i] = k * (u - seen)

    sweep(compare)
    wrap(adj)
    first_sweep(adj, -0.5)

    def back(i):
        m = i - 1
        gr, gi = add_around(adj, rim, i, -0.2)
        grad = gi * w1[0, i] - gr * w1[1, i]
        grads[1, :, strided(m), :] = grad[:NLB]
        co, si = trig[1, 0, :, strided(m), :], trig[1, 1, :, strided(m), :]
        back1[0, i] = gr * co + gi * si
        back1[1, i] = gi * co - gr * si

    sweep(back)
    late, early = (
        [Scatter(wire, place, grads, plane, u, bufs[5 * k : 5 * k + 5]) for k, u in pairs]
        for plane, pairs in ((0, tuple(enumerate(RS_UNITS))), (1, tuple(enumerate(RS_UNITS, 2))))
    )
    for s in early:
        s.start_first()
    for s in early:
        s.early_first()
    wrap(back1)
    first_sweep(back1, -0.5)

    def finish(i):
        gr, gi = add_around(back1, rim, i, -0.2)
        grad = gi * w0[0, i] - gr * w0[1, i]
        grads[0, :, strided(i - 1), :] = grad[:NLB]

    sweep(finish)

    for s in late:
        s.start_first()
    for s in early:
        s.middle_first()
    for s in late:
        s.early_first()
    for s in late:
        s.middle_first()
    for s in early:
        s.start_second()
    for s in late:
        s.start_second()
    for s in early:
        s.middle_second()
    for s in late:
        s.middle_second()
    for plane, parts in ((1, early), (0, late)):
        blocks = [block for s in parts for block in s.end_second()]
        for b, block in enumerate(swapped(blocks)):
            out[plane, :, 128 * b : 128 * (b + 1)] = block
    wire.all_sent()
    assert len(wire.groups) <= N_SEM


def per_device(phase_delay, angles, measured):
    f32 = jnp.float32
    field = pltpu.VMEM((2, STEPS + 2, NLB + 1, 8, 128), f32)
    scratch = [
        pltpu.VMEM((2, EXT, COLS + 128), f32),
        pltpu.VMEM((2, 2, NLB + 1, EXT, 128), f32),
        pltpu.VMEM((2, 8, COLS), f32),
        pltpu.VMEM((2, 2, 8, 128), f32),
        pltpu.VMEM((2, ROWS, COLS), jnp.bfloat16),
        pltpu.VMEM((2, NLB, EXT, 128), f32),
        pltpu.VMEM((2, 2, ROWS, 128), f32),
        pltpu.VMEM((2, 2, EXT, 128), f32),
        field,
        field,
        field,
        field,
        field,
        pltpu.VMEM((2, STEPS, 8, 128), f32),
        pltpu.VMEM((2, NLB + 1, 8, 128), f32),
        pltpu.VMEM((STEPS, 8, 128), f32),
        pltpu.VMEM((2, 8, 128), f32),
        pltpu.VMEM((6, 8, 128), f32),
        pltpu.VMEM((2, NLB, EXT, 128), f32),
        pltpu.VMEM((SPAN, 8, 128), f32),
    ]
    for b0, b1, _ in RS_UNITS * 2:
        n = b1 - b0
        scratch += [
            pltpu.VMEM((2, 4, n - n // 2, 8, 128), f32),
            pltpu.VMEM((2, 4, n, 8, 128), f32),
            pltpu.VMEM((4, n, 8, 128), f32),
            pltpu.VMEM((2, n - n // 2, 8, 128), f32),
            pltpu.VMEM((2, n, 8, 128), f32),
        ]
    scratch += [
        pltpu.SemaphoreType.DMA((2,)),
        pltpu.SemaphoreType.DMA((1,)),
        pltpu.SemaphoreType.DMA((N_SEM,)),
    ]
    return pl.pallas_call(
        kernel,
        out_shape=jax.ShapeDtypeStruct(phase_delay.shape, f32),
        in_specs=[
            pl.BlockSpec(memory_space=pl.ANY),
            pl.BlockSpec(memory_space=pltpu.SMEM),
            pl.BlockSpec(memory_space=pl.ANY),
        ],
        out_specs=pl.BlockSpec(memory_space=pltpu.VMEM),
        scratch_shapes=scratch,
        compiler_params=pltpu.CompilerParams(
            collective_id=0, has_side_effects=True, vmem_limit_bytes=56 << 20
        ),
        name="tomography",
    )(phase_delay, angles, measured)


def solution(mesh):
    placed = (P(None, ("row", "illum"), "col"), P("illum", None), P(None, "illum", "row", "col"))
    return jax.shard_map(
        per_device,
        mesh=mesh,
        in_specs=placed,
        out_specs=P(None, ("row", "illum"), "col"),
        check_vma=False,
    )
```
